512 devices in a mesh: dp: 8 (over x, z_hi), row: 8 (over y, core), col: 8 (over z_lo).
Axes of the slice: x: 4, y: 4, z: 16 (z_hi: 2, z_lo: 8; z = z_hi * 8 + z_lo), core: 2. Of those that a mesh axis runs over, the one named last changes fastest.
Arguments:
- inputs: bfloat16 [8, 1024, 4096], P('dp', 'col', 'row'), may hold values from -6 to 6
- weights: bfloat16 [4096, 3, 4096], P('row', None, 'col'), may hold values from -0.09375 to 0.09375
- feature_taps: float32 [3, 3, 4096], P(None, None, 'col'), may hold values from -2.5 to 2.5
- inner_taps: float32 [7, 4096], P(None, 'col'), may hold values from -2.5 to 2.5
- grad_out: bfloat16 [8, 1024, 4096], P('dp', 'row', 'col'), may hold values from -6 to 6
Outputs:
- grad_in: bfloat16 [8, 1024, 4096], P('dp', 'col', 'row')
- grad_weights: float32 [4096, 3, 4096], P('row', None, 'col')
The draws below stay inside these ranges and needn't reach their ends.
All inputs are finite; a program needn't handle non-finite values.
Results may differ from the reference program's by a relative error of at most 0.033.
Values may be sent and summed in bfloat16 or wider, within the bound.
A program may use at most 64 MiB of HBM per device.

```python
import jax
import jax.numpy as jnp
from jax import lax

D = 4096
FEAT_TAPS = 3
TAPS = 7
TOKENS = 1024
GROUPS = 8
N_ROW = 8
N_COL = 8


def block_scale(stream_key, extent, cuts, smallest, high):
    def one(axis_at, blocks):
        draws = jax.random.uniform(jax.random.fold_in(jax.random.fold_in(stream_key, 6), axis_at), (blocks,), jnp.float32, smallest / len(cuts), high / len(cuts))
        return jnp.repeat(jnp.exp(draws), extent[axis_at] // blocks).reshape((-1,) + (1,) * (len(extent) - axis_at - 1))

    loudness = one(*cuts[0])
    for cut in cuts[1:]:
        loudness = loudness * one(*cut)
    return loudness


def scatter_about(own_key, extent, deviation, limit, shards=(), kind=jnp.bfloat16):
    gain = block_scale(own_key, extent, shards, -0.22, 0.18) if shards else 1.0
    drawn = jax.random.normal(own_key, extent, jnp.float32) * deviation * gain
    return jnp.minimum(jnp.maximum(drawn, -limit), limit).astype(kind)


def setup_inputs(seed: int = 0) -> dict:
    key_list = jax.random.split(jax.random.key(seed), 6)
    inputs = scatter_about(key_list[0], (GROUPS, TOKENS, D), 1.0, 6.0, ((0, 8), (1, 8), (2, 8)))
    weights = scatter_about(key_list[1], (D, 3, D), D ** -0.5, 0.09375, ((0, 8), (2, 8)))
    feature_taps = scatter_about(key_list[2], (FEAT_TAPS, 3, D), 0.5, 2.5, ((2, 8),), jnp.float32)
    inner_taps = scatter_about(key_list[3], (TAPS, D), 0.35, 2.5, ((1, 8),), jnp.float32)
    grad_out = scatter_about(key_list[4], (GROUPS, TOKENS, D), 1.0, 6.0, ((0, 8), (1, 8), (2, 8)))
    return {"inputs": inputs, "weights": weights, "feature_taps": feature_taps, "inner_taps": inner_taps, "grad_out": grad_out}


def causal(seq, taps):
    total = taps[0] * seq
    for lag in range(1, taps.shape[0]):
        pad = jnp.zeros((lag,) + seq.shape[1:], jnp.float32)
        total = total + taps[lag] * jnp.concatenate([pad, seq[:-lag]], axis=0)
    return total


def anticausal(seq, taps):
    total = taps[0] * seq
    for lag in range(1, taps.shape[0]):
        pad = jnp.zeros((lag,) + seq.shape[1:], jnp.float32)
        total = total + taps[lag] * jnp.concatenate([seq[lag:], pad], axis=0)
    return total


def rounded(value):
    return lax.optimization_barrier(value.astype(jnp.bfloat16)).astype(jnp.float32)


def one_group(tokens, cotangent, weights, feature_taps, inner_taps):
    width_row = D // N_ROW
    width_col = D // N_COL
    flat_w = weights.reshape(D, 3 * D)

    def add_rows(total, index):
        block = lax.dynamic_slice_in_dim(tokens, index * width_row, width_row, 1)
        rows_w = lax.dynamic_slice_in_dim(flat_w, index * width_row, width_row, 0)
        return total + rounded(jnp.dot(block, rows_w, preferred_element_type=jnp.float32)), None

    proj_sum, unused = lax.scan(add_rows, jnp.zeros((TOKENS, 3 * D), jnp.float32), jnp.arange(N_ROW, dtype=jnp.int32))
    proj = rounded(proj_sum).reshape(TOKENS, 3, D)
    mixed = causal(proj, feature_taps)
    query = mixed[:, 0]
    key = mixed[:, 1]
    value = mixed[:, 2]
    product = rounded(key * value)
    inner = causal(product, inner_taps)
    upstream = cotangent.astype(jnp.float32)
    grad_query = upstream * inner
    grad_inner = upstream * query
    grad_product = anticausal(grad_inner, inner_taps)
    grad_mixed = jnp.stack([grad_query, grad_product * value, grad_product * key], axis=1)
    grad_proj = anticausal(grad_mixed, feature_taps).astype(jnp.bfloat16)

    def add_cols(total, index):
        block = lax.dynamic_slice_in_dim(grad_proj, index * width_col, width_col, 2).reshape(TOKENS, 3 * width_col)
        cols_w = lax.dynamic_slice_in_dim(weights, index * width_col, width_col, 2).reshape(D, 3 * width_col)
        part = lax.dot_general(block, cols_w, (((1,), (1,)), ((), ())), preferred_element_type=jnp.float32)
        return total + rounded(part), None

    grad_sum, unused = lax.scan(add_cols, jnp.zeros((TOKENS, D), jnp.float32), jnp.arange(N_COL, dtype=jnp.int32))
    grad_in = grad_sum.astype(jnp.bfloat16)
    grad_w = lax.dot_general(tokens, grad_proj.reshape(TOKENS, 3 * D), (((0,), (0,)), ((), ())), preferred_element_type=jnp.float32)
    return grad_in, grad_w


def reference(inputs, weights, feature_taps, inner_taps, grad_out):
    def step(total, pair):
        grad_in, grad_w = one_group(pair[0], pair[1], weights, feature_taps, inner_taps)
        return total + grad_w, grad_in

    total, grad_in = lax.scan(step, jnp.zeros((D, 3 * D), jnp.float32), (inputs, grad_out))
    return grad_in, total.reshape(D, 3, D)
```

```python
import functools

import jax
import jax.numpy as jnp
from jax import lax
from jax.experimental import pallas as pl
from jax.experimental.pallas import tpu as pltpu
from jax.sharding import PartitionSpec as P

MESH = pl.DeviceIdType.MESH
NT = (((1,), (1,)), ((), ()))
CHUNKS = 6
RING = 4
F32 = jnp.float32
BF16 = jnp.bfloat16


class Place:
    def __init__(self):
        self.dp, self.row, self.col = (lax.axis_index(a) for a in ("dp", "row", "col"))
        self.x, self.zh = self.dp // 2, self.dp % 2
        self.y, self.core = self.row // 2, self.row % 2

    def at_x(self, by):
        return (((self.x + by + RING) % RING) * 2 + self.zh, self.row, self.col)

    def at_y(self, by):
        return (self.dp, ((self.y + by + RING) % RING) * 2 + self.core, self.col)

    def sibling(self):
        return (self.dp, self.y * 2 + 1 - self.core, self.col)

    def at_z(self, by):
        z = (self.zh * 8 + self.col + by + 16) % 16
        return (self.x * 2 + z // 8, self.row, z % 8)

    def at_col(self, by):
        return (self.dp, self.row, (self.col + by + 8) % 8)


def greet(partners):
    barrier = pltpu.get_barrier_semaphore()
    for partner in partners:
        pl.semaphore_signal(barrier, inc=1, device_id=partner, device_id_type=MESH)
    pl.semaphore_wait(barrier, len(partners))


class Sends:
    def __init__(self, sems):
        self.sems, self.copies = sems, []

    def start(self, src, dst, recv, device):
        copy = pltpu.make_async_remote_copy(
            src_ref=src, dst_ref=dst, send_sem=self.sems.at[len(self.copies)], recv_sem=recv,
            device_id=device, device_id_type=MESH,
        )
        copy.start()
        self.copies.append(copy)

    def finish(self):
        for copy in self.copies:
            copy.wait_send()


def arrived(ref, sem, place):
    pltpu.make_async_copy(ref, ref, sem).wait()


def tail_kernel(
    gp, xg, w, gx, dw,
    G, XT, D, xrel, xrec, S, zrel, zrec, rr, rl, part,
    sends, col_send, g_recv, xrel_sem, xrec_sem, zrel_sem, zrec_sem, out_sem, rr_sem, rl_sem,
):
    me = Place()
    rows = gp.shape[0]
    half = rows // 2
    wide = w.shape[2]
    step = 3 * wide // CHUNKS
    per = wide // step
    right, left = me.at_y(1), me.at_y(-1)
    sibling = me.sibling()
    xr, xl = me.at_x(1), me.at_x(-1)
    up, down = me.at_z(4), me.at_z(-4)
    col_up, col_down = me.at_col(1), me.at_col(-1)
    greet([right, left, sibling, xr, xl, up, down, col_up, col_down])
    out = Sends(sends)

    def g_at(slot, h):
        return G.at[pl.ds(pl.multiple_of(slot * rows + h * half, half), half)]

    def g_send(src, slot, h, device):
        out.start(src, g_at(slot, h), g_recv.at[slot, h], device)

    def g_wait(slot, h):
        arrived(g_at(slot, h), g_recv.at[slot, h], me)

    def same(by):
        return ((me.y + by + RING) % RING) * 2 + me.core

    def other(by):
        return ((me.y + by + RING) % RING) * 2 + 1 - me.core

    own = [gp.at[pl.ds(h * half, half)] for h in range(2)]
    g_send(own[0], me.row, 0, right)
    g_send(own[1], me.row, 1, left)
    g_send(own[1], me.row, 1, right)
    g_send(own[0], me.row, 0, left)
    for h in range(2):
        g_send(own[h], me.row, h, sibling)
    G[pl.ds(pl.multiple_of(me.row * rows, rows), rows), :] = gp[...]
    for b in range(8):
        XT[:, b * rows : (b + 1) * rows] = xg[b * rows : (b + 1) * rows, :].T

    @pl.when(me.col == 7)
    def _():
        rr[...] = jnp.zeros_like(rr)

    @pl.when(me.col == 0)
    def _():
        rl[...] = jnp.zeros_like(rl)

    g_wait(same(-1), 0)
    g_send(g_at(same(-1), 0), same(-1), 0, right)
    g_send(g_at(same(-1), 0), same(-1), 0, sibling)
    g_wait(same(1), 1)
    g_send(g_at(same(1), 1), same(1), 1, left)
    g_send(g_at(same(1), 1), same(1), 1, sibling)
    g_wait(same(-1), 1)
    g_send(g_at(same(-1), 1), same(-1), 1, sibling)
    g_wait(same(1), 0)
    g_send(g_at(same(1), 0), same(1), 0, sibling)
    g_wait(same(2), 0)
    g_send(g_at(same(2), 0), same(2), 0, sibling)
    g_wait(same(2), 1)
    g_send(g_at(same(2), 1), same(2), 1, sibling)
    for by in (0, -1, 1, 2):
        for h in range(2):
            g_wait(other(by), h)

    def grad_in_of(block):
        at = pl.ds(pl.multiple_of(block * rows, rows), rows)
        total = lax.dot_general(G[at, 0:wide], w[0], NT, preferred_element_type=F32)
        for c in range(1, 3):
            total = total + lax.dot_general(
                G[at, c * wide : (c + 1) * wide], w[c], NT, preferred_element_type=F32
            )
        return total

    def col_copy(block, side):
        landing, sems, device = ((rr, rr_sem, col_down), (rl, rl_sem, col_up))[side]
        return pltpu.make_async_remote_copy(
            src_ref=part.at[block], dst_ref=landing.at[block], send_sem=col_send.at[block],
            recv_sem=sems.at[block], device_id=device, device_id_type=MESH,
        )

    def col_round(s):
        @pl.when(s + me.col >= 7)
        def _():
            block = s + me.col - 7

            @pl.when(me.col < 7)
            def _():
                arrived(rr.at[block], rr_sem.at[block], me)

            part[block] = (grad_in_of(block) + rr[block].astype(F32)).astype(BF16)
            col_copy(block, 0).start()

        @pl.when(s >= me.col)
        def _():
            block = 7 - s + me.col

            @pl.when(me.col > 0)
            def _():
                arrived(rl.at[block], rl_sem.at[block], me)

            part[block] = (grad_in_of(block) + rl[block].astype(F32)).astype(BF16)
            col_copy(block, 1).start()

    def col_last():
        total = grad_in_of(me.col)

        @pl.when(me.col < 7)
        def _():
            arrived(rr.at[me.col], rr_sem.at[me.col], me)

        @pl.when(me.col > 0)
        def _():
            arrived(rl.at[me.col], rl_sem.at[me.col], me)

        gx[...] = (total + rr[me.col].astype(F32) + rl[me.col].astype(F32)).astype(BF16)

        for block in range(8):

            @pl.when(block < me.col)
            def _():
                col_copy(block, 0).wait_send()

            @pl.when(block > me.col)
            def _():
                col_copy(block, 1).wait_send()

    top, bottom = pl.ds(0, half), pl.ds(half, half)
    halves = (top, bottom)
    to_r, to_l, to_o = ((me.x + by + RING) % RING for by in (1, 3, 2))

    def dw_at(q, h, m):
        return dw.at[
            m // per,
            pl.ds(pl.multiple_of(q * rows + h * half, half), half),
            pl.ds((m % per) * step, step),
        ]

    def multiply(m):
        for q in range(RING):
            D[q, m] = jnp.dot(
                XT[q * rows : (q + 1) * rows, :], G[:, m * step : (m + 1) * step],
                preferred_element_type=F32,
            ).astype(BF16)
        out.start(D.at[to_o, m, top], xrel.at[0, m], xrel_sem.at[0, m], xr)
        out.start(D.at[to_o, m, bottom], xrel.at[1, m], xrel_sem.at[1, m], xl)
        out.start(D.at[to_r, m, bottom], xrec.at[0, m, bottom], xrec_sem.at[0, 1, m], xr)
        out.start(D.at[to_l, m, top], xrec.at[1, m, top], xrec_sem.at[1, 0, m], xl)

    def relay_x(m):
        arrived(xrel.at[0, m], xrel_sem.at[0, m], me)
        D[to_r, m, top] = (D[to_r, m, top].astype(F32) + xrel[0, m].astype(F32)).astype(BF16)
        out.start(D.at[to_r, m, top], xrec.at[0, m, top], xrec_sem.at[0, 0, m], xr)
        arrived(xrel.at[1, m], xrel_sem.at[1, m], me)
        D[to_l, m, bottom] = (D[to_l, m, bottom].astype(F32) + xrel[1, m].astype(F32)).astype(BF16)
        out.start(D.at[to_l, m, bottom], xrec.at[1, m, bottom], xrec_sem.at[1, 1, m], xl)

    def exchange(m):
        for side in range(2):
            for h in range(2):
                arrived(xrec.at[side, m, halves[h]], xrec_sem.at[side, h, m], me)
        S[m] = (D[me.x, m].astype(F32) + xrec[0, m].astype(F32) + xrec[1, m].astype(F32)).astype(BF16)
        out.start(S.at[m, top], zrel.at[0, m], zrel_sem.at[0, m], up)
        out.start(S.at[m, bottom], zrel.at[1, m], zrel_sem.at[1, m], down)

    def relay_z(m):
        arrived(zrel.at[0, m], zrel_sem.at[0, m], me)
        out.start(zrel.at[0, m], zrec.at[m, top], zrec_sem.at[0, m], up)
        arrived(zrel.at[1, m], zrel_sem.at[1, m], me)
        out.start(zrel.at[1, m], zrec.at[m, bottom], zrec_sem.at[1, m], down)

    def gather(q, h, m, device):
        out.start(dw_at(q, h, m), dw_at(q, h, m), out_sem.at[q, h, m], device)

    def gathered(q, h, m):
        arrived(dw_at(q, h, m), out_sem.at[q, h, m], me)

    def total_of(m):
        for h in range(2):
            arrived(zrec.at[m, halves[h]], zrec_sem.at[h, m], me)
        dw[
            m // per, pl.ds(pl.multiple_of(me.x * rows, rows), rows), pl.ds((m % per) * step, step)
        ] = (S[m].astype(F32) + zrec[m].astype(F32)).astype(BF16)
        gather(me.x, 0, m, xr)
        gather(me.x, 1, m, xl)
        gather(me.x, 1, m, xr)
        gather(me.x, 0, m, xl)

    def relay_out(m):
        gathered(to_l, 0, m)
        gather(to_l, 0, m, xr)
        gathered(to_r, 1, m)
        gather(to_r, 1, m, xl)

    def last_out(m):
        gathered(to_l, 1, m)
        gathered(to_r, 0, m)
        gathered(to_o, 0, m)
        gathered(to_o, 1, m)

    stages = [multiply, relay_x, exchange, relay_z, total_of, relay_out, last_out]
    order = []
    lag = [0, 2, 3, 5, 7, 8, 9]
    for slot in range(CHUNKS + lag[-1]):
        for k in reversed(range(len(stages))):
            m = slot - lag[k]
            if 0 <= m < CHUNKS:
                order.append((stages[k], m))
        if 1 <= slot < 8:
            order.append((col_round, slot - 1))
        if slot == 8:
            order.append((lambda unused: col_last(), 0))
    for stage, m in order:
        stage(m)
    out.finish()


SENDS = 6 + 8 + CHUNKS * (4 + 2 + 2 + 2 + 4 + 2)


def tail(gp, xg, w):
    rows, wide = gp.shape[0], w.shape[2]
    half, step = rows // 2, 3 * wide // CHUNKS
    vmem, sem = pltpu.VMEM, pltpu.SemaphoreType.DMA
    return pl.pallas_call(
        tail_kernel,
        out_shape=(
            jax.ShapeDtypeStruct((rows, w.shape[1]), BF16),
            jax.ShapeDtypeStruct(w.shape, BF16),
        ),
        in_specs=[pl.BlockSpec(memory_space=pltpu.VMEM)] * 3,
        out_specs=(pl.BlockSpec(memory_space=pltpu.VMEM),) * 2,
        scratch_shapes=[
            vmem((8 * rows, 3 * wide), BF16),
            vmem((w.shape[1], 8 * rows), BF16),
            vmem((RING, CHUNKS, rows, step), BF16),
            vmem((2, CHUNKS, half, step), BF16),
            vmem((2, CHUNKS, rows, step), BF16),
            vmem((CHUNKS, rows, step), BF16),
            vmem((2, CHUNKS, half, step), BF16),
            vmem((CHUNKS, rows, step), BF16),
            vmem((8, rows, w.shape[1]), BF16),
            vmem((8, rows, w.shape[1]), BF16),
            vmem((8, rows, w.shape[1]), BF16),
            sem((SENDS,)),
            sem((8,)),
            sem((8, 2)),
            sem((2, CHUNKS)),
            sem((2, 2, CHUNKS)),
            sem((2, CHUNKS)),
            sem((2, CHUNKS)),
            sem((RING, 2, CHUNKS)),
            sem((8,)),
            sem((8,)),
        ],
        compiler_params=pltpu.CompilerParams(
            collective_id=1, has_side_effects=True, vmem_limit_bytes=44 * 2**20
        ),
        name="tail",
    )(gp, xg, w)


def with_halo(cells, sides, width):
    for axis, dim in sides:
        count = lax.axis_size(axis)
        ends = count - 1
        head = lax.slice_in_dim(cells, 0, width, axis=dim)
        tail = lax.slice_in_dim(cells, cells.shape[dim] - width, cells.shape[dim], axis=dim)
        cells = jnp.concatenate(
            [
                lax.ppermute(tail, axis, [(i, (i + 1) % count) for i in range(ends)]),
                cells,
                lax.ppermute(head, axis, [((i + 1) % count, i) for i in range(ends)]),
            ],
            axis=dim,
        )
    return cells


def shifted(shard, axis, by):
    length = lax.axis_size(axis)
    pairs = [(i, i + by) for i in range(length) if 0 <= i + by < length]
    return lax.ppermute(shard, axis, pairs)


def causal(seq, taps):
    total = taps[0] * seq
    for lag in range(1, taps.shape[0]):
        pad = jnp.zeros((lag,) + seq.shape[1:], jnp.float32)
        total = total + taps[lag] * jnp.concatenate([pad, seq[:-lag]], axis=0)
    return total


def anticausal(seq, taps):
    total = taps[0] * seq
    for lag in range(1, taps.shape[0]):
        pad = jnp.zeros((lag,) + seq.shape[1:], jnp.float32)
        total = total + taps[lag] * jnp.concatenate([seq[lag:], pad], axis=0)
    return total


def rounded(value):
    return lax.optimization_barrier(value.astype(jnp.bfloat16)).astype(jnp.float32)


def on_device(inputs, weights, feature_taps, inner_taps, grad_out):
    tile = inputs[0]
    upstream_tile = grad_out[0]
    rows_dev = upstream_tile.shape[0]
    width_row = weights.shape[0]
    width_col = weights.shape[2]
    margin = feature_taps.shape[0] - 1 + (inner_taps.shape[0] - 1)
    flat_w = weights.reshape(width_row, 3 * width_col)
    columns = lax.all_gather(tile, "col", axis=0, tiled=True)
    block = columns
    proj = lax.psum_scatter(
        jnp.dot(block, flat_w, preferred_element_type=jnp.float32).astype(jnp.bfloat16),
        "row",
        scatter_dimension=0,
        tiled=True,
    )
    padded = with_halo(proj, (("row", 0),), margin)
    after = shifted(upstream_tile[:margin], "row", -1)
    length = rows_dev + 2 * margin
    window = padded.astype(jnp.float32).reshape(length, 3, width_col)
    upstream = jnp.concatenate(
        [
            jnp.zeros((margin, width_col), jnp.float32),
            upstream_tile.astype(jnp.float32),
            after.astype(jnp.float32),
        ],
        axis=0,
    )
    mixed = causal(window, feature_taps)
    query = mixed[:, 0]
    key = mixed[:, 1]
    value = mixed[:, 2]
    product = rounded(key * value)
    inner = causal(product, inner_taps)
    grad_query = upstream * inner
    grad_inner = upstream * query
    grad_product = anticausal(grad_inner, inner_taps)
    grad_mixed = jnp.stack([grad_query, grad_product * value, grad_product * key], axis=1)
    grad_proj = anticausal(grad_mixed, feature_taps)[margin : margin + rows_dev].astype(
        jnp.bfloat16
    )
    grad_x, grad_w = tail(
        grad_proj.reshape(rows_dev, 3 * width_col), columns, weights.transpose(1, 0, 2)
    )
    return grad_x[None], grad_w.astype(jnp.float32).transpose(1, 0, 2)


def solution(mesh):
    placed = (
        P("dp", "col", "row"),
        P("row", None, "col"),
        P(None, None, "col"),
        P(None, "col"),
        P("dp", "row", "col"),
    )
    return jax.shard_map(
        on_device,
        mesh=mesh,
        in_specs=placed,
        out_specs=(P("dp", "col", "row"), P("row", None, "col")),
        check_vma=False,
    )
```

```python
import jax
import jax.numpy as jnp
from jax import lax
from jax.experimental import pallas as pl
from jax.experimental.pallas import tpu as pltpu
from jax.sharding import PartitionSpec as P

MESH = pl.DeviceIdType.MESH
NT = (((1,), (1,)), ((), ()))
CHUNKS = 6
HALO = 16
LANES = 128
RING = 4
F32 = jnp.float32
BF16 = jnp.bfloat16


class Place:
    def __init__(self):
        self.dp, self.row, self.col = (lax.axis_index(a) for a in ("dp", "row", "col"))
        self.x, self.zh = self.dp // 2, self.dp % 2
        self.y, self.core = self.row // 2, self.row % 2

    def at_x(self, by):
        return (((self.x + by + RING) % RING) * 2 + self.zh, self.row, self.col)

    def at_y(self, by):
        return (self.dp, ((self.y + by + RING) % RING) * 2 + self.core, self.col)

    def sibling(self):
        return (self.dp, self.y * 2 + 1 - self.core, self.col)

    def at_z(self, by):
        z = (self.zh * 8 + self.col + by + 16) % 16
        return (self.x * 2 + z // 8, self.row, z % 8)

    def at_col(self, by):
        return (self.dp, self.row, (self.col + by + 8) % 8)


def greet(partners):
    barrier = pltpu.get_barrier_semaphore()
    for partner in partners:
        pl.semaphore_signal(barrier, inc=1, device_id=partner, device_id_type=MESH)
    pl.semaphore_wait(barrier, len(partners))


class Sends:
    def __init__(self, sems):
        self.sems, self.copies = sems, []

    def start(self, src, dst, recv, device):
        copy = pltpu.make_async_remote_copy(
            src_ref=src, dst_ref=dst, send_sem=self.sems.at[len(self.copies)], recv_sem=recv,
            device_id=device, device_id_type=MESH,
        )
        copy.start()
        self.copies.append(copy)

    def finish(self):
        for copy in self.copies:
            copy.wait_send()


def arrived(ref, sem, place):
    pltpu.make_async_copy(ref, ref, sem).wait()


def whole_kernel(
    tile, w, ft, it, go, gx, dw,
    XG, XT, acc, psend, pair, Dy, yrel, yrec, win, goa,
    G, D, xrel, xrec, S, zrel, zrec, rr, rl, part,
    sends, ag_send, ag_recv, p_send, p_recv, y_send, yrel_sem, yrec_sem, h_send, h_recv,
    col_send, g_recv, xrel_sem, xrec_sem, zrel_sem, zrec_sem, out_sem, rr_sem, rl_sem,
):
    me = Place()
    rows = tile.shape[0]
    half = rows // 2
    wide = w.shape[2]
    step = 3 * wide // CHUNKS
    per = wide // step
    right, left = me.at_y(1), me.at_y(-1)
    sibling = me.sibling()
    xr, xl = me.at_x(1), me.at_x(-1)
    up, down = me.at_z(4), me.at_z(-4)
    col_up, col_down = me.at_col(1), me.at_col(-1)
    far = (me.dp, (me.row + 2 * me.core + 7) % 8, me.col)
    greet([right, left, sibling, far, xr, xl, up, down, col_up, col_down])
    out = Sends(sends)
    top, bottom = pl.ds(0, half), pl.ds(half, half)
    halves = (top, bottom)

    before, after = (me.dp, (me.row + 7) % 8, me.col), (me.dp, (me.row + 1) % 8, me.col)

    def halo_copy(n):
        src, dst, device = (
            (go.at[pl.ds(0, HALO)], goa, before),
            (win.at[pl.ds(HALO, HALO)], win.at[pl.ds(rows + HALO, HALO)], before),
            (win.at[pl.ds(rows, HALO)], win.at[pl.ds(0, HALO)], after),
        )[n]
        return pltpu.make_async_remote_copy(
            src_ref=src, dst_ref=dst, send_sem=h_send.at[n], recv_sem=h_recv.at[n],
            device_id=device, device_id_type=MESH,
        )

    @pl.when(me.row > 0)
    def _():
        halo_copy(0).start()

    @pl.when(me.row == 0)
    def _():
        win[0:HALO, :] = jnp.zeros((HALO, 3 * wide), BF16)

    @pl.when(me.row == 7)
    def _():
        win[rows + HALO :, :] = jnp.zeros((HALO, 3 * wide), BF16)
        goa[...] = jnp.zeros_like(goa)

    def block_at(j):
        return pl.ds(pl.multiple_of(j * rows, rows), rows)

    def line_copy(j, device):
        return pltpu.make_async_remote_copy(
            src_ref=XG.at[block_at(j)], dst_ref=XG.at[block_at(j)], send_sem=ag_send.at[j],
            recv_sem=ag_recv.at[j], device_id=device, device_id_type=MESH,
        )

    def own_copy(n):
        return pltpu.make_async_remote_copy(
            src_ref=tile, dst_ref=XG.at[block_at(me.col)],
            send_sem=ag_send.at[8] if n else ag_send.at[me.col],
            recv_sem=ag_recv.at[me.col], device_id=col_down if n else col_up, device_id_type=MESH,
        )

    @pl.when(me.col < 7)
    def _():
        own_copy(0).start()

    @pl.when(me.col > 0)
    def _():
        own_copy(1).start()

    XG[block_at(me.col), :] = tile[...]

    def pair_copy(p):
        return pltpu.make_async_remote_copy(
            src_ref=psend.at[p], dst_ref=pair.at[p], send_sem=p_send.at[p], recv_sem=p_recv.at[p],
            device_id=sibling, device_id_type=MESH,
        )

    def project(j):
        x = XG[block_at(j), :]
        p = j // 2
        mine = j % 2 == me.core
        for c in range(3):
            at = slice(c * wide, (c + 1) * wide)
            product = jnp.dot(x, w[c], preferred_element_type=F32)

            @pl.when(mine)
            def _():
                acc[p, :, at] = product

            @pl.when(jnp.logical_not(mine))
            def _():
                psend[p, :, at] = product.astype(BF16)

        @pl.when(jnp.logical_not(mine))
        def _():
            pair_copy(p).start()

        XT[:, block_at(j)] = x.T

    y_opp, y_r, y_l = ((me.y + by) % RING for by in (2, 1, 3))

    def y_copy(n):
        src, dst, sem, device = (
            (Dy.at[y_opp, top], yrel.at[0], yrel_sem.at[0], right),
            (Dy.at[y_opp, bottom], yrel.at[1], yrel_sem.at[1], left),
            (Dy.at[y_r, bottom], yrec.at[0, bottom], yrec_sem.at[0, 1], right),
            (Dy.at[y_l, top], yrec.at[1, top], yrec_sem.at[1, 0], left),
            (Dy.at[y_r, top], yrec.at[0, top], yrec_sem.at[0, 0], right),
            (Dy.at[y_l, bottom], yrec.at[1, bottom], yrec_sem.at[1, 1], left),
        )[n]
        return pltpu.make_async_remote_copy(
            src_ref=src, dst_ref=dst, send_sem=y_send.at[n], recv_sem=sem, device_id=device,
            device_id_type=MESH,
        )

    def piece(d):
        sign = (2 * (d % 2) - 1) * (1 - 2 * (me.col % 2))
        p = me.col // 2 + sign * (d // 2)
        return p, jnp.logical_and(jnp.logical_and(p >= 0, p < RING), jnp.logical_and(d >= 1, d <= 7))

    def pair_sum(d):
        p, there = piece(d)
        role = (p - me.y + RING) % RING

        @pl.when(there)
        def _():
            arrived(pair.at[p], p_recv.at[p], me)

        @pl.when(jnp.logical_and(there, role == 0))
        def _():
            acc[p] = acc[p] + pair[p].astype(F32)

        @pl.when(jnp.logical_and(there, role != 0))
        def _():
            Dy[p] = (acc[p] + pair[p].astype(F32)).astype(BF16)

        @pl.when(jnp.logical_and(there, role == 2))
        def _():
            y_copy(0).start()
            y_copy(1).start()

        @pl.when(jnp.logical_and(there, role == 1))
        def _():
            y_copy(2).start()

        @pl.when(jnp.logical_and(there, role == 3))
        def _():
            y_copy(3).start()

    def relay_y(d):
        p, there = piece(d)
        role = (p - me.y + RING) % RING

        @pl.when(jnp.logical_and(there, role == 1))
        def _():
            arrived(yrel.at[0], yrel_sem.at[0], me)
            Dy[p, top] = (Dy[p, top].astype(F32) + yrel[0].astype(F32)).astype(BF16)
            y_copy(4).start()

        @pl.when(jnp.logical_and(there, role == 3))
        def _():
            arrived(yrel.at[1], yrel_sem.at[1], me)
            Dy[p, bottom] = (Dy[p, bottom].astype(F32) + yrel[1].astype(F32)).astype(BF16)
            y_copy(5).start()

    project(me.col)

    def line_step(d, carry):
        from_below = jnp.logical_and(d <= 7, me.col - d >= 0)
        from_above = jnp.logical_and(d <= 7, me.col + d <= 7)

        @pl.when(from_below)
        def _():
            j = me.col - d
            arrived(XG.at[block_at(j)], ag_recv.at[j], me)

            @pl.when(me.col < 7)
            def _():
                line_copy(j, col_up).start()

        @pl.when(from_above)
        def _():
            j = me.col + d
            arrived(XG.at[block_at(j)], ag_recv.at[j], me)

            @pl.when(me.col > 0)
            def _():
                line_copy(j, col_down).start()

        @pl.when(from_below)
        def _():
            project(me.col - d)

        @pl.when(from_above)
        def _():
            project(me.col + d)

        relay_y(d - 2)
        pair_sum(d - 1)
        return carry

    lax.fori_loop(1, 10, line_step, 0)

    for side in range(2):
        for h in range(2):
            arrived(yrec.at[side, halves[h]], yrec_sem.at[side, h], me)
    win[HALO : rows + HALO, :] = (acc[me.y] + yrec[0].astype(F32) + yrec[1].astype(F32)).astype(BF16)

    @pl.when(me.row > 0)
    def _():
        halo_copy(1).start()

    @pl.when(me.row < 7)
    def _():
        halo_copy(2).start()

    @pl.when(me.row > 0)
    def _():
        arrived(win.at[pl.ds(0, HALO)], h_recv.at[2], me)

    @pl.when(me.row < 7)
    def _():
        arrived(win.at[pl.ds(rows + HALO, HALO)], h_recv.at[1], me)
        arrived(goa, h_recv.at[0], me)

    length = rows + 2 * HALO

    def causal(seq, taps):
        total = taps[0] * seq
        for lag in range(1, len(taps)):
            total = total + taps[lag] * pltpu.roll(seq, lag, 0)
        return total

    def anticausal(seq, taps):
        total = taps[0] * seq
        for lag in range(1, len(taps)):
            total = total + taps[lag] * pltpu.roll(seq, length - lag, 0)
        return total

    mine = block_at(me.row)

    def channels(n, carry):
        def at(c):
            return pl.ds(pl.multiple_of(c * wide + n * LANES, LANES), LANES)

        taps = [[ft[s, c : c + 1, at(0)] for s in range(3)] for c in range(3)]
        inner_taps = [it[s : s + 1, at(0)] for s in range(7)]
        query, key, value = (causal(win[:, at(c)].astype(F32), taps[c]) for c in range(3))
        upstream = jnp.concatenate(
            [
                jnp.zeros((HALO, LANES), F32),
                go[:, at(0)].astype(F32),
                goa[:, at(0)].astype(F32),
            ],
            axis=0,
        )
        product = (key * value).astype(BF16).astype(F32)
        inner = causal(product, inner_taps)
        grad_product = anticausal(upstream * query, inner_taps)
        mixed = (upstream * inner, grad_product * value, grad_product * key)
        for c in range(3):
            grad = anticausal(mixed[c], taps[c])
            G[mine, at(c)] = grad[HALO : rows + HALO].astype(BF16)
        return carry

    lax.fori_loop(0, wide // LANES, channels, 0)

    def g_at(slot, h):
        return G.at[pl.ds(pl.multiple_of(slot * rows + h * half, half), half)]

    def g_send(slot, h, device):
        out.start(g_at(slot, h), g_at(slot, h), g_recv.at[slot, h], device)

    def g_wait(slot, h):
        arrived(g_at(slot, h), g_recv.at[slot, h], me)

    def same(by):
        return ((me.y + by + RING) % RING) * 2 + me.core

    def other(by):
        return ((me.y + by + RING) % RING) * 2 + 1 - me.core

    g_send(me.row, 0, right)
    g_send(me.row, 1, left)
    g_send(me.row, 1, right)
    g_send(me.row, 0, left)
    for h in range(2):
        g_send(me.row, h, sibling)

    @pl.when(me.col == 7)
    def _():
        rr[...] = jnp.zeros_like(rr)

    @pl.when(me.col == 0)
    def _():
        rl[...] = jnp.zeros_like(rl)

    g_wait(same(-1), 0)
    g_send(same(-1), 0, right)
    g_send(same(-1), 0, sibling)
    g_wait(same(1), 1)
    g_send(same(1), 1, left)
    g_send(same(1), 1, sibling)
    g_wait(same(-1), 1)
    g_send(same(-1), 1, sibling)
    g_wait(same(1), 0)
    g_send(same(1), 0, sibling)
    g_wait(same(2), 0)
    g_send(same(2), 0, sibling)
    g_wait(same(2), 1)
    g_send(same(2), 1, sibling)
    for by in (0, -1, 1, 2):
        for h in range(2):
            g_wait(other(by), h)

    def grad_in_of(block):
        at = pl.ds(pl.multiple_of(block * rows, rows), rows)
        total = lax.dot_general(G[at, 0:wide], w[0], NT, preferred_element_type=F32)
        for c in range(1, 3):
            total = total + lax.dot_general(
                G[at, c * wide : (c + 1) * wide], w[c], NT, preferred_element_type=F32
            )
        return total

    def col_copy(block, side):
        landing, sems, device = ((rr, rr_sem, col_down), (rl, rl_sem, col_up))[side]
        return pltpu.make_async_remote_copy(
            src_ref=part.at[block], dst_ref=landing.at[block], send_sem=col_send.at[block],
            recv_sem=sems.at[block], device_id=device, device_id_type=MESH,
        )

    def col_round(s):
        @pl.when(s + me.col >= 7)
        def _():
            block = s + me.col - 7

            @pl.when(me.col < 7)
            def _():
                arrived(rr.at[block], rr_sem.at[block], me)

            part[block] = (grad_in_of(block) + rr[block].astype(F32)).astype(BF16)
            col_copy(block, 0).start()

        @pl.when(s >= me.col)
        def _():
            block = 7 - s + me.col

            @pl.when(me.col > 0)
            def _():
                arrived(rl.at[block], rl_sem.at[block], me)

            part[block] = (grad_in_of(block) + rl[block].astype(F32)).astype(BF16)
            col_copy(block, 1).start()

    def col_last():
        total = grad_in_of(me.col)

        @pl.when(me.col < 7)
        def _():
            arrived(rr.at[me.col], rr_sem.at[me.col], me)

        @pl.when(me.col > 0)
        def _():
            arrived(rl.at[me.col], rl_sem.at[me.col], me)

        gx[...] = (total + rr[me.col].astype(F32) + rl[me.col].astype(F32)).astype(BF16)

        for block in range(8):

            @pl.when(block < me.col)
            def _():
                col_copy(block, 0).wait_send()

            @pl.when(block > me.col)
            def _():
                col_copy(block, 1).wait_send()

    to_r, to_l, to_o = ((me.x + by + RING) % RING for by in (1, 3, 2))

    def dw_at(q, h, m):
        return dw.at[
            m // per,
            pl.ds(pl.multiple_of(q * rows + h * half, half), half),
            pl.ds((m % per) * step, step),
        ]

    def multiply(m):
        for q in range(RING):
            D[q, m] = jnp.dot(
                XT[q * rows : (q + 1) * rows, :], G[:, m * step : (m + 1) * step],
                preferred_element_type=F32,
            ).astype(BF16)
        out.start(D.at[to_o, m, top], xrel.at[0, m], xrel_sem.at[0, m], xr)
        out.start(D.at[to_o, m, bottom], xrel.at[1, m], xrel_sem.at[1, m], xl)
        out.start(D.at[to_r, m, bottom], xrec.at[0, m, bottom], xrec_sem.at[0, 1, m], xr)
        out.start(D.at[to_l, m, top], xrec.at[1, m, top], xrec_sem.at[1, 0, m], xl)

    def relay_x(m):
        arrived(xrel.at[0, m], xrel_sem.at[0, m], me)
        D[to_r, m, top] = (D[to_r, m, top].astype(F32) + xrel[0, m].astype(F32)).astype(BF16)
        out.start(D.at[to_r, m, top], xrec.at[0, m, top], xrec_sem.at[0, 0, m], xr)
        arrived(xrel.at[1, m], xrel_sem.at[1, m], me)
        D[to_l, m, bottom] = (D[to_l, m, bottom].astype(F32) + xrel[1, m].astype(F32)).astype(BF16)
        out.start(D.at[to_l, m, bottom], xrec.at[1, m, bottom], xrec_sem.at[1, 1, m], xl)

    def exchange(m):
        for side in range(2):
            for h in range(2):
                arrived(xrec.at[side, m, halves[h]], xrec_sem.at[side, h, m], me)
        S[m] = (D[me.x, m].astype(F32) + xrec[0, m].astype(F32) + xrec[1, m].astype(F32)).astype(BF16)
        out.start(S.at[m, top], zrel.at[0, m], zrel_sem.at[0, m], up)
        out.start(S.at[m, bottom], zrel.at[1, m], zrel_sem.at[1, m], down)

    def relay_z(m):
        arrived(zrel.at[0, m], zrel_sem.at[0, m], me)
        out.start(zrel.at[0, m], zrec.at[m, top], zrec_sem.at[0, m], up)
        arrived(zrel.at[1, m], zrel_sem.at[1, m], me)
        out.start(zrel.at[1, m], zrec.at[m, bottom], zrec_sem.at[1, m], down)

    def gather(q, h, m, device):
        out.start(dw_at(q, h, m), dw_at(q, h, m), out_sem.at[q, h, m], device)

    def gathered(q, h, m):
        arrived(dw_at(q, h, m), out_sem.at[q, h, m], me)

    def total_of(m):
        for h in range(2):
            arrived(zrec.at[m, halves[h]], zrec_sem.at[h, m], me)
        dw[
            m // per, pl.ds(pl.multiple_of(me.x * rows, rows), rows), pl.ds((m % per) * step, step)
        ] = (S[m].astype(F32) + zrec[m].astype(F32)).astype(BF16)
        gather(me.x, 0, m, xr)
        gather(me.x, 1, m, xl)
        gather(me.x, 1, m, xr)
        gather(me.x, 0, m, xl)

    def relay_out(m):
        gathered(to_l, 0, m)
        gather(to_l, 0, m, xr)
        gathered(to_r, 1, m)
        gather(to_r, 1, m, xl)

    def last_out(m):
        gathered(to_l, 1, m)
        gathered(to_r, 0, m)
        gathered(to_o, 0, m)
        gathered(to_o, 1, m)

    stages = [multiply, relay_x, exchange, relay_z, total_of, relay_out, last_out]
    order = []
    lag = [0, 2, 3, 5, 7, 8, 9]
    for slot in range(CHUNKS + lag[-1]):
        for k in reversed(range(len(stages))):
            m = slot - lag[k]
            if 0 <= m < CHUNKS:
                order.append((stages[k], m))
        if 1 <= slot < 8:
            order.append((col_round, slot - 1))
        if slot == 8:
            order.append((lambda unused: col_last(), 0))
    for stage, m in order:
        stage(m)
    out.finish()

    @pl.when(me.col < 7)
    def _():
        own_copy(0).wait_send()

    @pl.when(me.col > 0)
    def _():
        own_copy(1).wait_send()

    for j in range(8):

        @pl.when(jnp.logical_and(j < me.col, me.col < 7))
        def _():
            line_copy(j, col_up).wait_send()

        @pl.when(jnp.logical_and(j > me.col, me.col > 0))
        def _():
            line_copy(j, col_down).wait_send()

    for p in range(RING):
        pair_copy(p).wait_send()
    for n in range(6):
        y_copy(n).wait_send()

    @pl.when(me.row > 0)
    def _():
        halo_copy(0).wait_send()
        halo_copy(1).wait_send()

    @pl.when(me.row < 7)
    def _():
        halo_copy(2).wait_send()


SENDS = 6 + 8 + CHUNKS * (4 + 2 + 2 + 2 + 4 + 2)


def whole(tile, w, ft, it, go):
    rows, wide, deep = tile.shape[0], w.shape[2], w.shape[1]
    half, step = rows // 2, 3 * wide // CHUNKS
    vmem, sem = pltpu.VMEM, pltpu.SemaphoreType.DMA
    return pl.pallas_call(
        whole_kernel,
        out_shape=(jax.ShapeDtypeStruct((rows, deep), BF16), jax.ShapeDtypeStruct(w.shape, BF16)),
        in_specs=[pl.BlockSpec(memory_space=pltpu.VMEM)] * 5,
        out_specs=(pl.BlockSpec(memory_space=pltpu.VMEM),) * 2,
        scratch_shapes=[
            vmem((8 * rows, deep), BF16),
            vmem((deep, 8 * rows), BF16),
            vmem((RING, rows, 3 * wide), F32),
            vmem((RING, rows, 3 * wide), BF16),
            vmem((RING, rows, 3 * wide), BF16),
            vmem((RING, rows, 3 * wide), BF16),
            vmem((2, half, 3 * wide), BF16),
            vmem((2, rows, 3 * wide), BF16),
            vmem((rows + 2 * HALO, 3 * wide), BF16),
            vmem((HALO, wide), BF16),
            vmem((8 * rows, 3 * wide), BF16),
            vmem((RING, CHUNKS, rows, step), BF16),
            vmem((2, CHUNKS, half, step), BF16),
            vmem((2, CHUNKS, rows, step), BF16),
            vmem((CHUNKS, rows, step), BF16),
            vmem((2, CHUNKS, half, step), BF16),
            vmem((CHUNKS, rows, step), BF16),
            vmem((8, rows, deep), BF16),
            vmem((8, rows, deep), BF16),
            vmem((8, rows, deep), BF16),
            sem((SENDS,)),
            sem((9,)),
            sem((8,)),
            sem((RING,)),
            sem((RING,)),
            sem((6,)),
            sem((2,)),
            sem((2, 2)),
            sem((3,)),
            sem((3,)),
            sem((8,)),
            sem((8, 2)),
            sem((2, CHUNKS)),
            sem((2, 2, CHUNKS)),
            sem((2, CHUNKS)),
            sem((2, CHUNKS)),
            sem((RING, 2, CHUNKS)),
            sem((8,)),
            sem((8,)),
        ],
        compiler_params=pltpu.CompilerParams(
            collective_id=1, has_side_effects=True, vmem_limit_bytes=50 * 2**20
        ),
        name="whole",
    )(tile, w, ft, it, go)


def on_device(inputs, weights, feature_taps, inner_taps, grad_out):
    grad_x, grad_w = whole(
        inputs[0], weights.transpose(1, 0, 2), feature_taps, inner_taps, grad_out[0]
    )
    return grad_x[None], grad_w.astype(F32).transpose(1, 0, 2)


def solution(mesh):
    placed = (
        P("dp", "col", "row"),
        P("row", None, "col"),
        P(None, None, "col"),
        P(None, "col"),
        P("dp", "row", "col"),
    )
    return jax.shard_map(
        on_device,
        mesh=mesh,
        in_specs=placed,
        out_specs=(P("dp", "col", "row"), P("row", None, "col")),
        check_vma=False,
    )
```

```python
import jax
import jax.numpy as jnp
from jax import lax
from jax.experimental import pallas as pl
from jax.experimental.pallas import tpu as pltpu
from jax.sharding import PartitionSpec as P

MESH = pl.DeviceIdType.MESH
NT = (((1,), (1,)), ((), ()))
CHUNKS = 6
HALO = 16
LANES = 128
SUBS = 4
RING = 4
ORDER = (
    "M0 M1 C0 X0", "M2 E0 X1 M3", "E1 C1 X2 M4", "E2 X3 M5 E3",
    "C2 X4 E4 X5", "E5 C3 Z0 Z1", "Z2 Z3 Z4 Z5", "C4 T0 T1 O0",
    "C5 T2 O1 T3", "O2 L0 C6 T4", "O3 L1 G0 T5", "O4 L2 L3 O5",
    "L4 L5",
)
F32 = jnp.float32
BF16 = jnp.bfloat16


class Place:
    def __init__(self):
        self.dp, self.row, self.col = (lax.axis_index(a) for a in ("dp", "row", "col"))
        self.x, self.zh = self.dp // 2, self.dp % 2
        self.y, self.core = self.row // 2, self.row % 2

    def at_x(self, by):
        return (((self.x + by + RING) % RING) * 2 + self.zh, self.row, self.col)

    def at_y(self, by):
        return (self.dp, ((self.y + by + RING) % RING) * 2 + self.core, self.col)

    def sibling(self):
        return (self.dp, self.y * 2 + 1 - self.core, self.col)

    def at_z(self, by):
        z = (self.zh * 8 + self.col + by + 16) % 16
        return (self.x * 2 + z // 8, self.row, z % 8)

    def at_col(self, by):
        return (self.dp, self.row, (self.col + by + 8) % 8)


def greet(partners):
    barrier = pltpu.get_barrier_semaphore()
    for partner in partners:
        pl.semaphore_signal(barrier, inc=1, device_id=partner, device_id_type=MESH)
    pl.semaphore_wait(barrier, len(partners))


class Sends:
    def __init__(self, sems):
        self.sems, self.copies = sems, []

    def start(self, src, dst, recv, device):
        copy = pltpu.make_async_remote_copy(
            src_ref=src, dst_ref=dst, send_sem=self.sems.at[len(self.copies)], recv_sem=recv,
            device_id=device, device_id_type=MESH,
        )
        copy.start()
        self.copies.append(copy)

    def finish(self):
        for copy in self.copies:
            copy.wait_send()


def arrived(ref, sem, place):
    pltpu.make_async_copy(ref, ref, sem).wait()


def whole_kernel(
    tile, w_hbm, ft, it, go_hbm, gx, dw,
    w, go, XG, XT, acc, psend, pair, Dy, yrel, yrec, win, goa,
    G, D, xrel, xrec, S, zrel, zrec, rr, rl, part,
    fetch_sem, sends, ag_send, ag_recv, p_send, p_recv, y_send, yrel_sem, yrec_sem, h_send, h_recv,
    col_send, g_recv, xrel_sem, xrec_sem, zrel_sem, zrec_sem, out_sem, rr_sem, rl_sem,
):
    me = Place()
    rows = tile.shape[0]
    half = rows // 2
    wide = w.shape[2]
    step = 3 * wide // CHUNKS
    per = wide // step
    right, left = me.at_y(1), me.at_y(-1)
    sibling = me.sibling()
    xr, xl = me.at_x(1), me.at_x(-1)
    up, down = me.at_z(4), me.at_z(-4)
    col_up, col_down = me.at_col(1), me.at_col(-1)
    far = (me.dp, (me.row + 2 * me.core + 7) % 8, me.col)
    own_rows = pl.ds(pl.multiple_of(me.col * rows, rows), rows)
    fetches = [
        pltpu.make_async_copy(tile, XG.at[own_rows], fetch_sem.at[0]),
        pltpu.make_async_copy(w_hbm, w, fetch_sem.at[1]),
        pltpu.make_async_copy(go_hbm, go, fetch_sem.at[2]),
    ]
    for copy in fetches:
        copy.start()
    greet([right, left, sibling, far, xr, xl, up, down, col_up, col_down])
    out = Sends(sends)
    top, bottom = pl.ds(0, half), pl.ds(half, half)
    halves = (top, bottom)

    before, after = (me.dp, (me.row + 7) % 8, me.col), (me.dp, (me.row + 1) % 8, me.col)

    def halo_copy(n):
        src, dst, device = (
            (go_hbm.at[pl.ds(0, HALO)], goa, before),
            (win.at[pl.ds(HALO, HALO)], win.at[pl.ds(rows + HALO, HALO)], before),
            (win.at[pl.ds(rows, HALO)], win.at[pl.ds(0, HALO)], after),
        )[n]
        return pltpu.make_async_remote_copy(
            src_ref=src, dst_ref=dst, send_sem=h_send.at[n], recv_sem=h_recv.at[n],
            device_id=device, device_id_type=MESH,
        )

    @pl.when(me.row > 0)
    def _():
        halo_copy(0).start()

    @pl.when(me.row == 0)
    def _():
        win[0:HALO, :] = jnp.zeros((HALO, 3 * wide), BF16)

    @pl.when(me.row == 7)
    def _():
        win[rows + HALO :, :] = jnp.zeros((HALO, 3 * wide), BF16)
        goa[...] = jnp.zeros_like(goa)

    def block_at(j):
        return pl.ds(pl.multiple_of(j * rows, rows), rows)

    def sub_at(j, u):
        sub = rows // SUBS
        return pl.ds(pl.multiple_of(j * rows + u * sub, sub), sub)

    def line_copy(j, u, device):
        return pltpu.make_async_remote_copy(
            src_ref=XG.at[sub_at(j, u)], dst_ref=XG.at[sub_at(j, u)], send_sem=ag_send.at[j, u],
            recv_sem=ag_recv.at[j, u], device_id=device, device_id_type=MESH,
        )

    def own_copy(n, u):
        sub = rows // SUBS
        return pltpu.make_async_remote_copy(
            src_ref=tile.at[pl.ds(u * sub, sub)], dst_ref=XG.at[sub_at(me.col, u)],
            send_sem=ag_send.at[8, u] if n else ag_send.at[me.col, u],
            recv_sem=ag_recv.at[me.col, u], device_id=col_down if n else col_up,
            device_id_type=MESH,
        )

    @pl.when(me.col < 7)
    def _():
        for u in range(SUBS):
            own_copy(0, u).start()

    @pl.when(me.col > 0)
    def _():
        for u in range(SUBS):
            own_copy(1, u).start()

    for copy in fetches:
        copy.wait()

    def pair_copy(p):
        return pltpu.make_async_remote_copy(
            src_ref=psend.at[p], dst_ref=pair.at[p], send_sem=p_send.at[p], recv_sem=p_recv.at[p],
            device_id=sibling, device_id_type=MESH,
        )

    def project(j):
        x = XG[block_at(j), :]
        p = j // 2
        mine = j % 2 == me.core
        for c in range(3):
            at = slice(c * wide, (c + 1) * wide)
            product = jnp.dot(x, w[c], preferred_element_type=F32)

            @pl.when(mine)
            def _():
                acc[p, :, at] = product

            @pl.when(jnp.logical_not(mine))
            def _():
                psend[p, :, at] = product.astype(BF16)

        @pl.when(jnp.logical_not(mine))
        def _():
            pair_copy(p).start()

        XT[:, block_at(j)] = x.T

    y_opp, y_r, y_l = ((me.y + by) % RING for by in (2, 1, 3))

    def y_copy(n):
        src, dst, sem, device = (
            (Dy.at[y_opp, top], yrel.at[0], yrel_sem.at[0], right),
            (Dy.at[y_opp, bottom], yrel.at[1], yrel_sem.at[1], left),
            (Dy.at[y_r, bottom], yrec.at[0, bottom], yrec_sem.at[0, 1], right),
            (Dy.at[y_l, top], yrec.at[1, top], yrec_sem.at[1, 0], left),
            (Dy.at[y_r, top], yrec.at[0, top], yrec_sem.at[0, 0], right),
            (Dy.at[y_l, bottom], yrec.at[1, bottom], yrec_sem.at[1, 1], left),
        )[n]
        return pltpu.make_async_remote_copy(
            src_ref=src, dst_ref=dst, send_sem=y_send.at[n], recv_sem=sem, device_id=device,
            device_id_type=MESH,
        )

    def piece(d):
        sign = (2 * (d % 2) - 1) * (1 - 2 * (me.col % 2))
        p = me.col // 2 + sign * (d // 2)
        return p, jnp.logical_and(jnp.logical_and(p >= 0, p < RING), jnp.logical_and(d >= 1, d <= 7))

    def pair_sum(d):
        p, there = piece(d)
        role = (p - me.y + RING) % RING

        @pl.when(there)
        def _():
            arrived(pair.at[p], p_recv.at[p], me)

        @pl.when(jnp.logical_and(there, role == 0))
        def _():
            acc[p] = acc[p] + pair[p].astype(F32)

        @pl.when(jnp.logical_and(there, role != 0))
        def _():
            Dy[p] = (acc[p] + pair[p].astype(F32)).astype(BF16)

        @pl.when(jnp.logical_and(there, role == 2))
        def _():
            y_copy(0).start()
            y_copy(1).start()

        @pl.when(jnp.logical_and(there, role == 1))
        def _():
            y_copy(2).start()

        @pl.when(jnp.logical_and(there, role == 3))
        def _():
            y_copy(3).start()

    def relay_y(d):
        p, there = piece(d)
        role = (p - me.y + RING) % RING

        @pl.when(jnp.logical_and(there, role == 1))
        def _():
            arrived(yrel.at[0], yrel_sem.at[0], me)
            Dy[p, top] = (Dy[p, top].astype(F32) + yrel[0].astype(F32)).astype(BF16)
            y_copy(4).start()

        @pl.when(jnp.logical_and(there, role == 3))
        def _():
            arrived(yrel.at[1], yrel_sem.at[1], me)
            Dy[p, bottom] = (Dy[p, bottom].astype(F32) + yrel[1].astype(F32)).astype(BF16)
            y_copy(5).start()

    def pass_on(d, some):
        @pl.when(jnp.logical_and(d <= 7, me.col - d >= 0))
        def _():
            j = me.col - d
            for u in some:
                arrived(XG.at[sub_at(j, u)], ag_recv.at[j, u], me)

                @pl.when(me.col < 7)
                def _():
                    line_copy(j, u, col_up).start()

        @pl.when(jnp.logical_and(d <= 7, me.col + d <= 7))
        def _():
            j = me.col + d
            for u in some:
                arrived(XG.at[sub_at(j, u)], ag_recv.at[j, u], me)

                @pl.when(me.col > 0)
                def _():
                    line_copy(j, u, col_down).start()

    def line_step(d, carry):
        last = d - 1
        pass_on(d, range(SUBS // 2))

        @pl.when(jnp.logical_and(last <= 7, me.col - last >= 0))
        def _():
            project(me.col - last)

        pass_on(d, range(SUBS // 2, SUBS))

        @pl.when(jnp.logical_and(jnp.logical_and(last >= 1, last <= 7), me.col + last <= 7))
        def _():
            project(me.col + last)

        relay_y(d - 3)
        pair_sum(d - 2)
        return carry

    lax.fori_loop(1, 11, line_step, 0)

    for side in range(2):
        for h in range(2):
            arrived(yrec.at[side, halves[h]], yrec_sem.at[side, h], me)
    win[HALO : rows + HALO, :] = (acc[me.y] + yrec[0].astype(F32) + yrec[1].astype(F32)).astype(BF16)

    @pl.when(me.row > 0)
    def _():
        halo_copy(1).start()

    @pl.when(me.row < 7)
    def _():
        halo_copy(2).start()

    @pl.when(me.row > 0)
    def _():
        arrived(win.at[pl.ds(0, HALO)], h_recv.at[2], me)

    @pl.when(me.row < 7)
    def _():
        arrived(win.at[pl.ds(rows + HALO, HALO)], h_recv.at[1], me)
        arrived(goa, h_recv.at[0], me)

    length = rows + 2 * HALO

    def causal(seq, taps):
        total = taps[0] * seq
        for lag in range(1, len(taps)):
            total = total + taps[lag] * pltpu.roll(seq, lag, 0)
        return total

    def anticausal(seq, taps):
        total = taps[0] * seq
        for lag in range(1, len(taps)):
            total = total + taps[lag] * pltpu.roll(seq, length - lag, 0)
        return total

    mine = block_at(me.row)

    def channels(n, carry):
        def at(c):
            return pl.ds(pl.multiple_of(c * wide + n * LANES, LANES), LANES)

        taps = [[ft[s, c : c + 1, at(0)] for s in range(3)] for c in range(3)]
        inner_taps = [it[s : s + 1, at(0)] for s in range(7)]
        query, key, value = (causal(win[:, at(c)].astype(F32), taps[c]) for c in range(3))
        upstream = jnp.concatenate(
            [
                jnp.zeros((HALO, LANES), F32),
                go[:, at(0)].astype(F32),
                goa[:, at(0)].astype(F32),
            ],
            axis=0,
        )
        product = (key * value).astype(BF16).astype(F32)
        inner = causal(product, inner_taps)
        grad_product = anticausal(upstream * query, inner_taps)
        mixed = (upstream * inner, grad_product * value, grad_product * key)
        for c in range(3):
            grad = anticausal(mixed[c], taps[c])
            G[mine, at(c)] = grad[HALO : rows + HALO].astype(BF16)
        return carry

    lax.fori_loop(0, wide // LANES, channels, 0)

    def g_at(slot, h):
        return G.at[pl.ds(pl.multiple_of(slot * rows + h * half, half), half)]

    def g_send(slot, h, device):
        out.start(g_at(slot, h), g_at(slot, h), g_recv.at[slot, h], device)

    def g_wait(slot, h):
        arrived(g_at(slot, h), g_recv.at[slot, h], me)

    def same(by):
        return ((me.y + by + RING) % RING) * 2 + me.core

    def other(by):
        return ((me.y + by + RING) % RING) * 2 + 1 - me.core

    g_send(me.row, 0, right)
    g_send(me.row, 1, left)
    g_send(me.row, 1, right)
    g_send(me.row, 0, left)
    for h in range(2):
        g_send(me.row, h, sibling)

    @pl.when(me.col == 7)
    def _():
        rr[...] = jnp.zeros_like(rr)

    @pl.when(me.col == 0)
    def _():
        rl[...] = jnp.zeros_like(rl)

    g_wait(same(-1), 0)
    g_send(same(-1), 0, right)
    g_send(same(-1), 0, sibling)
    g_wait(same(1), 1)
    g_send(same(1), 1, left)
    g_send(same(1), 1, sibling)
    g_wait(same(-1), 1)
    g_send(same(-1), 1, sibling)
    g_wait(same(1), 0)
    g_send(same(1), 0, sibling)
    g_wait(same(2), 0)
    g_send(same(2), 0, sibling)
    g_wait(same(2), 1)
    g_send(same(2), 1, sibling)
    for by in (0, -1, 1, 2):
        for h in range(2):
            g_wait(other(by), h)

    def grad_in_of(block):
        at = pl.ds(pl.multiple_of(block * rows, rows), rows)
        total = lax.dot_general(G[at, 0:wide], w[0], NT, preferred_element_type=F32)
        for c in range(1, 3):
            total = total + lax.dot_general(
                G[at, c * wide : (c + 1) * wide], w[c], NT, preferred_element_type=F32
            )
        return total

    def col_copy(block, side, h):
        landing, sems, device = ((rr, rr_sem, col_down), (rl, rl_sem, col_up))[side]
        return pltpu.make_async_remote_copy(
            src_ref=part.at[block, halves[h]], dst_ref=landing.at[block, halves[h]],
            send_sem=col_send.at[block, h], recv_sem=sems.at[block, h], device_id=device,
            device_id_type=MESH,
        )

    def col_pass(block, side, inner):
        landing, sems = ((rr, rr_sem), (rl, rl_sem))[side]
        total = grad_in_of(block)
        for h in range(2):

            @pl.when(inner)
            def _():
                arrived(landing.at[block, halves[h]], sems.at[block, h], me)

            own = total[h * half : (h + 1) * half]
            part[block, halves[h]] = (own + landing[block, halves[h]].astype(F32)).astype(BF16)
            col_copy(block, side, h).start()

    def col_round(s):
        @pl.when(s + me.col >= 7)
        def _():
            col_pass(s + me.col - 7, 0, me.col < 7)

        @pl.when(s >= me.col)
        def _():
            col_pass(7 - s + me.col, 1, me.col > 0)

    def col_last(unused):
        total = grad_in_of(me.col)
        for h in range(2):

            @pl.when(me.col < 7)
            def _():
                arrived(rr.at[me.col, halves[h]], rr_sem.at[me.col, h], me)

            @pl.when(me.col > 0)
            def _():
                arrived(rl.at[me.col, halves[h]], rl_sem.at[me.col, h], me)

        gx[...] = (total + rr[me.col].astype(F32) + rl[me.col].astype(F32)).astype(BF16)

        for block in range(8):
            for h in range(2):

                @pl.when(block < me.col)
                def _():
                    col_copy(block, 0, h).wait_send()

                @pl.when(block > me.col)
                def _():
                    col_copy(block, 1, h).wait_send()

    to_r, to_l, to_o = ((me.x + by + RING) % RING for by in (1, 3, 2))

    def dw_at(q, h, m):
        return dw.at[
            m // per,
            pl.ds(pl.multiple_of(q * rows + h * half, half), half),
            pl.ds((m % per) * step, step),
        ]

    def multiply(m):
        for q in range(RING):
            D[q, m] = jnp.dot(
                XT[q * rows : (q + 1) * rows, :], G[:, m * step : (m + 1) * step],
                preferred_element_type=F32,
            ).astype(BF16)
        out.start(D.at[to_o, m, top], xrel.at[0, m], xrel_sem.at[0, m], xr)
        out.start(D.at[to_o, m, bottom], xrel.at[1, m], xrel_sem.at[1, m], xl)
        out.start(D.at[to_r, m, bottom], xrec.at[0, m, bottom], xrec_sem.at[0, 1, m], xr)
        out.start(D.at[to_l, m, top], xrec.at[1, m, top], xrec_sem.at[1, 0, m], xl)

    def relay_x(m):
        arrived(xrel.at[0, m], xrel_sem.at[0, m], me)
        D[to_r, m, top] = (D[to_r, m, top].astype(F32) + xrel[0, m].astype(F32)).astype(BF16)
        out.start(D.at[to_r, m, top], xrec.at[0, m, top], xrec_sem.at[0, 0, m], xr)
        arrived(xrel.at[1, m], xrel_sem.at[1, m], me)
        D[to_l, m, bottom] = (D[to_l, m, bottom].astype(F32) + xrel[1, m].astype(F32)).astype(BF16)
        out.start(D.at[to_l, m, bottom], xrec.at[1, m, bottom], xrec_sem.at[1, 1, m], xl)

    def exchange(m):
        for side in range(2):
            for h in range(2):
                arrived(xrec.at[side, m, halves[h]], xrec_sem.at[side, h, m], me)
        S[m] = (D[me.x, m].astype(F32) + xrec[0, m].astype(F32) + xrec[1, m].astype(F32)).astype(BF16)
        out.start(S.at[m, top], zrel.at[0, m], zrel_sem.at[0, m], up)
        out.start(S.at[m, bottom], zrel.at[1, m], zrel_sem.at[1, m], down)

    def relay_z(m):
        arrived(zrel.at[0, m], zrel_sem.at[0, m], me)
        out.start(zrel.at[0, m], zrec.at[m, top], zrec_sem.at[0, m], up)
        arrived(zrel.at[1, m], zrel_sem.at[1, m], me)
        out.start(zrel.at[1, m], zrec.at[m, bottom], zrec_sem.at[1, m], down)

    def gather(q, h, m, device):
        out.start(dw_at(q, h, m), dw_at(q, h, m), out_sem.at[q, h, m], device)

    def gathered(q, h, m):
        arrived(dw_at(q, h, m), out_sem.at[q, h, m], me)

    def total_of(m):
        for h in range(2):
            arrived(zrec.at[m, halves[h]], zrec_sem.at[h, m], me)
        dw[
            m // per, pl.ds(pl.multiple_of(me.x * rows, rows), rows), pl.ds((m % per) * step, step)
        ] = (S[m].astype(F32) + zrec[m].astype(F32)).astype(BF16)
        gather(me.x, 0, m, xr)
        gather(me.x, 1, m, xl)
        gather(me.x, 1, m, xr)
        gather(me.x, 0, m, xl)

    def relay_out(m):
        gathered(to_l, 0, m)
        gather(to_l, 0, m, xr)
        gathered(to_r, 1, m)
        gather(to_r, 1, m, xl)

    def last_out(m):
        gathered(to_l, 1, m)
        gathered(to_r, 0, m)
        gathered(to_o, 0, m)
        gathered(to_o, 1, m)

    stages = {
        "M": multiply, "X": relay_x, "E": exchange, "Z": relay_z, "T": total_of, "O": relay_out,
        "L": last_out, "C": col_round, "G": col_last,
    }
    for group in ORDER:
        for name in group.split():
            stages[name[0]](int(name[1]))
    out.finish()

    @pl.when(me.col < 7)
    def _():
        for u in range(SUBS):
            own_copy(0, u).wait_send()

    @pl.when(me.col > 0)
    def _():
        for u in range(SUBS):
            own_copy(1, u).wait_send()

    for j in range(8):

        @pl.when(jnp.logical_and(j < me.col, me.col < 7))
        def _():
            for u in range(SUBS):
                line_copy(j, u, col_up).wait_send()

        @pl.when(jnp.logical_and(j > me.col, me.col > 0))
        def _():
            for u in range(SUBS):
                line_copy(j, u, col_down).wait_send()

    for p in range(RING):
        pair_copy(p).wait_send()
    for n in range(6):
        y_copy(n).wait_send()

    @pl.when(me.row > 0)
    def _():
        halo_copy(0).wait_send()
        halo_copy(1).wait_send()

    @pl.when(me.row < 7)
    def _():
        halo_copy(2).wait_send()


SENDS = 6 + 8 + CHUNKS * (4 + 2 + 2 + 2 + 4 + 2)


def whole(tile, w, ft, it, go):
    rows, wide, deep = tile.shape[0], w.shape[2], w.shape[1]
    half, step = rows // 2, 3 * wide // CHUNKS
    vmem, sem = pltpu.VMEM, pltpu.SemaphoreType.DMA
    return pl.pallas_call(
        whole_kernel,
        out_shape=(jax.ShapeDtypeStruct((rows, deep), BF16), jax.ShapeDtypeStruct(w.shape, BF16)),
        in_specs=[
            pl.BlockSpec(memory_space=space) for space in (pl.ANY, pl.ANY, vmem, vmem, pl.ANY)
        ],
        out_specs=(pl.BlockSpec(memory_space=pltpu.VMEM),) * 2,
        scratch_shapes=[
            vmem(w.shape, BF16),
            vmem((rows, wide), BF16),
            vmem((8 * rows, deep), BF16),
            vmem((deep, 8 * rows), BF16),
            vmem((RING, rows, 3 * wide), F32),
            vmem((RING, rows, 3 * wide), BF16),
            vmem((RING, rows, 3 * wide), BF16),
            vmem((RING, rows, 3 * wide), BF16),
            vmem((2, half, 3 * wide), BF16),
            vmem((2, rows, 3 * wide), BF16),
            vmem((rows + 2 * HALO, 3 * wide), BF16),
            vmem((HALO, wide), BF16),
            vmem((8 * rows, 3 * wide), BF16),
            vmem((RING, CHUNKS, rows, step), BF16),
            vmem((2, CHUNKS, half, step), BF16),
            vmem((2, CHUNKS, rows, step), BF16),
            vmem((CHUNKS, rows, step), BF16),
            vmem((2, CHUNKS, half, step), BF16),
            vmem((CHUNKS, rows, step), BF16),
            vmem((8, rows, deep), BF16),
            vmem((8, rows, deep), BF16),
            vmem((8, rows, deep), BF16),
            sem((3,)),
            sem((SENDS,)),
            sem((9, SUBS)),
            sem((8, SUBS)),
            sem((RING,)),
            sem((RING,)),
            sem((6,)),
            sem((2,)),
            sem((2, 2)),
            sem((3,)),
            sem((3,)),
            sem((8, 2)),
            sem((8, 2)),
            sem((2, CHUNKS)),
            sem((2, 2, CHUNKS)),
            sem((2, CHUNKS)),
            sem((2, CHUNKS)),
            sem((RING, 2, CHUNKS)),
            sem((8, 2)),
            sem((8, 2)),
        ],
        compiler_params=pltpu.CompilerParams(
            collective_id=1, has_side_effects=True, vmem_limit_bytes=50 * 2**20
        ),
        name="whole",
    )(tile, w, ft, it, go)


def on_device(inputs, weights, feature_taps, inner_taps, grad_out):
    grad_x, grad_w = whole(
        inputs[0], weights.transpose(1, 0, 2), feature_taps, inner_taps, grad_out[0]
    )
    return grad_x[None], grad_w.astype(F32).transpose(1, 0, 2)


def solution(mesh):
    placed = (
        P("dp", "col", "row"),
        P("row", None, "col"),
        P(None, None, "col"),
        P(None, "col"),
        P("dp", "row", "col"),
    )
    return jax.shard_map(
        on_device,
        mesh=mesh,
        in_specs=placed,
        out_specs=(P("dp", "col", "row"), P("row", None, "col")),
        check_vma=False,
    )
```

```python
import jax
import jax.numpy as jnp
from jax import lax
from jax.experimental import pallas as pl
from jax.experimental.pallas import tpu as pltpu
from jax.sharding import PartitionSpec as P

MESH = pl.DeviceIdType.MESH
NT = (((1,), (1,)), ((), ()))
CHUNKS = 4
HALO = 16
LANES = 128
SUBS = 4
RING = 4
ORDER = (
    "F0 F1 H0 F2", "H1 F3 H2 A0", "H3 A1 B0 A2", "B1 W0 M0 A3",
    "B2 W1 M1 X0", "B3 E0 W2 M2", "X1 E1 W3 M3", "X2 E2 Z0 C0",
    "X3 E3 Z1 C1", "Z2 C2 Z3 C3", "T0 C4 O0 T1", "C5 O1 L0 T2",
    "C6 O2 L1 T3", "G0 O3 L2 L3",
)
F32 = jnp.float32
BF16 = jnp.bfloat16


class Place:
    def __init__(self):
        self.dp, self.row, self.col = (lax.axis_index(a) for a in ("dp", "row", "col"))
        self.x, self.zh = self.dp // 2, self.dp % 2
        self.y, self.core = self.row // 2, self.row % 2

    def at_x(self, by):
        return (((self.x + by + RING) % RING) * 2 + self.zh, self.row, self.col)

    def at_y(self, by):
        return (self.dp, ((self.y + by + RING) % RING) * 2 + self.core, self.col)

    def sibling(self):
        return (self.dp, self.y * 2 + 1 - self.core, self.col)

    def at_z(self, by):
        z = (self.zh * 8 + self.col + by + 16) % 16
        return (self.x * 2 + z // 8, self.row, z % 8)

    def at_col(self, by):
        return (self.dp, self.row, (self.col + by + 8) % 8)


def greet(partners):
    barrier = pltpu.get_barrier_semaphore()
    for partner in partners:
        pl.semaphore_signal(barrier, inc=1, device_id=partner, device_id_type=MESH)
    pl.semaphore_wait(barrier, len(partners))


class Sends:
    def __init__(self, sems):
        self.sems, self.copies = sems, []

    def start(self, src, dst, recv, device):
        copy = pltpu.make_async_remote_copy(
            src_ref=src, dst_ref=dst, send_sem=self.sems.at[len(self.copies)], recv_sem=recv,
            device_id=device, device_id_type=MESH,
        )
        copy.start()
        self.copies.append(copy)

    def finish(self):
        for copy in self.copies:
            copy.wait_send()


def arrived(ref, sem, place):
    pltpu.make_async_copy(ref, ref, sem).wait()


def whole_kernel(
    tile, w_hbm, ft_hbm, it_hbm, go_hbm, gx, dw,
    w, ft, it, go, XG, XT, acc, psend, pair, Dy, yrel, yrec, win, goa,
    G, D, xrel, xrec, S, zrel, zrec, rr, rl, part,
    fetch_sem, sends, ag_send, ag_recv, p_send, p_recv, y_send, yrel_sem, yrec_sem, h_send, h_recv,
    col_send, g_recv, xrel_sem, xrec_sem, zrel_sem, zrec_sem, out_sem, rr_sem, rl_sem,
):
    me = Place()
    rows = tile.shape[0]
    half = rows // 2
    step = 3 * LANES
    right, left = me.at_y(1), me.at_y(-1)
    sibling = me.sibling()
    xr, xl = me.at_x(1), me.at_x(-1)
    up, down = me.at_z(4), me.at_z(-4)
    col_up, col_down = me.at_col(1), me.at_col(-1)
    far = (me.dp, (me.row + 2 * me.core + 7) % 8, me.col)
    own_rows = pl.ds(pl.multiple_of(me.col * rows, rows), rows)
    fetches = [
        pltpu.make_async_copy(tile, XG.at[own_rows], fetch_sem.at[0]),
        pltpu.make_async_copy(go_hbm, go, fetch_sem.at[1]),
        pltpu.make_async_copy(ft_hbm, ft, fetch_sem.at[2]),
        pltpu.make_async_copy(it_hbm, it, fetch_sem.at[3]),
    ]
    for n in range(CHUNKS):
        for c in range(3):
            lanes, to = pl.ds(n * LANES, LANES), pl.ds(c * LANES, LANES)
            fetches.append(
                pltpu.make_async_copy(
                    w_hbm.at[c, :, lanes], w.at[n, :, to], fetch_sem.at[4 + 3 * n + c]
                )
            )
    for copy in fetches:
        copy.start()
    greet([right, left, sibling, far, xr, xl, up, down, col_up, col_down])
    out = Sends(sends)
    top, bottom = pl.ds(0, half), pl.ds(half, half)
    halves = (top, bottom)

    before, after = (me.dp, (me.row + 7) % 8, me.col), (me.dp, (me.row + 1) % 8, me.col)

    goa_copy = pltpu.make_async_remote_copy(
        src_ref=go_hbm.at[pl.ds(0, HALO)], dst_ref=goa, send_sem=h_send.at[2, 0],
        recv_sem=h_recv.at[2, 0], device_id=before, device_id_type=MESH,
    )

    def halo_copy(side, n):
        src, dst, device = (
            (pl.ds(HALO, HALO), pl.ds(rows + HALO, HALO), before),
            (pl.ds(rows, HALO), pl.ds(0, HALO), after),
        )[side]
        return pltpu.make_async_remote_copy(
            src_ref=win.at[n, src], dst_ref=win.at[n, dst], send_sem=h_send.at[side, n],
            recv_sem=h_recv.at[side, n], device_id=device, device_id_type=MESH,
        )

    @pl.when(me.row > 0)
    def _():
        goa_copy.start()

    @pl.when(me.row == 0)
    def _():
        win[:, 0:HALO, :] = jnp.zeros((CHUNKS, HALO, step), BF16)

    @pl.when(me.row == 7)
    def _():
        win[:, rows + HALO :, :] = jnp.zeros((CHUNKS, HALO, step), BF16)
        goa[...] = jnp.zeros_like(goa)

    def block_at(j):
        return pl.ds(pl.multiple_of(j * rows, rows), rows)

    def sub_at(j, u):
        sub = rows // SUBS
        return pl.ds(pl.multiple_of(j * rows + u * sub, sub), sub)

    def line_copy(j, u, device):
        return pltpu.make_async_remote_copy(
            src_ref=XG.at[sub_at(j, u)], dst_ref=XG.at[sub_at(j, u)], send_sem=ag_send.at[j, u],
            recv_sem=ag_recv.at[j, u], device_id=device, device_id_type=MESH,
        )

    def own_copy(n, u):
        sub = rows // SUBS
        return pltpu.make_async_remote_copy(
            src_ref=tile.at[pl.ds(u * sub, sub)], dst_ref=XG.at[sub_at(me.col, u)],
            send_sem=ag_send.at[8, u] if n else ag_send.at[me.col, u],
            recv_sem=ag_recv.at[me.col, u], device_id=col_down if n else col_up,
            device_id_type=MESH,
        )

    @pl.when(me.col < 7)
    def _():
        for u in range(SUBS):
            own_copy(0, u).start()

    @pl.when(me.col > 0)
    def _():
        for u in range(SUBS):
            own_copy(1, u).start()

    for copy in fetches:
        copy.wait()

    def pair_copy(p, n):
        return pltpu.make_async_remote_copy(
            src_ref=psend.at[p, n], dst_ref=pair.at[p, n], send_sem=p_send.at[p, n],
            recv_sem=p_recv.at[p, n], device_id=sibling, device_id_type=MESH,
        )

    def project(j):
        x = XG[block_at(j), :]
        p = j // 2
        mine = j % 2 == me.core
        for n in range(CHUNKS):
            product = jnp.dot(x, w[n], preferred_element_type=F32)

            @pl.when(mine)
            def _():
                acc[p, n] = product

            @pl.when(jnp.logical_not(mine))
            def _():
                psend[p, n] = product.astype(BF16)
                pair_copy(p, n).start()

        XT[:, block_at(j)] = x.T

    y_opp, y_r, y_l = ((me.y + by) % RING for by in (2, 1, 3))

    def y_copy(k, n):
        src, dst, sem, device = (
            (Dy.at[y_opp, n, top], yrel.at[0, n], yrel_sem.at[0, n], right),
            (Dy.at[y_opp, n, bottom], yrel.at[1, n], yrel_sem.at[1, n], left),
            (Dy.at[y_r, n, bottom], yrec.at[0, n, bottom], yrec_sem.at[0, 1, n], right),
            (Dy.at[y_l, n, top], yrec.at[1, n, top], yrec_sem.at[1, 0, n], left),
            (Dy.at[y_r, n, top], yrec.at[0, n, top], yrec_sem.at[0, 0, n], right),
            (Dy.at[y_l, n, bottom], yrec.at[1, n, bottom], yrec_sem.at[1, 1, n], left),
        )[k]
        return pltpu.make_async_remote_copy(
            src_ref=src, dst_ref=dst, send_sem=y_send.at[k, n], recv_sem=sem, device_id=device,
            device_id_type=MESH,
        )

    def piece(d):
        sign = (2 * (d % 2) - 1) * (1 - 2 * (me.col % 2))
        p = me.col // 2 + sign * (d // 2)
        return p, jnp.logical_and(jnp.logical_and(p >= 0, p < RING), jnp.logical_and(d >= 1, d <= 7))

    def pair_sum(d):
        p, there = piece(d)
        role = (p - me.y + RING) % RING

        for n in range(CHUNKS):

            @pl.when(there)
            def _():
                arrived(pair.at[p, n], p_recv.at[p, n], me)

            @pl.when(jnp.logical_and(there, role == 0))
            def _():
                acc[p, n] = acc[p, n] + pair[p, n].astype(F32)

            @pl.when(jnp.logical_and(there, role != 0))
            def _():
                Dy[p, n] = (acc[p, n] + pair[p, n].astype(F32)).astype(BF16)

            @pl.when(jnp.logical_and(there, role == 2))
            def _():
                y_copy(0, n).start()
                y_copy(1, n).start()

            @pl.when(jnp.logical_and(there, role == 1))
            def _():
                y_copy(2, n).start()

            @pl.when(jnp.logical_and(there, role == 3))
            def _():
                y_copy(3, n).start()

    def relay_y(d):
        p, there = piece(d)
        role = (p - me.y + RING) % RING

        @pl.when(jnp.logical_and(there, role == 1))
        def _():
            for n in range(CHUNKS):
                arrived(yrel.at[0, n], yrel_sem.at[0, n], me)
                Dy[p, n, top] = (Dy[p, n, top].astype(F32) + yrel[0, n].astype(F32)).astype(BF16)
                y_copy(4, n).start()

        @pl.when(jnp.logical_and(there, role == 3))
        def _():
            for n in range(CHUNKS):
                arrived(yrel.at[1, n], yrel_sem.at[1, n], me)
                Dy[p, n, bottom] = (
                    Dy[p, n, bottom].astype(F32) + yrel[1, n].astype(F32)
                ).astype(BF16)
                y_copy(5, n).start()

    def pass_on(d, some):
        @pl.when(jnp.logical_and(d <= 7, me.col - d >= 0))
        def _():
            j = me.col - d
            for u in some:
                arrived(XG.at[sub_at(j, u)], ag_recv.at[j, u], me)

                @pl.when(me.col < 7)
                def _():
                    line_copy(j, u, col_up).start()

        @pl.when(jnp.logical_and(d <= 7, me.col + d <= 7))
        def _():
            j = me.col + d
            for u in some:
                arrived(XG.at[sub_at(j, u)], ag_recv.at[j, u], me)

                @pl.when(me.col > 0)
                def _():
                    line_copy(j, u, col_down).start()

    def line_step(d, carry):
        last = d - 1
        pass_on(d, range(SUBS // 2))

        @pl.when(jnp.logical_and(last <= 7, me.col - last >= 0))
        def _():
            project(me.col - last)

        pass_on(d, range(SUBS // 2, SUBS))

        @pl.when(jnp.logical_and(jnp.logical_and(last >= 1, last <= 7), me.col + last <= 7))
        def _():
            project(me.col + last)

        relay_y(d - 3)
        pair_sum(d - 2)
        return carry

    lax.fori_loop(1, 11, line_step, 0)

    def projection(n):
        for side in range(2):
            for h in range(2):
                arrived(yrec.at[side, n, halves[h]], yrec_sem.at[side, h, n], me)
        total = acc[me.y, n] + yrec[0, n].astype(F32) + yrec[1, n].astype(F32)
        win[n, HALO : rows + HALO, :] = total.astype(BF16)

        @pl.when(me.row > 0)
        def _():
            halo_copy(0, n).start()

        @pl.when(me.row < 7)
        def _():
            halo_copy(1, n).start()

    length = rows + 2 * HALO

    def causal(seq, taps):
        total = taps[0] * seq
        for lag in range(1, len(taps)):
            total = total + taps[lag] * pltpu.roll(seq, lag, 0)
        return total

    def anticausal(seq, taps):
        total = taps[0] * seq
        for lag in range(1, len(taps)):
            total = total + taps[lag] * pltpu.roll(seq, length - lag, 0)
        return total

    own_block = block_at(me.row)

    def channels(n):
        @pl.when(me.row > 0)
        def _():
            arrived(win.at[n, pl.ds(0, HALO)], h_recv.at[1, n], me)

        @pl.when(me.row < 7)
        def _():
            arrived(win.at[n, pl.ds(rows + HALO, HALO)], h_recv.at[0, n], me)

            if n == 0:
                arrived(goa, h_recv.at[2, 0], me)

        lanes = slice(n * LANES, (n + 1) * LANES)
        parts = [slice(c * LANES, (c + 1) * LANES) for c in range(3)]
        taps = [[ft[s, c : c + 1, lanes] for s in range(3)] for c in range(3)]
        inner_taps = [it[s : s + 1, lanes] for s in range(7)]
        query, key, value = (causal(win[n, :, parts[c]].astype(F32), taps[c]) for c in range(3))
        upstream = jnp.concatenate(
            [jnp.zeros((HALO, LANES), F32), go[:, lanes].astype(F32), goa[:, lanes].astype(F32)],
            axis=0,
        )
        product = (key * value).astype(BF16).astype(F32)
        inner = causal(product, inner_taps)
        grad_product = anticausal(upstream * query, inner_taps)
        mixed = (upstream * inner, grad_product * value, grad_product * key)
        for c in range(3):
            grad = anticausal(mixed[c], taps[c])
            G[n, own_block, parts[c]] = grad[HALO : rows + HALO].astype(BF16)
        g_send(me.row, 0, n, right)
        g_send(me.row, 1, n, left)
        g_send(me.row, 1, n, right)
        g_send(me.row, 0, n, left)
        for h in range(2):
            g_send(me.row, h, n, sibling)

    def g_at(slot, h, n):
        return G.at[n, pl.ds(pl.multiple_of(slot * rows + h * half, half), half)]

    def g_send(slot, h, n, device):
        out.start(g_at(slot, h, n), g_at(slot, h, n), g_recv.at[slot, h, n], device)

    def g_wait(slot, h, n):
        arrived(g_at(slot, h, n), g_recv.at[slot, h, n], me)

    def same(by):
        return ((me.y + by + RING) % RING) * 2 + me.core

    def other(by):
        return ((me.y + by + RING) % RING) * 2 + 1 - me.core

    @pl.when(me.col == 7)
    def _():
        rr[...] = jnp.zeros_like(rr)

    @pl.when(me.col == 0)
    def _():
        rl[...] = jnp.zeros_like(rl)

    def relay_g(n):
        g_wait(same(-1), 0, n)
        g_send(same(-1), 0, n, right)
        g_send(same(-1), 0, n, sibling)
        g_wait(same(1), 1, n)
        g_send(same(1), 1, n, left)
        g_send(same(1), 1, n, sibling)
        g_wait(same(-1), 1, n)
        g_send(same(-1), 1, n, sibling)
        g_wait(same(1), 0, n)
        g_send(same(1), 0, n, sibling)

    def share_g(n):
        for h in range(2):
            g_wait(same(2), h, n)
            g_send(same(2), h, n, sibling)

    def whole_g(n):
        for by in (0, -1, 1, 2):
            for h in range(2):
                g_wait(other(by), h, n)

    def grad_in_of(block):
        at = pl.ds(pl.multiple_of(block * rows, rows), rows)
        total = lax.dot_general(G[0, at], w[0], NT, preferred_element_type=F32)
        for n in range(1, CHUNKS):
            total = total + lax.dot_general(G[n, at], w[n], NT, preferred_element_type=F32)
        return total

    def col_copy(block, side, h):
        landing, sems, device = ((rr, rr_sem, col_down), (rl, rl_sem, col_up))[side]
        return pltpu.make_async_remote_copy(
            src_ref=part.at[block, halves[h]], dst_ref=landing.at[block, halves[h]],
            send_sem=col_send.at[block, h], recv_sem=sems.at[block, h], device_id=device,
            device_id_type=MESH,
        )

    def col_pass(block, side, inner):
        landing, sems = ((rr, rr_sem), (rl, rl_sem))[side]
        total = grad_in_of(block)
        for h in range(2):

            @pl.when(inner)
            def _():
                arrived(landing.at[block, halves[h]], sems.at[block, h], me)

            own = total[h * half : (h + 1) * half]
            part[block, halves[h]] = (own + landing[block, halves[h]].astype(F32)).astype(BF16)
            col_copy(block, side, h).start()

    def col_round(s):
        @pl.when(s + me.col >= 7)
        def _():
            col_pass(s + me.col - 7, 0, me.col < 7)

        @pl.when(s >= me.col)
        def _():
            col_pass(7 - s + me.col, 1, me.col > 0)

    def col_last(unused):
        total = grad_in_of(me.col)
        for h in range(2):

            @pl.when(me.col < 7)
            def _():
                arrived(rr.at[me.col, halves[h]], rr_sem.at[me.col, h], me)

            @pl.when(me.col > 0)
            def _():
                arrived(rl.at[me.col, halves[h]], rl_sem.at[me.col, h], me)

        gx[...] = (total + rr[me.col].astype(F32) + rl[me.col].astype(F32)).astype(BF16)

        for block in range(8):
            for h in range(2):

                @pl.when(block < me.col)
                def _():
                    col_copy(block, 0, h).wait_send()

                @pl.when(block > me.col)
                def _():
                    col_copy(block, 1, h).wait_send()

    to_r, to_l, to_o = ((me.x + by + RING) % RING for by in (1, 3, 2))

    def dw_at(q, h, m):
        return dw.at[
            :, pl.ds(pl.multiple_of(q * rows + h * half, half), half), pl.ds(m * LANES, LANES)
        ]

    def multiply(m):
        for q in range(RING):
            D[q, m] = jnp.dot(
                XT[q * rows : (q + 1) * rows, :], G[m], preferred_element_type=F32
            ).astype(BF16)
        out.start(D.at[to_o, m, top], xrel.at[0, m], xrel_sem.at[0, m], xr)
        out.start(D.at[to_o, m, bottom], xrel.at[1, m], xrel_sem.at[1, m], xl)
        out.start(D.at[to_r, m, bottom], xrec.at[0, m, bottom], xrec_sem.at[0, 1, m], xr)
        out.start(D.at[to_l, m, top], xrec.at[1, m, top], xrec_sem.at[1, 0, m], xl)

    def relay_x(m):
        arrived(xrel.at[0, m], xrel_sem.at[0, m], me)
        D[to_r, m, top] = (D[to_r, m, top].astype(F32) + xrel[0, m].astype(F32)).astype(BF16)
        out.start(D.at[to_r, m, top], xrec.at[0, m, top], xrec_sem.at[0, 0, m], xr)
        arrived(xrel.at[1, m], xrel_sem.at[1, m], me)
        D[to_l, m, bottom] = (D[to_l, m, bottom].astype(F32) + xrel[1, m].astype(F32)).astype(BF16)
        out.start(D.at[to_l, m, bottom], xrec.at[1, m, bottom], xrec_sem.at[1, 1, m], xl)

    def exchange(m):
        for side in range(2):
            for h in range(2):
                arrived(xrec.at[side, m, halves[h]], xrec_sem.at[side, h, m], me)
        S[m] = (D[me.x, m].astype(F32) + xrec[0, m].astype(F32) + xrec[1, m].astype(F32)).astype(BF16)
        out.start(S.at[m, top], zrel.at[0, m], zrel_sem.at[0, m], up)
        out.start(S.at[m, bottom], zrel.at[1, m], zrel_sem.at[1, m], down)

    def relay_z(m):
        arrived(zrel.at[0, m], zrel_sem.at[0, m], me)
        out.start(zrel.at[0, m], zrec.at[m, top], zrec_sem.at[0, m], up)
        arrived(zrel.at[1, m], zrel_sem.at[1, m], me)
        out.start(zrel.at[1, m], zrec.at[m, bottom], zrec_sem.at[1, m], down)

    def gather(q, h, m, device):
        out.start(dw_at(q, h, m), dw_at(q, h, m), out_sem.at[q, h, m], device)

    def gathered(q, h, m):
        arrived(dw_at(q, h, m), out_sem.at[q, h, m], me)

    def total_of(m):
        for h in range(2):
            arrived(zrec.at[m, halves[h]], zrec_sem.at[h, m], me)
        total = (S[m].astype(F32) + zrec[m].astype(F32)).astype(BF16)
        own_rows_x = pl.ds(pl.multiple_of(me.x * rows, rows), rows)
        for c in range(3):
            dw[c, own_rows_x, m * LANES : (m + 1) * LANES] = total[:, c * LANES : (c + 1) * LANES]
        gather(me.x, 0, m, xr)
        gather(me.x, 1, m, xl)
        gather(me.x, 1, m, xr)
        gather(me.x, 0, m, xl)

    def relay_out(m):
        gathered(to_l, 0, m)
        gather(to_l, 0, m, xr)
        gathered(to_r, 1, m)
        gather(to_r, 1, m, xl)

    def last_out(m):
        gathered(to_l, 1, m)
        gathered(to_r, 0, m)
        gathered(to_o, 0, m)
        gathered(to_o, 1, m)

    stages = {
        "F": projection, "H": channels, "A": relay_g, "B": share_g, "W": whole_g,
        "M": multiply, "X": relay_x, "E": exchange, "Z": relay_z, "T": total_of, "O": relay_out,
        "L": last_out, "C": col_round, "G": col_last,
    }
    for group in ORDER:
        for name in group.split():
            stages[name[0]](int(name[1]))
    out.finish()

    @pl.when(me.col < 7)
    def _():
        for u in range(SUBS):
            own_copy(0, u).wait_send()

    @pl.when(me.col > 0)
    def _():
        for u in range(SUBS):
            own_copy(1, u).wait_send()

    for j in range(8):

        @pl.when(jnp.logical_and(j < me.col, me.col < 7))
        def _():
            for u in range(SUBS):
                line_copy(j, u, col_up).wait_send()

        @pl.when(jnp.logical_and(j > me.col, me.col > 0))
        def _():
            for u in range(SUBS):
                line_copy(j, u, col_down).wait_send()

    for n in range(CHUNKS):
        for p in range(RING):
            pair_copy(p, n).wait_send()
        for k in range(6):
            y_copy(k, n).wait_send()

    @pl.when(me.row > 0)
    def _():
        goa_copy.wait_send()
        for n in range(CHUNKS):
            halo_copy(0, n).wait_send()

    @pl.when(me.row < 7)
    def _():
        for n in range(CHUNKS):
            halo_copy(1, n).wait_send()


SENDS = CHUNKS * (6 + 8 + 4 + 2 + 2 + 2 + 4 + 2)


def whole(tile, w, ft, it, go):
    rows, wide, deep = tile.shape[0], w.shape[2], w.shape[1]
    half, step = rows // 2, 3 * LANES
    vmem, sem = pltpu.VMEM, pltpu.SemaphoreType.DMA
    return pl.pallas_call(
        whole_kernel,
        out_shape=(jax.ShapeDtypeStruct((rows, deep), BF16), jax.ShapeDtypeStruct(w.shape, BF16)),
        in_specs=[
            pl.BlockSpec(memory_space=pltpu.HBM) for _ in range(5)
        ],
        out_specs=(pl.BlockSpec(memory_space=pltpu.VMEM),) * 2,
        scratch_shapes=[
            vmem((CHUNKS, deep, step), BF16),
            vmem(ft.shape, F32),
            vmem(it.shape, F32),
            vmem((rows, wide), BF16),
            vmem((8 * rows, deep), BF16),
            vmem((deep, 8 * rows), BF16),
            vmem((RING, CHUNKS, rows, step), F32),
            vmem((RING, CHUNKS, rows, step), BF16),
            vmem((RING, CHUNKS, rows, step), BF16),
            vmem((RING, CHUNKS, rows, step), BF16),
            vmem((2, CHUNKS, half, step), BF16),
            vmem((2, CHUNKS, rows, step), BF16),
            vmem((CHUNKS, rows + 2 * HALO, step), BF16),
            vmem((HALO, wide), BF16),
            vmem((CHUNKS, 8 * rows, step), BF16),
            vmem((RING, CHUNKS, rows, step), BF16),
            vmem((2, CHUNKS, half, step), BF16),
            vmem((2, CHUNKS, rows, step), BF16),
            vmem((CHUNKS, rows, step), BF16),
            vmem((2, CHUNKS, half, step), BF16),
            vmem((CHUNKS, rows, step), BF16),
            vmem((8, rows, deep), BF16),
            vmem((8, rows, deep), BF16),
            vmem((8, rows, deep), BF16),
            sem((4 + 3 * CHUNKS,)),
            sem((SENDS,)),
            sem((9, SUBS)),
            sem((8, SUBS)),
            sem((RING, CHUNKS)),
            sem((RING, CHUNKS)),
            sem((6, CHUNKS)),
            sem((2, CHUNKS)),
            sem((2, 2, CHUNKS)),
            sem((3, CHUNKS)),
            sem((3, CHUNKS)),
            sem((8, 2)),
            sem((8, 2, CHUNKS)),
            sem((2, CHUNKS)),
            sem((2, 2, CHUNKS)),
            sem((2, CHUNKS)),
            sem((2, CHUNKS)),
            sem((RING, 2, CHUNKS)),
            sem((8, 2)),
            sem((8, 2)),
        ],
        compiler_params=pltpu.CompilerParams(
            collective_id=1, has_side_effects=True, vmem_limit_bytes=50 * 2**20
        ),
        name="whole",
    )(tile, w, ft, it, go)


def on_device(inputs, weights, feature_taps, inner_taps, grad_out):
    grad_x, grad_w = whole(
        inputs[0], weights.transpose(1, 0, 2), feature_taps, inner_taps, grad_out[0]
    )
    return grad_x[None], grad_w.astype(F32).transpose(1, 0, 2)


def solution(mesh):
    placed = (
        P("dp", "col", "row"),
        P("row", None, "col"),
        P(None, None, "col"),
        P(None, "col"),
        P("dp", "row", "col"),
    )
    return jax.shard_map(
        on_device,
        mesh=mesh,
        in_specs=placed,
        out_specs=(P("dp", "col", "row"), P("row", None, "col")),
        check_vma=False,
    )
```

```python
import jax
import jax.numpy as jnp
from jax import lax
from jax.experimental import pallas as pl
from jax.experimental.pallas import tpu as pltpu
from jax.sharding import PartitionSpec as P

MESH = pl.DeviceIdType.MESH
NT = (((1,), (1,)), ((), ()))
CHUNKS = 4
HALO = 16
LANES = 128
SUBS = 4
RING = 4
ORDER = (
    "F3 F0 F1 F2", "H1 H2 H0 H3", "K0 M0 A0 A1", "X0 A2 A3 E0",
    "B0 B1 W1 M1", "X1 B2 B3 E1", "W2 M2 X2 E2", "W3 M3 Z0 X3",
    "E3 C0 Z1 C1", "T0 Z2 C2 O0", "Z3 C3 T1 C4", "O1 L0 C5 T2",
    "O2 L1 C6 T3", "G0 O3 L2 L3",
)
F32 = jnp.float32
BF16 = jnp.bfloat16


class Place:
    def __init__(self):
        self.dp, self.row, self.col = (lax.axis_index(a) for a in ("dp", "row", "col"))
        self.x, self.zh = self.dp // 2, self.dp % 2
        self.y, self.core = self.row // 2, self.row % 2

    def at_x(self, by):
        return (((self.x + by + RING) % RING) * 2 + self.zh, self.row, self.col)

    def at_y(self, by):
        return (self.dp, ((self.y + by + RING) % RING) * 2 + self.core, self.col)

    def in_row(self, by, core):
        return (self.dp, ((self.y + by) % RING) * 2 + core, self.col)

    def sibling(self):
        return self.in_row(0, 1 - self.core)

    def at_z(self, by):
        z = (self.zh * 8 + self.col + by + 16) % 16
        return (self.x * 2 + z // 8, self.row, z % 8)

    def at_col(self, by):
        return (self.dp, self.row, (self.col + by + 8) % 8)


def greet(partners):
    barrier = pltpu.get_barrier_semaphore()
    for partner in partners:
        pl.semaphore_signal(barrier, inc=1, device_id=partner, device_id_type=MESH)
    pl.semaphore_wait(barrier, len(partners))


class Sends:
    def __init__(self, sems):
        self.sems, self.copies = sems, []

    def start(self, src, dst, recv, device):
        copy = pltpu.make_async_remote_copy(
            src_ref=src, dst_ref=dst, send_sem=self.sems.at[len(self.copies)], recv_sem=recv,
            device_id=device, device_id_type=MESH,
        )
        copy.start()
        self.copies.append(copy)

    def finish(self):
        for copy in self.copies:
            copy.wait_send()


def arrived(ref, sem, place):
    pltpu.make_async_copy(ref, ref, sem).wait()


def whole_kernel(
    tile, w_hbm, ft_hbm, it_hbm, go_hbm, gx, dw,
    w, ft, it, XG, XT, acc, psend, pair, Dy, yrel, yrec, win, ups,
    G, D, xrel, xrec, S, zrel, zrec, rr, rl, part,
    fetch_sem, sends, ag_send, ag_recv, p_send, p_recv, y_send, yrel_sem, yrec_sem, h_send, h_recv, go_recv,
    col_send, g_recv, xrel_sem, xrec_sem, zrel_sem, zrec_sem, out_sem, rr_sem, rl_sem,
):
    me = Place()
    rows = tile.shape[0]
    half = rows // 2
    step = 3 * LANES
    right, left = me.at_y(1), me.at_y(-1)
    sibling = me.sibling()
    xr, xl = me.at_x(1), me.at_x(-1)
    up, down = me.at_z(4), me.at_z(-4)
    col_up, col_down = me.at_col(1), me.at_col(-1)
    others = [me.in_row(by, 1 - me.core) for by in (1, 2, 3)]
    own_rows = pl.ds(pl.multiple_of(me.col * rows, rows), rows)
    fetches = [
        pltpu.make_async_copy(tile, XG.at[own_rows], fetch_sem.at[0]),
        pltpu.make_async_copy(ft_hbm, ft, fetch_sem.at[1]),
        pltpu.make_async_copy(it_hbm, it, fetch_sem.at[2]),
    ]
    for n in range(CHUNKS):
        for c in range(3):
            lanes, to = pl.ds(n * LANES, LANES), pl.ds(c * LANES, LANES)
            fetches.append(
                pltpu.make_async_copy(
                    w_hbm.at[c, :, lanes], w.at[n, :, to], fetch_sem.at[3 + 3 * n + c]
                )
            )
    for copy in fetches:
        copy.start()
    greet([right, left, me.at_y(2), sibling, *others, xr, xl, up, down, col_up, col_down])
    out = Sends(sends)
    top, bottom = pl.ds(0, half), pl.ds(half, half)
    halves = (top, bottom)

    span = 4 * rows
    token_half = me.y // 2

    def go_part(by, head):
        n = (me.y + by) % RING
        lanes = pl.ds(pl.multiple_of(n * LANES, LANES), LANES)
        slot = me.row % 4
        if head:
            src, dst = go_hbm.at[pl.ds(0, HALO), lanes], ups.at[pl.ds(HALO + span, HALO)]
            recv, device = go_recv.at[4], me.in_row(by, 0)
        else:
            src = go_hbm.at[:, lanes]
            dst = ups.at[pl.ds(pl.multiple_of(HALO + slot * rows, HALO), rows)]
            recv, device = go_recv.at[slot], me.in_row(by, token_half)
        remote = pltpu.make_async_remote_copy(
            src_ref=src, dst_ref=dst, send_sem=h_send.at[2 + by + 4 * head], recv_sem=recv,
            device_id=device, device_id_type=MESH,
        )
        return remote, pltpu.make_async_copy(src, dst, recv)

    stays = token_half == me.core
    has_head = me.row == 4
    for by in range(RING):
        remote, local = go_part(by, 0)
        if by:
            remote.start()
        else:

            @pl.when(stays)
            def _():
                local.start()

            @pl.when(jnp.logical_not(stays))
            def _():
                remote.start()

        remote_head, local_head = go_part(by, 1)

        @pl.when(has_head)
        def _():
            (remote_head if by else local_head).start()

    ups[0:HALO, :] = jnp.zeros((HALO, LANES), BF16)

    @pl.when(me.core == 0)
    def _():
        win[0:HALO, :] = jnp.zeros((HALO, step), BF16)

    @pl.when(me.core == 1)
    def _():
        win[span + HALO :, :] = jnp.zeros((HALO, step), BF16)
        ups[span + HALO :, :] = jnp.zeros((HALO, LANES), BF16)

    tail_copy, head_copy = (
        pltpu.make_async_remote_copy(
            src_ref=win.at[pl.ds(src, HALO)], dst_ref=win.at[pl.ds(dst, HALO)],
            send_sem=h_send.at[k], recv_sem=h_recv.at[k], device_id=sibling, device_id_type=MESH,
        )
        for k, (src, dst) in enumerate(((span, 0), (HALO, span + HALO)))
    )

    def block_at(j):
        return pl.ds(pl.multiple_of(j * rows, rows), rows)

    def sub_at(j, u):
        sub = rows // SUBS
        return pl.ds(pl.multiple_of(j * rows + u * sub, sub), sub)

    def line_copy(j, u, device):
        return pltpu.make_async_remote_copy(
            src_ref=XG.at[sub_at(j, u)], dst_ref=XG.at[sub_at(j, u)], send_sem=ag_send.at[j, u],
            recv_sem=ag_recv.at[j, u], device_id=device, device_id_type=MESH,
        )

    def own_copy(n, u):
        sub = rows // SUBS
        return pltpu.make_async_remote_copy(
            src_ref=tile.at[pl.ds(u * sub, sub)], dst_ref=XG.at[sub_at(me.col, u)],
            send_sem=ag_send.at[8, u] if n else ag_send.at[me.col, u],
            recv_sem=ag_recv.at[me.col, u], device_id=col_down if n else col_up,
            device_id_type=MESH,
        )

    @pl.when(me.col < 7)
    def _():
        for u in range(SUBS):
            own_copy(0, u).start()

    @pl.when(me.col > 0)
    def _():
        for u in range(SUBS):
            own_copy(1, u).start()

    for copy in fetches:
        copy.wait()

    def pair_copy(s, n):
        return pltpu.make_async_remote_copy(
            src_ref=psend.at[s, n], dst_ref=pair.at[s, n], send_sem=p_send.at[s, n],
            recv_sem=p_recv.at[s, n], device_id=sibling, device_id_type=MESH,
        )

    y_opp, y_r, y_l = ((me.y + by) % RING for by in (2, 1, 3))

    def project(j):
        x = XG[block_at(j), :]
        s = j % 4
        mine = j // 4 == me.core
        for n in (y_opp, y_r, y_l, me.y):
            product = jnp.dot(x, w[n], preferred_element_type=F32)

            @pl.when(mine)
            def _():
                acc[s, n] = product

            @pl.when(jnp.logical_not(mine))
            def _():
                psend[s, n] = product.astype(BF16)
                pair_copy(s, n).start()

        XT[:, block_at(j)] = x.T

    def y_copy(k, s):
        src, dst, sem, device = (
            (Dy.at[s, y_opp, top], yrel.at[0, s], yrel_sem.at[0, s], right),
            (Dy.at[s, y_opp, bottom], yrel.at[1, s], yrel_sem.at[1, s], left),
            (Dy.at[s, y_r, bottom], yrec.at[0, s, bottom], yrec_sem.at[0, 1, s], right),
            (Dy.at[s, y_l, top], yrec.at[1, s, top], yrec_sem.at[1, 0, s], left),
            (Dy.at[s, y_r, top], yrec.at[0, s, top], yrec_sem.at[0, 0, s], right),
            (Dy.at[s, y_l, bottom], yrec.at[1, s, bottom], yrec_sem.at[1, 1, s], left),
        )[k]
        return pltpu.make_async_remote_copy(
            src_ref=src, dst_ref=dst, send_sem=y_send.at[k, s], recv_sem=sem, device_id=device,
            device_id_type=MESH,
        )

    def pair_sum(s):
        for n, copies in ((y_opp, (0, 1)), (y_r, (2,)), (y_l, (3,)), (me.y, ())):
            arrived(pair.at[s, n], p_recv.at[s, n], me)
            total = acc[s, n] + pair[s, n].astype(F32)
            if copies:
                Dy[s, n] = total.astype(BF16)
                for k in copies:
                    y_copy(k, s).start()
            else:
                acc[s, n] = total

    def relay_y(s):
        for side, n, at, k in ((0, y_r, top, 4), (1, y_l, bottom, 5)):
            arrived(yrel.at[side, s], yrel_sem.at[side, s], me)
            Dy[s, n, at] = (Dy[s, n, at].astype(F32) + yrel[side, s].astype(F32)).astype(BF16)
            y_copy(k, s).start()

    def for_kept(stage, d):
        for side in (-1, 1):
            j = me.col + side * d
            there = jnp.logical_and(jnp.logical_and(j >= 0, j <= 7), d >= (side + 1) // 2)
            there = jnp.logical_and(there, (j + 8) // 4 - 2 == me.core)

            @pl.when(there)
            def _():
                stage(j % 4)

    def pass_on(d, some):
        @pl.when(jnp.logical_and(d <= 7, me.col - d >= 0))
        def _():
            j = me.col - d
            for u in some:
                arrived(XG.at[sub_at(j, u)], ag_recv.at[j, u], me)

                @pl.when(me.col < 7)
                def _():
                    line_copy(j, u, col_up).start()

        @pl.when(jnp.logical_and(d <= 7, me.col + d <= 7))
        def _():
            j = me.col + d
            for u in some:
                arrived(XG.at[sub_at(j, u)], ag_recv.at[j, u], me)

                @pl.when(me.col > 0)
                def _():
                    line_copy(j, u, col_down).start()

    def line_step(d, carry):
        last = d - 1
        pass_on(d, range(SUBS // 2))

        @pl.when(jnp.logical_and(last <= 7, me.col - last >= 0))
        def _():
            project(me.col - last)

        pass_on(d, range(SUBS // 2, SUBS))

        @pl.when(jnp.logical_and(jnp.logical_and(last >= 1, last <= 7), me.col + last <= 7))
        def _():
            project(me.col + last)

        for_kept(relay_y, d - 3)
        for_kept(pair_sum, d - 2)
        return carry

    lax.fori_loop(1, 11, line_step, 0)

    def projection(s):
        for side in range(2):
            for h in range(2):
                arrived(yrec.at[side, s, halves[h]], yrec_sem.at[side, h, s], me)
        total = acc[s, me.y] + yrec[0, s].astype(F32) + yrec[1, s].astype(F32)
        win[HALO + s * rows : HALO + (s + 1) * rows, :] = total.astype(BF16)
        if s == 3:

            @pl.when(me.core == 0)
            def _():
                tail_copy.start()

        if s == 0:

            @pl.when(me.core == 1)
            def _():
                head_copy.start()

    length = rows + 2 * HALO

    def causal(seq, taps):
        total = taps[0] * seq
        for lag in range(1, len(taps)):
            total = total + taps[lag] * pltpu.roll(seq, lag, 0)
        return total

    def anticausal(seq, taps):
        total = taps[0] * seq
        for lag in range(1, len(taps)):
            total = total + taps[lag] * pltpu.roll(seq, length - lag, 0)
        return total

    def take_grad_out():
        for s in range(4):
            arrived(ups.at[pl.ds(HALO + s * rows, rows)], go_recv.at[s], me)

        @pl.when(me.core == 0)
        def _():
            arrived(ups.at[pl.ds(HALO + span, HALO)], go_recv.at[4], me)

    def channels(s):
        if s == 1:
            take_grad_out()
        if s == 0:

            @pl.when(me.core == 1)
            def _():
                arrived(win.at[pl.ds(0, HALO)], h_recv.at[0], me)

        if s == 3:

            @pl.when(me.core == 0)
            def _():
                arrived(win.at[pl.ds(span + HALO, HALO)], h_recv.at[1], me)

        lanes = pl.ds(pl.multiple_of(me.y * LANES, LANES), LANES)
        parts = [slice(c * LANES, (c + 1) * LANES) for c in range(3)]
        taps = [[ft[k, c : c + 1, lanes] for k in range(3)] for c in range(3)]
        inner_taps = [it[k : k + 1, lanes] for k in range(7)]
        tokens = slice(s * rows, s * rows + length)
        query, key, value = (
            causal(win[tokens, parts[c]].astype(F32), taps[c]) for c in range(3)
        )
        upstream = ups[tokens, :].astype(F32)
        product = (key * value).astype(BF16).astype(F32)
        inner = causal(product, inner_taps)
        grad_product = anticausal(upstream * query, inner_taps)
        mixed = (upstream * inner, grad_product * value, grad_product * key)
        at = pl.ds(pl.multiple_of(me.core * span + s * rows, rows), rows)
        for c in range(3):
            grad = anticausal(mixed[c], taps[c])
            G[me.y, at, parts[c]] = grad[HALO : rows + HALO].astype(BF16)
        for h in range(2):
            g_send(me.y, h, s, sibling)
        g_send(me.y, 0, s, right)
        g_send(me.y, 1, s, left)
        g_send(me.y, 1, s, right)
        g_send(me.y, 0, s, left)

    def g_at(n, core, h, s):
        first = core * span + s * rows + h * half
        return G.at[n, pl.ds(pl.multiple_of(first, half), half)]

    def g_send(n, h, s, device):
        at = g_at(n, me.core, h, s)
        out.start(at, at, g_recv.at[n * 2 + me.core, h, s], device)

    def g_wait(n, core, h, s):
        arrived(g_at(n, core, h, s), g_recv.at[n * 2 + core, h, s], me)

    @pl.when(me.col == 7)
    def _():
        rr[...] = jnp.zeros_like(rr)

    @pl.when(me.col == 0)
    def _():
        rl[...] = jnp.zeros_like(rl)

    def relay_g(s):
        g_wait(y_l, me.core, 0, s)
        g_send(y_l, 0, s, right)
        g_send(y_l, 0, s, sibling)
        g_wait(y_r, me.core, 1, s)
        g_send(y_r, 1, s, left)
        g_send(y_r, 1, s, sibling)
        g_wait(y_l, me.core, 1, s)
        g_send(y_l, 1, s, sibling)
        g_wait(y_r, me.core, 0, s)
        g_send(y_r, 0, s, sibling)

    def share_g(s):
        for h in range(2):
            g_wait(y_opp, me.core, h, s)
            g_send(y_opp, h, s, sibling)

    chunk = (me.y, y_r, y_l, y_opp)

    def whole_g(k):
        for s in range(4):
            for h in range(2):
                g_wait(chunk[k], 1 - me.core, h, s)

    def grad_in_of(block):
        at = pl.ds(pl.multiple_of(block * rows, rows), rows)
        total = lax.dot_general(G[0, at], w[0], NT, preferred_element_type=F32)
        for n in range(1, CHUNKS):
            total = total + lax.dot_general(G[n, at], w[n], NT, preferred_element_type=F32)
        return total

    def col_copy(block, side, h):
        landing, sems, device = ((rr, rr_sem, col_down), (rl, rl_sem, col_up))[side]
        return pltpu.make_async_remote_copy(
            src_ref=part.at[block, halves[h]], dst_ref=landing.at[block, halves[h]],
            send_sem=col_send.at[block, h], recv_sem=sems.at[block, h], device_id=device,
            device_id_type=MESH,
        )

    def col_pass(block, side, inner):
        landing, sems = ((rr, rr_sem), (rl, rl_sem))[side]
        total = grad_in_of(block)
        for h in range(2):

            @pl.when(inner)
            def _():
                arrived(landing.at[block, halves[h]], sems.at[block, h], me)

            own = total[h * half : (h + 1) * half]
            part[block, halves[h]] = (own + landing[block, halves[h]].astype(F32)).astype(BF16)
            col_copy(block, side, h).start()

    def col_round(s):
        @pl.when(s + me.col >= 7)
        def _():
            col_pass(s + me.col - 7, 0, me.col < 7)

        @pl.when(s >= me.col)
        def _():
            col_pass(7 - s + me.col, 1, me.col > 0)

    def col_last(unused):
        total = grad_in_of(me.col)
        for h in range(2):

            @pl.when(me.col < 7)
            def _():
                arrived(rr.at[me.col, halves[h]], rr_sem.at[me.col, h], me)

            @pl.when(me.col > 0)
            def _():
                arrived(rl.at[me.col, halves[h]], rl_sem.at[me.col, h], me)

        gx[...] = (total + rr[me.col].astype(F32) + rl[me.col].astype(F32)).astype(BF16)

        for block in range(8):
            for h in range(2):

                @pl.when(block < me.col)
                def _():
                    col_copy(block, 0, h).wait_send()

                @pl.when(block > me.col)
                def _():
                    col_copy(block, 1, h).wait_send()

    to_r, to_l, to_o = ((me.x + by + RING) % RING for by in (1, 3, 2))

    def lanes_of(m):
        return pl.ds(pl.multiple_of(chunk[m] * LANES, LANES), LANES)

    def dw_at(q, h, m):
        return dw.at[
            :, pl.ds(pl.multiple_of(q * rows + h * half, half), half), lanes_of(m)
        ]

    def multiply(m):
        for q in range(RING):
            D[q, m] = jnp.dot(
                XT[q * rows : (q + 1) * rows, :], G[chunk[m]], preferred_element_type=F32
            ).astype(BF16)
        out.start(D.at[to_o, m, top], xrel.at[0, m], xrel_sem.at[0, m], xr)
        out.start(D.at[to_o, m, bottom], xrel.at[1, m], xrel_sem.at[1, m], xl)
        out.start(D.at[to_r, m, bottom], xrec.at[0, m, bottom], xrec_sem.at[0, 1, m], xr)
        out.start(D.at[to_l, m, top], xrec.at[1, m, top], xrec_sem.at[1, 0, m], xl)

    def relay_x(m):
        arrived(xrel.at[0, m], xrel_sem.at[0, m], me)
        D[to_r, m, top] = (D[to_r, m, top].astype(F32) + xrel[0, m].astype(F32)).astype(BF16)
        out.start(D.at[to_r, m, top], xrec.at[0, m, top], xrec_sem.at[0, 0, m], xr)
        arrived(xrel.at[1, m], xrel_sem.at[1, m], me)
        D[to_l, m, bottom] = (D[to_l, m, bottom].astype(F32) + xrel[1, m].astype(F32)).astype(BF16)
        out.start(D.at[to_l, m, bottom], xrec.at[1, m, bottom], xrec_sem.at[1, 1, m], xl)

    def exchange(m):
        for side in range(2):
            for h in range(2):
                arrived(xrec.at[side, m, halves[h]], xrec_sem.at[side, h, m], me)
        S[m] = (D[me.x, m].astype(F32) + xrec[0, m].astype(F32) + xrec[1, m].astype(F32)).astype(BF16)
        out.start(S.at[m, top], zrel.at[0, m], zrel_sem.at[0, m], up)
        out.start(S.at[m, bottom], zrel.at[1, m], zrel_sem.at[1, m], down)

    def relay_z(m):
        arrived(zrel.at[0, m], zrel_sem.at[0, m], me)
        out.start(zrel.at[0, m], zrec.at[m, top], zrec_sem.at[0, m], up)
        arrived(zrel.at[1, m], zrel_sem.at[1, m], me)
        out.start(zrel.at[1, m], zrec.at[m, bottom], zrec_sem.at[1, m], down)

    def gather(q, h, m, device):
        out.start(dw_at(q, h, m), dw_at(q, h, m), out_sem.at[q, h, m], device)

    def gathered(q, h, m):
        arrived(dw_at(q, h, m), out_sem.at[q, h, m], me)

    def total_of(m):
        for h in range(2):
            arrived(zrec.at[m, halves[h]], zrec_sem.at[h, m], me)
        total = (S[m].astype(F32) + zrec[m].astype(F32)).astype(BF16)
        own_rows_x = pl.ds(pl.multiple_of(me.x * rows, rows), rows)
        for c in range(3):
            dw[c, own_rows_x, lanes_of(m)] = total[:, c * LANES : (c + 1) * LANES]
        gather(me.x, 0, m, xr)
        gather(me.x, 1, m, xl)
        gather(me.x, 1, m, xr)
        gather(me.x, 0, m, xl)

    def relay_out(m):
        gathered(to_l, 0, m)
        gather(to_l, 0, m, xr)
        gathered(to_r, 1, m)
        gather(to_r, 1, m, xl)

    def last_out(m):
        gathered(to_l, 1, m)
        gathered(to_r, 0, m)
        gathered(to_o, 0, m)
        gathered(to_o, 1, m)

    stages = {
        "F": projection, "H": channels, "A": relay_g, "B": share_g, "K": whole_g, "W": whole_g,
        "M": multiply, "X": relay_x, "E": exchange, "Z": relay_z, "T": total_of, "O": relay_out,
        "L": last_out, "C": col_round, "G": col_last,
    }
    for group in ORDER:
        for name in group.split():
            stages[name[0]](int(name[1]))
    out.finish()

    @pl.when(me.col < 7)
    def _():
        for u in range(SUBS):
            own_copy(0, u).wait_send()

    @pl.when(me.col > 0)
    def _():
        for u in range(SUBS):
            own_copy(1, u).wait_send()

    for j in range(8):

        @pl.when(jnp.logical_and(j < me.col, me.col < 7))
        def _():
            for u in range(SUBS):
                line_copy(j, u, col_up).wait_send()

        @pl.when(jnp.logical_and(j > me.col, me.col > 0))
        def _():
            for u in range(SUBS):
                line_copy(j, u, col_down).wait_send()

    for n in range(CHUNKS):
        for p in range(RING):
            pair_copy(p, n).wait_send()
        for k in range(6):
            y_copy(k, n).wait_send()

    @pl.when(me.core == 0)
    def _():
        tail_copy.wait_send()

    @pl.when(me.core == 1)
    def _():
        head_copy.wait_send()

    for by in range(RING):
        if by:
            go_part(by, 0)[0].wait_send()

            @pl.when(has_head)
            def _():
                go_part(by, 1)[0].wait_send()

        else:

            @pl.when(jnp.logical_not(stays))
            def _():
                go_part(0, 0)[0].wait_send()


SENDS = CHUNKS * (6 + 8 + 4 + 2 + 2 + 2 + 4 + 2)


def whole(tile, w, ft, it, go):
    rows, deep = tile.shape[0], w.shape[1]
    half, step = rows // 2, 3 * LANES
    vmem, sem = pltpu.VMEM, pltpu.SemaphoreType.DMA
    return pl.pallas_call(
        whole_kernel,
        out_shape=(jax.ShapeDtypeStruct((rows, deep), BF16), jax.ShapeDtypeStruct(w.shape, BF16)),
        in_specs=[
            pl.BlockSpec(memory_space=pltpu.HBM) for _ in range(5)
        ],
        out_specs=(pl.BlockSpec(memory_space=pltpu.VMEM),) * 2,
        scratch_shapes=[
            vmem((CHUNKS, deep, step), BF16),
            vmem(ft.shape, F32),
            vmem(it.shape, F32),
            vmem((8 * rows, deep), BF16),
            vmem((deep, 8 * rows), BF16),
            vmem((RING, CHUNKS, rows, step), F32),
            vmem((RING, CHUNKS, rows, step), BF16),
            vmem((RING, CHUNKS, rows, step), BF16),
            vmem((RING, CHUNKS, rows, step), BF16),
            vmem((2, CHUNKS, half, step), BF16),
            vmem((2, CHUNKS, rows, step), BF16),
            vmem((4 * rows + 2 * HALO, step), BF16),
            vmem((4 * rows + 2 * HALO, LANES), BF16),
            vmem((CHUNKS, 8 * rows, step), BF16),
            vmem((RING, CHUNKS, rows, step), BF16),
            vmem((2, CHUNKS, half, step), BF16),
            vmem((2, CHUNKS, rows, step), BF16),
            vmem((CHUNKS, rows, step), BF16),
            vmem((2, CHUNKS, half, step), BF16),
            vmem((CHUNKS, rows, step), BF16),
            vmem((8, rows, deep), BF16),
            vmem((8, rows, deep), BF16),
            vmem((8, rows, deep), BF16),
            sem((3 + 3 * CHUNKS,)),
            sem((SENDS,)),
            sem((9, SUBS)),
            sem((8, SUBS)),
            sem((RING, CHUNKS)),
            sem((RING, CHUNKS)),
            sem((6, CHUNKS)),
            sem((2, CHUNKS)),
            sem((2, 2, CHUNKS)),
            sem((10,)),
            sem((2,)),
            sem((5,)),
            sem((8, 2)),
            sem((8, 2, CHUNKS)),
            sem((2, CHUNKS)),
            sem((2, 2, CHUNKS)),
            sem((2, CHUNKS)),
            sem((2, CHUNKS)),
            sem((RING, 2, CHUNKS)),
            sem((8, 2)),
            sem((8, 2)),
        ],
        compiler_params=pltpu.CompilerParams(
            collective_id=1, has_side_effects=True, vmem_limit_bytes=63 * 2**20
        ),
        name="whole",
    )(tile, w, ft, it, go)


def on_device(inputs, weights, feature_taps, inner_taps, grad_out):
    grad_x, grad_w = whole(
        inputs[0], weights.transpose(1, 0, 2), feature_taps, inner_taps, grad_out[0]
    )
    return grad_x[None], grad_w.astype(F32).transpose(1, 0, 2)


def solution(mesh):
    placed = (
        P("dp", "col", "row"),
        P("row", None, "col"),
        P(None, None, "col"),
        P(None, "col"),
        P("dp", "row", "col"),
    )
    return jax.shard_map(
        on_device,
        mesh=mesh,
        in_specs=placed,
        out_specs=(P("dp", "col", "row"), P("row", None, "col")),
        check_vma=False,
    )
```

```python
import jax
import jax.numpy as jnp
from jax import lax
from jax.experimental import pallas as pl
from jax.experimental.pallas import tpu as pltpu
from jax.sharding import PartitionSpec as P

MESH = pl.DeviceIdType.MESH
NT = (((1,), (1,)), ((), ()))
CHUNKS = 4
HALO = 16
LANES = 128
SUBS = 4
RING = 4
ORDER = (
    "F3 F0 F1 F2", "H1 H2 H0 H3", "K0 M0 A0 X0", "A1 A2 A3 E0",
    "B0 B1 W1 M1", "X1 B2 B3 E1", "W2 M2 Z0 X2", "W3 M3 E2 X3",
    "Z1 E3 C0 Z2", "T0 C1 O0 Z3", "C2 L0 T1 C3", "O1 T2 C4 L1",
    "O2 C5 T3 C6", "O3 L2 G0 L3",
)
F32 = jnp.float32
BF16 = jnp.bfloat16


class Place:
    def __init__(self):
        self.dp, self.row, self.col = (lax.axis_index(a) for a in ("dp", "row", "col"))
        self.x, self.zh = self.dp // 2, self.dp % 2
        self.y, self.core = self.row // 2, self.row % 2

    def at_x(self, by):
        return (((self.x + by + RING) % RING) * 2 + self.zh, self.row, self.col)

    def at_y(self, by):
        return (self.dp, ((self.y + by + RING) % RING) * 2 + self.core, self.col)

    def in_row(self, by, core):
        return (self.dp, ((self.y + by) % RING) * 2 + core, self.col)

    def sibling(self):
        return self.in_row(0, 1 - self.core)

    def at_z(self, by):
        z = (self.zh * 8 + self.col + by + 16) % 16
        return (self.x * 2 + z // 8, self.row, z % 8)

    def at_col(self, by):
        return (self.dp, self.row, (self.col + by + 8) % 8)


def greet(partners):
    barrier = pltpu.get_barrier_semaphore()
    for partner in partners:
        pl.semaphore_signal(barrier, inc=1, device_id=partner, device_id_type=MESH)
    pl.semaphore_wait(barrier, len(partners))


class Sends:
    def __init__(self, sems):
        self.sems, self.copies = sems, []

    def start(self, src, dst, recv, device):
        copy = pltpu.make_async_remote_copy(
            src_ref=src, dst_ref=dst, send_sem=self.sems.at[len(self.copies)], recv_sem=recv,
            device_id=device, device_id_type=MESH,
        )
        copy.start()
        self.copies.append(copy)

    def finish(self):
        for copy in self.copies:
            copy.wait_send()


def arrived(ref, sem, place):
    pltpu.make_async_copy(ref, ref, sem).wait()


def whole_kernel(
    tile, w_hbm, ft_hbm, it_hbm, go_hbm, gx, dw,
    w, ft, it, XG, XT, acc, psend, pair, Dy, yrel, yrec, win, ups,
    G, D, xrel, xrec, S, zrel, zrec, rr, rl, part,
    fetch_sem, sends, ag_send, ag_recv, p_send, p_recv, y_send, yrel_sem, yrec_sem, h_send, h_recv, go_recv,
    col_send, g_recv, xrel_sem, xrec_sem, zrel_sem, zrec_sem, out_sem, rr_sem, rl_sem,
):
    me = Place()
    rows = tile.shape[0]
    half = rows // 2
    step = 3 * LANES
    right, left = me.at_y(1), me.at_y(-1)
    sibling = me.sibling()
    xr, xl = me.at_x(1), me.at_x(-1)
    up, down = me.at_z(4), me.at_z(-4)
    col_up, col_down = me.at_col(1), me.at_col(-1)
    others = [me.in_row(by, 1 - me.core) for by in (1, 2, 3)]
    own_rows = pl.ds(pl.multiple_of(me.col * rows, rows), rows)
    fetches = [
        pltpu.make_async_copy(tile, XG.at[own_rows], fetch_sem.at[0]),
        pltpu.make_async_copy(ft_hbm, ft, fetch_sem.at[1]),
        pltpu.make_async_copy(it_hbm, it, fetch_sem.at[2]),
    ]
    for n in range(CHUNKS):
        for c in range(3):
            lanes, to = pl.ds(n * LANES, LANES), pl.ds(c * LANES, LANES)
            fetches.append(
                pltpu.make_async_copy(
                    w_hbm.at[c, :, lanes], w.at[n, :, to], fetch_sem.at[3 + 3 * n + c]
                )
            )
    for copy in fetches:
        copy.start()
    greet([right, left, me.at_y(2), sibling, *others, xr, xl, up, down, col_up, col_down])
    out = Sends(sends)
    top, bottom = pl.ds(0, half), pl.ds(half, half)
    halves = (top, bottom)

    span = 4 * rows
    token_half = me.y // 2

    def go_part(by, head):
        n = (me.y + by) % RING
        lanes = pl.ds(pl.multiple_of(n * LANES, LANES), LANES)
        slot = me.row % 4
        if head:
            src, dst = go_hbm.at[pl.ds(0, HALO), lanes], ups.at[pl.ds(HALO + span, HALO)]
            recv, device = go_recv.at[4], me.in_row(by, 0)
        else:
            src = go_hbm.at[:, lanes]
            dst = ups.at[pl.ds(pl.multiple_of(HALO + slot * rows, HALO), rows)]
            recv, device = go_recv.at[slot], me.in_row(by, token_half)
        remote = pltpu.make_async_remote_copy(
            src_ref=src, dst_ref=dst, send_sem=h_send.at[2 + by + 4 * head], recv_sem=recv,
            device_id=device, device_id_type=MESH,
        )
        return remote, pltpu.make_async_copy(src, dst, recv)

    stays = token_half == me.core
    has_head = me.row == 4
    for by in range(RING):
        remote, local = go_part(by, 0)
        if by:
            remote.start()
        else:

            @pl.when(stays)
            def _():
                local.start()

            @pl.when(jnp.logical_not(stays))
            def _():
                remote.start()

        remote_head, local_head = go_part(by, 1)

        @pl.when(has_head)
        def _():
            (remote_head if by else local_head).start()

    ups[0:HALO, :] = jnp.zeros((HALO, LANES), BF16)

    @pl.when(me.core == 0)
    def _():
        win[0:HALO, :] = jnp.zeros((HALO, step), BF16)

    @pl.when(me.core == 1)
    def _():
        win[span + HALO :, :] = jnp.zeros((HALO, step), BF16)
        ups[span + HALO :, :] = jnp.zeros((HALO, LANES), BF16)

    tail_copy, head_copy = (
        pltpu.make_async_remote_copy(
            src_ref=win.at[pl.ds(src, HALO)], dst_ref=win.at[pl.ds(dst, HALO)],
            send_sem=h_send.at[k], recv_sem=h_recv.at[k], device_id=sibling, device_id_type=MESH,
        )
        for k, (src, dst) in enumerate(((span, 0), (HALO, span + HALO)))
    )

    def block_at(j):
        return pl.ds(pl.multiple_of(j * rows, rows), rows)

    def sub_at(j, u):
        sub = rows // SUBS
        return pl.ds(pl.multiple_of(j * rows + u * sub, sub), sub)

    def line_copy(j, u, device):
        return pltpu.make_async_remote_copy(
            src_ref=XG.at[sub_at(j, u)], dst_ref=XG.at[sub_at(j, u)], send_sem=ag_send.at[j, u],
            recv_sem=ag_recv.at[j, u], device_id=device, device_id_type=MESH,
        )

    def own_copy(n, u):
        sub = rows // SUBS
        return pltpu.make_async_remote_copy(
            src_ref=tile.at[pl.ds(u * sub, sub)], dst_ref=XG.at[sub_at(me.col, u)],
            send_sem=ag_send.at[8, u] if n else ag_send.at[me.col, u],
            recv_sem=ag_recv.at[me.col, u], device_id=col_down if n else col_up,
            device_id_type=MESH,
        )

    @pl.when(me.col < 7)
    def _():
        for u in range(SUBS):
            own_copy(0, u).start()

    @pl.when(me.col > 0)
    def _():
        for u in range(SUBS):
            own_copy(1, u).start()

    for copy in fetches:
        copy.wait()

    def pair_copy(s, n):
        return pltpu.make_async_remote_copy(
            src_ref=psend.at[s, n], dst_ref=pair.at[s, n], send_sem=p_send.at[s, n],
            recv_sem=p_recv.at[s, n], device_id=sibling, device_id_type=MESH,
        )

    y_opp, y_r, y_l = ((me.y + by) % RING for by in (2, 1, 3))

    def project(j):
        x = XG[block_at(j), :]
        s = j % 4
        mine = j // 4 == me.core
        for n in (y_opp, y_r, y_l, me.y):
            product = jnp.dot(x, w[n], preferred_element_type=F32)

            @pl.when(mine)
            def _():
                acc[s, n] = product

            @pl.when(jnp.logical_not(mine))
            def _():
                psend[s, n] = product.astype(BF16)
                pair_copy(s, n).start()

        XT[:, block_at(j)] = x.T

    def y_copy(k, s):
        src, dst, sem, device = (
            (Dy.at[s, y_opp, top], yrel.at[0, s], yrel_sem.at[0, s], right),
            (Dy.at[s, y_opp, bottom], yrel.at[1, s], yrel_sem.at[1, s], left),
            (Dy.at[s, y_r, bottom], yrec.at[0, s, bottom], yrec_sem.at[0, 1, s], right),
            (Dy.at[s, y_l, top], yrec.at[1, s, top], yrec_sem.at[1, 0, s], left),
            (Dy.at[s, y_r, top], yrec.at[0, s, top], yrec_sem.at[0, 0, s], right),
            (Dy.at[s, y_l, bottom], yrec.at[1, s, bottom], yrec_sem.at[1, 1, s], left),
        )[k]
        return pltpu.make_async_remote_copy(
            src_ref=src, dst_ref=dst, send_sem=y_send.at[k, s], recv_sem=sem, device_id=device,
            device_id_type=MESH,
        )

    def pair_sum(s):
        for n, copies in ((y_opp, (0, 1)), (y_r, (2,)), (y_l, (3,)), (me.y, ())):
            arrived(pair.at[s, n], p_recv.at[s, n], me)
            total = acc[s, n] + pair[s, n].astype(F32)
            if copies:
                Dy[s, n] = total.astype(BF16)
                for k in copies:
                    y_copy(k, s).start()
            else:
                acc[s, n] = total

    def relay_y(s):
        for side, n, at, k in ((0, y_r, top, 4), (1, y_l, bottom, 5)):
            arrived(yrel.at[side, s], yrel_sem.at[side, s], me)
            Dy[s, n, at] = (Dy[s, n, at].astype(F32) + yrel[side, s].astype(F32)).astype(BF16)
            y_copy(k, s).start()

    def for_kept(stage, d):
        for side in (-1, 1):
            j = me.col + side * d
            there = jnp.logical_and(jnp.logical_and(j >= 0, j <= 7), d >= (side + 1) // 2)
            there = jnp.logical_and(there, (j + 8) // 4 - 2 == me.core)

            @pl.when(there)
            def _():
                stage(j % 4)

    def pass_on(d, some):
        @pl.when(jnp.logical_and(d <= 7, me.col - d >= 0))
        def _():
            j = me.col - d
            for u in some:
                arrived(XG.at[sub_at(j, u)], ag_recv.at[j, u], me)

                @pl.when(me.col < 7)
                def _():
                    line_copy(j, u, col_up).start()

        @pl.when(jnp.logical_and(d <= 7, me.col + d <= 7))
        def _():
            j = me.col + d
            for u in some:
                arrived(XG.at[sub_at(j, u)], ag_recv.at[j, u], me)

                @pl.when(me.col > 0)
                def _():
                    line_copy(j, u, col_down).start()

    def line_step(d, carry):
        last = d - 1
        pass_on(d, range(SUBS // 2))

        @pl.when(jnp.logical_and(last <= 7, me.col - last >= 0))
        def _():
            project(me.col - last)

        pass_on(d, range(SUBS // 2, SUBS))

        @pl.when(jnp.logical_and(jnp.logical_and(last >= 1, last <= 7), me.col + last <= 7))
        def _():
            project(me.col + last)

        for_kept(relay_y, d - 3)
        for_kept(pair_sum, d - 2)
        return carry

    lax.fori_loop(1, 11, line_step, 0)

    def projection(s):
        for side in range(2):
            for h in range(2):
                arrived(yrec.at[side, s, halves[h]], yrec_sem.at[side, h, s], me)
        total = acc[s, me.y] + yrec[0, s].astype(F32) + yrec[1, s].astype(F32)
        win[HALO + s * rows : HALO + (s + 1) * rows, :] = total.astype(BF16)
        if s == 3:

            @pl.when(me.core == 0)
            def _():
                tail_copy.start()

        if s == 0:

            @pl.when(me.core == 1)
            def _():
                head_copy.start()

    length = rows + 2 * HALO

    def causal(seq, taps):
        total = taps[0] * seq
        for lag in range(1, len(taps)):
            total = total + taps[lag] * pltpu.roll(seq, lag, 0)
        return total

    def anticausal(seq, taps):
        total = taps[0] * seq
        for lag in range(1, len(taps)):
            total = total + taps[lag] * pltpu.roll(seq, length - lag, 0)
        return total

    def take_grad_out():
        for s in range(4):
            arrived(ups.at[pl.ds(HALO + s * rows, rows)], go_recv.at[s], me)

        @pl.when(me.core == 0)
        def _():
            arrived(ups.at[pl.ds(HALO + span, HALO)], go_recv.at[4], me)

    def channels(s):
        if s == 1:
            take_grad_out()
        if s == 0:

            @pl.when(me.core == 1)
            def _():
                arrived(win.at[pl.ds(0, HALO)], h_recv.at[0], me)

        if s == 3:

            @pl.when(me.core == 0)
            def _():
                arrived(win.at[pl.ds(span + HALO, HALO)], h_recv.at[1], me)

        lanes = pl.ds(pl.multiple_of(me.y * LANES, LANES), LANES)
        parts = [slice(c * LANES, (c + 1) * LANES) for c in range(3)]
        taps = [[ft[k, c : c + 1, lanes] for k in range(3)] for c in range(3)]
        inner_taps = [it[k : k + 1, lanes] for k in range(7)]
        tokens = slice(s * rows, s * rows + length)
        query, key, value = (
            causal(win[tokens, parts[c]].astype(F32), taps[c]) for c in range(3)
        )
        upstream = ups[tokens, :].astype(F32)
        product = (key * value).astype(BF16).astype(F32)
        inner = causal(product, inner_taps)
        grad_product = anticausal(upstream * query, inner_taps)
        mixed = (upstream * inner, grad_product * value, grad_product * key)
        at = pl.ds(pl.multiple_of(me.core * span + s * rows, rows), rows)
        for c in range(3):
            grad = anticausal(mixed[c], taps[c])
            G[me.y, at, parts[c]] = grad[HALO : rows + HALO].astype(BF16)
        for h in range(2):
            g_send(me.y, h, s, sibling)
        g_send(me.y, 0, s, right)
        g_send(me.y, 1, s, left)
        g_send(me.y, 1, s, right)
        g_send(me.y, 0, s, left)

    def g_at(n, core, h, s):
        first = core * span + s * rows + h * half
        return G.at[n, pl.ds(pl.multiple_of(first, half), half)]

    def g_send(n, h, s, device):
        at = g_at(n, me.core, h, s)
        out.start(at, at, g_recv.at[n * 2 + me.core, h, s], device)

    def g_wait(n, core, h, s):
        arrived(g_at(n, core, h, s), g_recv.at[n * 2 + core, h, s], me)

    @pl.when(me.col == 7)
    def _():
        rr[...] = jnp.zeros_like(rr)

    @pl.when(me.col == 0)
    def _():
        rl[...] = jnp.zeros_like(rl)

    def relay_g(s):
        g_wait(y_l, me.core, 0, s)
        g_send(y_l, 0, s, right)
        g_send(y_l, 0, s, sibling)
        g_wait(y_r, me.core, 1, s)
        g_send(y_r, 1, s, left)
        g_send(y_r, 1, s, sibling)
        g_wait(y_l, me.core, 1, s)
        g_send(y_l, 1, s, sibling)
        g_wait(y_r, me.core, 0, s)
        g_send(y_r, 0, s, sibling)

    def share_g(s):
        for h in range(2):
            g_wait(y_opp, me.core, h, s)
            g_send(y_opp, h, s, sibling)

    chunk = (me.y, y_r, y_l, y_opp)

    def whole_g(k):
        for s in range(4):
            for h in range(2):
                g_wait(chunk[k], 1 - me.core, h, s)

    def grad_in_of(block):
        at = pl.ds(pl.multiple_of(block * rows, rows), rows)
        total = lax.dot_general(G[0, at], w[0], NT, preferred_element_type=F32)
        for n in range(1, CHUNKS):
            total = total + lax.dot_general(G[n, at], w[n], NT, preferred_element_type=F32)
        return total

    def col_copy(block, side, h):
        landing, sems, device = ((rr, rr_sem, col_down), (rl, rl_sem, col_up))[side]
        return pltpu.make_async_remote_copy(
            src_ref=part.at[block, halves[h]], dst_ref=landing.at[block, halves[h]],
            send_sem=col_send.at[block, h], recv_sem=sems.at[block, h], device_id=device,
            device_id_type=MESH,
        )

    def col_pass(block, side, inner):
        landing, sems = ((rr, rr_sem), (rl, rl_sem))[side]
        total = grad_in_of(block)
        for h in range(2):

            @pl.when(inner)
            def _():
                arrived(landing.at[block, halves[h]], sems.at[block, h], me)

            own = total[h * half : (h + 1) * half]
            part[block, halves[h]] = (own + landing[block, halves[h]].astype(F32)).astype(BF16)
            col_copy(block, side, h).start()

    def col_round(s):
        @pl.when(s + me.col >= 7)
        def _():
            col_pass(s + me.col - 7, 0, me.col < 7)

        @pl.when(s >= me.col)
        def _():
            col_pass(7 - s + me.col, 1, me.col > 0)

    def col_last(unused):
        total = grad_in_of(me.col)
        for h in range(2):

            @pl.when(me.col < 7)
            def _():
                arrived(rr.at[me.col, halves[h]], rr_sem.at[me.col, h], me)

            @pl.when(me.col > 0)
            def _():
                arrived(rl.at[me.col, halves[h]], rl_sem.at[me.col, h], me)

        gx[...] = (total + rr[me.col].astype(F32) + rl[me.col].astype(F32)).astype(BF16)

        for block in range(8):
            for h in range(2):

                @pl.when(block < me.col)
                def _():
                    col_copy(block, 0, h).wait_send()

                @pl.when(block > me.col)
                def _():
                    col_copy(block, 1, h).wait_send()

    to_r, to_l, to_o = ((me.x + by + RING) % RING for by in (1, 3, 2))

    def lanes_of(m):
        return pl.ds(pl.multiple_of(chunk[m] * LANES, LANES), LANES)

    def dw_at(q, h, m):
        return dw.at[
            :, pl.ds(pl.multiple_of(q * rows + h * half, half), half), lanes_of(m)
        ]

    def multiply(m):
        for q in range(RING):
            D[q, m] = jnp.dot(
                XT[q * rows : (q + 1) * rows, :], G[chunk[m]], preferred_element_type=F32
            ).astype(BF16)
        out.start(D.at[to_o, m, top], xrel.at[0, m], xrel_sem.at[0, m], xr)
        out.start(D.at[to_o, m, bottom], xrel.at[1, m], xrel_sem.at[1, m], xl)
        out.start(D.at[to_r, m, bottom], xrec.at[0, m, bottom], xrec_sem.at[0, 1, m], xr)
        out.start(D.at[to_l, m, top], xrec.at[1, m, top], xrec_sem.at[1, 0, m], xl)

    def relay_x(m):
        arrived(xrel.at[0, m], xrel_sem.at[0, m], me)
        D[to_r, m, top] = (D[to_r, m, top].astype(F32) + xrel[0, m].astype(F32)).astype(BF16)
        out.start(D.at[to_r, m, top], xrec.at[0, m, top], xrec_sem.at[0, 0, m], xr)
        arrived(xrel.at[1, m], xrel_sem.at[1, m], me)
        D[to_l, m, bottom] = (D[to_l, m, bottom].astype(F32) + xrel[1, m].astype(F32)).astype(BF16)
        out.start(D.at[to_l, m, bottom], xrec.at[1, m, bottom], xrec_sem.at[1, 1, m], xl)

    def exchange(m):
        for side in range(2):
            for h in range(2):
                arrived(xrec.at[side, m, halves[h]], xrec_sem.at[side, h, m], me)
        S[m] = (D[me.x, m].astype(F32) + xrec[0, m].astype(F32) + xrec[1, m].astype(F32)).astype(BF16)
        out.start(S.at[m, top], zrel.at[0, m], zrel_sem.at[0, m], up)
        out.start(S.at[m, bottom], zrel.at[1, m], zrel_sem.at[1, m], down)

    def relay_z(m):
        arrived(zrel.at[0, m], zrel_sem.at[0, m], me)
        out.start(zrel.at[0, m], zrec.at[m, top], zrec_sem.at[0, m], up)
        arrived(zrel.at[1, m], zrel_sem.at[1, m], me)
        out.start(zrel.at[1, m], zrec.at[m, bottom], zrec_sem.at[1, m], down)

    def gather(q, h, m, device):
        out.start(dw_at(q, h, m), dw_at(q, h, m), out_sem.at[q, h, m], device)

    def gathered(q, h, m):
        arrived(dw_at(q, h, m), out_sem.at[q, h, m], me)

    def total_of(m):
        for h in range(2):
            arrived(zrec.at[m, halves[h]], zrec_sem.at[h, m], me)
        total = (S[m].astype(F32) + zrec[m].astype(F32)).astype(BF16)
        own_rows_x = pl.ds(pl.multiple_of(me.x * rows, rows), rows)
        for c in range(3):
            dw[c, own_rows_x, lanes_of(m)] = total[:, c * LANES : (c + 1) * LANES]
        gather(me.x, 0, m, xr)
        gather(me.x, 1, m, xl)
        gather(me.x, 1, m, xr)
        gather(me.x, 0, m, xl)

    def relay_out(m):
        gathered(to_l, 0, m)
        gather(to_l, 0, m, xr)
        gathered(to_r, 1, m)
        gather(to_r, 1, m, xl)

    def last_out(m):
        gathered(to_l, 1, m)
        gathered(to_r, 0, m)
        gathered(to_o, 0, m)
        gathered(to_o, 1, m)

    stages = {
        "F": projection, "H": channels, "A": relay_g, "B": share_g, "K": whole_g, "W": whole_g,
        "M": multiply, "X": relay_x, "E": exchange, "Z": relay_z, "T": total_of, "O": relay_out,
        "L": last_out, "C": col_round, "G": col_last,
    }
    for group in ORDER:
        for name in group.split():
            stages[name[0]](int(name[1]))
    out.finish()

    @pl.when(me.col < 7)
    def _():
        for u in range(SUBS):
            own_copy(0, u).wait_send()

    @pl.when(me.col > 0)
    def _():
        for u in range(SUBS):
            own_copy(1, u).wait_send()

    for j in range(8):

        @pl.when(jnp.logical_and(j < me.col, me.col < 7))
        def _():
            for u in range(SUBS):
                line_copy(j, u, col_up).wait_send()

        @pl.when(jnp.logical_and(j > me.col, me.col > 0))
        def _():
            for u in range(SUBS):
                line_copy(j, u, col_down).wait_send()

    for n in range(CHUNKS):
        for p in range(RING):
            pair_copy(p, n).wait_send()
        for k in range(6):
            y_copy(k, n).wait_send()

    @pl.when(me.core == 0)
    def _():
        tail_copy.wait_send()

    @pl.when(me.core == 1)
    def _():
        head_copy.wait_send()

    for by in range(RING):
        if by:
            go_part(by, 0)[0].wait_send()

            @pl.when(has_head)
            def _():
                go_part(by, 1)[0].wait_send()

        else:

            @pl.when(jnp.logical_not(stays))
            def _():
                go_part(0, 0)[0].wait_send()


SENDS = CHUNKS * (6 + 8 + 4 + 2 + 2 + 2 + 4 + 2)


def whole(tile, w, ft, it, go):
    rows, deep = tile.shape[0], w.shape[1]
    half, step = rows // 2, 3 * LANES
    vmem, sem = pltpu.VMEM, pltpu.SemaphoreType.DMA
    return pl.pallas_call(
        whole_kernel,
        out_shape=(jax.ShapeDtypeStruct((rows, deep), BF16), jax.ShapeDtypeStruct(w.shape, BF16)),
        in_specs=[
            pl.BlockSpec(memory_space=pltpu.HBM) for _ in range(5)
        ],
        out_specs=(pl.BlockSpec(memory_space=pltpu.VMEM),) * 2,
        scratch_shapes=[
            vmem((CHUNKS, deep, step), BF16),
            vmem(ft.shape, F32),
            vmem(it.shape, F32),
            vmem((8 * rows, deep), BF16),
            vmem((deep, 8 * rows), BF16),
            vmem((RING, CHUNKS, rows, step), F32),
            vmem((RING, CHUNKS, rows, step), BF16),
            vmem((RING, CHUNKS, rows, step), BF16),
            vmem((RING, CHUNKS, rows, step), BF16),
            vmem((2, CHUNKS, half, step), BF16),
            vmem((2, CHUNKS, rows, step), BF16),
            vmem((4 * rows + 2 * HALO, step), BF16),
            vmem((4 * rows + 2 * HALO, LANES), BF16),
            vmem((CHUNKS, 8 * rows, step), BF16),
            vmem((RING, CHUNKS, rows, step), BF16),
            vmem((2, CHUNKS, half, step), BF16),
            vmem((2, CHUNKS, rows, step), BF16),
            vmem((CHUNKS, rows, step), BF16),
            vmem((2, CHUNKS, half, step), BF16),
            vmem((CHUNKS, rows, step), BF16),
            vmem((8, rows, deep), BF16),
            vmem((8, rows, deep), BF16),
            vmem((8, rows, deep), BF16),
            sem((3 + 3 * CHUNKS,)),
            sem((SENDS,)),
            sem((9, SUBS)),
            sem((8, SUBS)),
            sem((RING, CHUNKS)),
            sem((RING, CHUNKS)),
            sem((6, CHUNKS)),
            sem((2, CHUNKS)),
            sem((2, 2, CHUNKS)),
            sem((10,)),
            sem((2,)),
            sem((5,)),
            sem((8, 2)),
            sem((8, 2, CHUNKS)),
            sem((2, CHUNKS)),
            sem((2, 2, CHUNKS)),
            sem((2, CHUNKS)),
            sem((2, CHUNKS)),
            sem((RING, 2, CHUNKS)),
            sem((8, 2)),
            sem((8, 2)),
        ],
        compiler_params=pltpu.CompilerParams(
            collective_id=1, has_side_effects=True, vmem_limit_bytes=63 * 2**20
        ),
        name="whole",
    )(tile, w, ft, it, go)


def on_device(inputs, weights, feature_taps, inner_taps, grad_out):
    grad_x, grad_w = whole(
        inputs[0], weights.transpose(1, 0, 2), feature_taps, inner_taps, grad_out[0]
    )
    return grad_x[None], grad_w.astype(F32).transpose(1, 0, 2)


def solution(mesh):
    placed = (
        P("dp", "col", "row"),
        P("row", None, "col"),
        P(None, None, "col"),
        P(None, "col"),
        P("dp", "row", "col"),
    )
    return jax.shard_map(
        on_device,
        mesh=mesh,
        in_specs=placed,
        out_specs=(P("dp", "col", "row"), P("row", None, "col")),
        check_vma=False,
    )
```

```python
import jax
import jax.numpy as jnp
from jax import lax
from jax.experimental import pallas as pl
from jax.experimental.pallas import tpu as pltpu
from jax.sharding import PartitionSpec as P

MESH = pl.DeviceIdType.MESH
NT = (((1,), (1,)), ((), ()))
CHUNKS = 4
HALO = 16
LANES = 128
SUBS = 4
RING = 4
ORDER = (
    "F3 F0 F1 F2", "H1 H2 H0 H3", "K0 M0 A0 X0", "A1 A2 A3 E0",
    "B0 B1 W1 M1", "X1 B2 B3 E1", "W2 M2 Z0 X2", "W3 M3 E2 X3",
    "Z1 E3 C0 Z2", "T0 C1 O0 Z3", "C2 L0 T1 C3", "O1 T2 C4 L1",
    "O2 C5 T3 C6", "O3 L2 G0 L3",
)
F32 = jnp.float32
BF16 = jnp.bfloat16


class Place:
    def __init__(self):
        self.dp, self.row, self.col = (lax.axis_index(a) for a in ("dp", "row", "col"))
        self.x, self.zh = self.dp // 2, self.dp % 2
        self.y, self.core = self.row // 2, self.row % 2

    def at_x(self, by):
        return (((self.x + by + RING) % RING) * 2 + self.zh, self.row, self.col)

    def at_y(self, by):
        return (self.dp, ((self.y + by + RING) % RING) * 2 + self.core, self.col)

    def in_row(self, by, core):
        return (self.dp, ((self.y + by) % RING) * 2 + core, self.col)

    def sibling(self):
        return self.in_row(0, 1 - self.core)

    def at_z(self, by):
        z = (self.zh * 8 + self.col + by + 16) % 16
        return (self.x * 2 + z // 8, self.row, z % 8)

    def at_col(self, by):
        return (self.dp, self.row, (self.col + by + 8) % 8)


def greet(partners):
    barrier = pltpu.get_barrier_semaphore()
    for partner in partners:
        pl.semaphore_signal(barrier, inc=1, device_id=partner, device_id_type=MESH)
    pl.semaphore_wait(barrier, len(partners))


class Sends:
    def __init__(self, sems):
        self.sems, self.copies = sems, []

    def start(self, src, dst, recv, device):
        copy = pltpu.make_async_remote_copy(
            src_ref=src, dst_ref=dst, send_sem=self.sems.at[len(self.copies)], recv_sem=recv,
            device_id=device, device_id_type=MESH,
        )
        copy.start()
        self.copies.append(copy)

    def finish(self):
        for copy in self.copies:
            copy.wait_send()


def arrived(ref, sem, place):
    pltpu.make_async_copy(ref, ref, sem).wait()


def whole_kernel(
    tile, w_hbm, ft_hbm, it_hbm, go_hbm, gx, dw,
    w, ft, it, XG, XT, acc, psend, pair, Dy, yrel, yrec, win, ups,
    G, D, xrel, xrec, S, zrel, zrec, rr, rl, part,
    fetch_sem, sends, ag_send, ag_recv, p_send, p_recv, y_send, yrel_sem, yrec_sem, h_send, h_recv, go_recv,
    col_send, g_recv, xrel_sem, xrec_sem, zrel_sem, zrec_sem, out_sem, rr_sem, rl_sem,
):
    me = Place()
    rows = tile.shape[0]
    half = rows // 2
    step = 3 * LANES
    right, left = me.at_y(1), me.at_y(-1)
    sibling = me.sibling()
    xr, xl = me.at_x(1), me.at_x(-1)
    up, down = me.at_z(4), me.at_z(-4)
    col_up, col_down = me.at_col(1), me.at_col(-1)
    others = [me.in_row(by, 1 - me.core) for by in (1, 2, 3)]
    own_rows = pl.ds(pl.multiple_of(me.col * rows, rows), rows)
    fetches = [
        pltpu.make_async_copy(tile, XG.at[own_rows], fetch_sem.at[0]),
        pltpu.make_async_copy(ft_hbm, ft, fetch_sem.at[1]),
        pltpu.make_async_copy(it_hbm, it, fetch_sem.at[2]),
    ]
    for n in range(CHUNKS):
        for c in range(3):
            lanes, to = pl.ds(n * LANES, LANES), pl.ds(c * LANES, LANES)
            fetches.append(
                pltpu.make_async_copy(
                    w_hbm.at[c, :, lanes], w.at[n, :, to], fetch_sem.at[3 + 3 * n + c]
                )
            )
    for copy in fetches:
        copy.start()
    greet([right, left, me.at_y(2), sibling, *others, xr, xl, up, down, col_up, col_down])
    out = Sends(sends)
    top, bottom = pl.ds(0, half), pl.ds(half, half)
    halves = (top, bottom)

    span = 4 * rows
    token_half = me.y // 2

    def go_part(by, head):
        n = (me.y + by) % RING
        lanes = pl.ds(pl.multiple_of(n * LANES, LANES), LANES)
        slot = me.row % 4
        if head:
            src, dst = go_hbm.at[pl.ds(0, HALO), lanes], ups.at[pl.ds(HALO + span, HALO)]
            recv, device = go_recv.at[4], me.in_row(by, 0)
        else:
            src = go_hbm.at[:, lanes]
            dst = ups.at[pl.ds(pl.multiple_of(HALO + slot * rows, HALO), rows)]
            recv, device = go_recv.at[slot], me.in_row(by, token_half)
        remote = pltpu.make_async_remote_copy(
            src_ref=src, dst_ref=dst, send_sem=h_send.at[2 + by + 4 * head], recv_sem=recv,
            device_id=device, device_id_type=MESH,
        )
        return remote, pltpu.make_async_copy(src, dst, recv)

    stays = token_half == me.core
    has_head = me.row == 4
    for by in range(RING):
        remote, local = go_part(by, 0)
        if by:
            remote.start()
        else:

            @pl.when(stays)
            def _():
                local.start()

            @pl.when(jnp.logical_not(stays))
            def _():
                remote.start()

        remote_head, local_head = go_part(by, 1)

        @pl.when(has_head)
        def _():
            (remote_head if by else local_head).start()

    ups[0:HALO, :] = jnp.zeros((HALO, LANES), BF16)

    @pl.when(me.core == 0)
    def _():
        win[0:HALO, :] = jnp.zeros((HALO, step), BF16)

    @pl.when(me.core == 1)
    def _():
        win[span + HALO :, :] = jnp.zeros((HALO, step), BF16)
        ups[span + HALO :, :] = jnp.zeros((HALO, LANES), BF16)

    tail_copy, head_copy = (
        pltpu.make_async_remote_copy(
            src_ref=win.at[pl.ds(src, HALO)], dst_ref=win.at[pl.ds(dst, HALO)],
            send_sem=h_send.at[k], recv_sem=h_recv.at[k], device_id=sibling, device_id_type=MESH,
        )
        for k, (src, dst) in enumerate(((span, 0), (HALO, span + HALO)))
    )

    def block_at(j):
        return pl.ds(pl.multiple_of(j * rows, rows), rows)

    def sub_at(j, u):
        sub = rows // SUBS
        return pl.ds(pl.multiple_of(j * rows + u * sub, sub), sub)

    def line_copy(j, u, device):
        return pltpu.make_async_remote_copy(
            src_ref=XG.at[sub_at(j, u)], dst_ref=XG.at[sub_at(j, u)], send_sem=ag_send.at[j, u],
            recv_sem=ag_recv.at[j, u], device_id=device, device_id_type=MESH,
        )

    def own_copy(n, u):
        sub = rows // SUBS
        return pltpu.make_async_remote_copy(
            src_ref=tile.at[pl.ds(u * sub, sub)], dst_ref=XG.at[sub_at(me.col, u)],
            send_sem=ag_send.at[8, u] if n else ag_send.at[me.col, u],
            recv_sem=ag_recv.at[me.col, u], device_id=col_down if n else col_up,
            device_id_type=MESH,
        )

    @pl.when(me.col < 7)
    def _():
        for u in range(SUBS):
            own_copy(0, u).start()

    @pl.when(me.col > 0)
    def _():
        for u in range(SUBS):
            own_copy(1, u).start()

    for copy in fetches:
        copy.wait()

    def pair_copy(s, n):
        return pltpu.make_async_remote_copy(
            src_ref=psend.at[s, n], dst_ref=pair.at[s, n], send_sem=p_send.at[s, n],
            recv_sem=p_recv.at[s, n], device_id=sibling, device_id_type=MESH,
        )

    y_opp, y_r, y_l = ((me.y + by) % RING for by in (2, 1, 3))

    def project(j):
        x = XG[block_at(j), :]
        s = j % 4
        mine = j // 4 == me.core
        for n in (y_opp, y_r, y_l, me.y):
            product = jnp.dot(x, w[n], preferred_element_type=F32)

            @pl.when(mine)
            def _():
                acc[s, n] = product

            @pl.when(jnp.logical_not(mine))
            def _():
                psend[s, n] = product.astype(BF16)
                pair_copy(s, n).start()

        XT[:, block_at(j)] = x.T

    def y_copy(k, s):
        src, dst, sem, device = (
            (Dy.at[s, y_opp, top], yrel.at[0, s], yrel_sem.at[0, s], right),
            (Dy.at[s, y_opp, bottom], yrel.at[1, s], yrel_sem.at[1, s], left),
            (Dy.at[s, y_r, bottom], yrec.at[0, s, bottom], yrec_sem.at[0, 1, s], right),
            (Dy.at[s, y_l, top], yrec.at[1, s, top], yrec_sem.at[1, 0, s], left),
            (Dy.at[s, y_r, top], yrec.at[0, s, top], yrec_sem.at[0, 0, s], right),
            (Dy.at[s, y_l, bottom], yrec.at[1, s, bottom], yrec_sem.at[1, 1, s], left),
        )[k]
        return pltpu.make_async_remote_copy(
            src_ref=src, dst_ref=dst, send_sem=y_send.at[k, s], recv_sem=sem, device_id=device,
            device_id_type=MESH,
        )

    def pair_sum(s):
        for n, copies in ((y_opp, (0, 1)), (y_r, (2,)), (y_l, (3,)), (me.y, ())):
            arrived(pair.at[s, n], p_recv.at[s, n], me)
            total = acc[s, n] + pair[s, n].astype(F32)
            if copies:
                Dy[s, n] = total.astype(BF16)
                for k in copies:
                    y_copy(k, s).start()
            else:
                acc[s, n] = total

    def relay_y(s):
        for side, n, at, k in ((0, y_r, top, 4), (1, y_l, bottom, 5)):
            arrived(yrel.at[side, s], yrel_sem.at[side, s], me)
            Dy[s, n, at] = (Dy[s, n, at].astype(F32) + yrel[side, s].astype(F32)).astype(BF16)
            y_copy(k, s).start()

    def for_kept(stage, d):
        for side in (-1, 1):
            j = me.col + side * d
            there = jnp.logical_and(jnp.logical_and(j >= 0, j <= 7), d >= (side + 1) // 2)
            there = jnp.logical_and(there, (j + 8) // 4 - 2 == me.core)

            @pl.when(there)
            def _():
                stage(j % 4)

    def pass_on(d, some):
        @pl.when(jnp.logical_and(d <= 7, me.col - d >= 0))
        def _():
            j = me.col - d
            for u in some:
                arrived(XG.at[sub_at(j, u)], ag_recv.at[j, u], me)

                @pl.when(me.col < 7)
                def _():
                    line_copy(j, u, col_up).start()

        @pl.when(jnp.logical_and(d <= 7, me.col + d <= 7))
        def _():
            j = me.col + d
            for u in some:
                arrived(XG.at[sub_at(j, u)], ag_recv.at[j, u], me)

                @pl.when(me.col > 0)
                def _():
                    line_copy(j, u, col_down).start()

    def line_step(d, carry):
        last = d - 1
        pass_on(d, range(SUBS // 2))

        @pl.when(jnp.logical_and(last <= 7, me.col - last >= 0))
        def _():
            project(me.col - last)

        pass_on(d, range(SUBS // 2, SUBS))

        @pl.when(jnp.logical_and(jnp.logical_and(last >= 1, last <= 7), me.col + last <= 7))
        def _():
            project(me.col + last)

        for_kept(relay_y, d - 3)
        for_kept(pair_sum, d - 2)
        return carry

    lax.fori_loop(1, 11, line_step, 0)

    def projection(s):
        for side in range(2):
            for h in range(2):
                arrived(yrec.at[side, s, halves[h]], yrec_sem.at[side, h, s], me)
        total = acc[s, me.y] + yrec[0, s].astype(F32) + yrec[1, s].astype(F32)
        win[HALO + s * rows : HALO + (s + 1) * rows, :] = total.astype(BF16)
        if s == 3:

            @pl.when(me.core == 0)
            def _():
                tail_copy.start()

        if s == 0:

            @pl.when(me.core == 1)
            def _():
                head_copy.start()

    length = rows + 2 * HALO

    def causal(seq, taps):
        total = taps[0] * seq
        for lag in range(1, len(taps)):
            total = total + taps[lag] * pltpu.roll(seq, lag, 0)
        return total

    def anticausal(seq, taps):
        total = taps[0] * seq
        for lag in range(1, len(taps)):
            total = total + taps[lag] * pltpu.roll(seq, length - lag, 0)
        return total

    def take_grad_out():
        for s in range(4):
            arrived(ups.at[pl.ds(HALO + s * rows, rows)], go_recv.at[s], me)

        @pl.when(me.core == 0)
        def _():
            arrived(ups.at[pl.ds(HALO + span, HALO)], go_recv.at[4], me)

    def channels(s):
        if s == 1:
            take_grad_out()
        if s == 0:

            @pl.when(me.core == 1)
            def _():
                arrived(win.at[pl.ds(0, HALO)], h_recv.at[0], me)

        if s == 3:

            @pl.when(me.core == 0)
            def _():
                arrived(win.at[pl.ds(span + HALO, HALO)], h_recv.at[1], me)

        lanes = pl.ds(pl.multiple_of(me.y * LANES, LANES), LANES)
        parts = [slice(c * LANES, (c + 1) * LANES) for c in range(3)]
        taps = [[ft[k, c : c + 1, lanes] for k in range(3)] for c in range(3)]
        inner_taps = [it[k : k + 1, lanes] for k in range(7)]
        tokens = slice(s * rows, s * rows + length)
        query, key, value = (
            causal(win[tokens, parts[c]].astype(F32), taps[c]) for c in range(3)
        )
        upstream = ups[tokens, :].astype(F32)
        product = (key * value).astype(BF16).astype(F32)
        inner = causal(product, inner_taps)
        grad_product = anticausal(upstream * query, inner_taps)
        mixed = (upstream * inner, grad_product * value, grad_product * key)
        at = pl.ds(pl.multiple_of(me.core * span + s * rows, rows), rows)
        for c in range(3):
            grad = anticausal(mixed[c], taps[c])
            G[me.y, at, parts[c]] = grad[HALO : rows + HALO].astype(BF16)
        for h in range(2):
            g_send(me.y, h, s, sibling)
        g_send(me.y, 0, s, right)
        g_send(me.y, 1, s, left)
        g_send(me.y, 1, s, right)
        g_send(me.y, 0, s, left)

    def g_at(n, core, h, s):
        first = core * span + s * rows + h * half
        return G.at[n, pl.ds(pl.multiple_of(first, half), half)]

    def g_send(n, h, s, device):
        at = g_at(n, me.core, h, s)
        out.start(at, at, g_recv.at[n * 2 + me.core, h, s], device)

    def g_wait(n, core, h, s):
        arrived(g_at(n, core, h, s), g_recv.at[n * 2 + core, h, s], me)

    @pl.when(me.col == 7)
    def _():
        rr[...] = jnp.zeros_like(rr)

    @pl.when(me.col == 0)
    def _():
        rl[...] = jnp.zeros_like(rl)

    def relay_g(s):
        g_wait(y_l, me.core, 0, s)
        g_send(y_l, 0, s, right)
        g_send(y_l, 0, s, sibling)
        g_wait(y_r, me.core, 1, s)
        g_send(y_r, 1, s, left)
        g_send(y_r, 1, s, sibling)
        g_wait(y_l, me.core, 1, s)
        g_send(y_l, 1, s, sibling)
        g_wait(y_r, me.core, 0, s)
        g_send(y_r, 0, s, sibling)

    def share_g(s):
        for h in range(2):
            g_wait(y_opp, me.core, h, s)
            g_send(y_opp, h, s, sibling)

    chunk = (me.y, y_r, y_l, y_opp)

    def whole_g(k):
        for s in range(4):
            for h in range(2):
                g_wait(chunk[k], 1 - me.core, h, s)

    def grad_in_of(block):
        at = pl.ds(pl.multiple_of(block * rows, rows), rows)
        total = lax.dot_general(G[0, at], w[0], NT, preferred_element_type=F32)
        for n in range(1, CHUNKS):
            total = total + lax.dot_general(G[n, at], w[n], NT, preferred_element_type=F32)
        return total

    def col_copy(block, side, h):
        landing, sems, device = ((rr, rr_sem, col_down), (rl, rl_sem, col_up))[side]
        return pltpu.make_async_remote_copy(
            src_ref=part.at[block, halves[h]], dst_ref=landing.at[block, halves[h]],
            send_sem=col_send.at[block, h], recv_sem=sems.at[block, h], device_id=device,
            device_id_type=MESH,
        )

    def col_pass(block, side, inner):
        landing, sems = ((rr, rr_sem), (rl, rl_sem))[side]
        total = grad_in_of(block)
        for h in range(2):

            @pl.when(inner)
            def _():
                arrived(landing.at[block, halves[h]], sems.at[block, h], me)

            own = total[h * half : (h + 1) * half]
            part[block, halves[h]] = (own + landing[block, halves[h]].astype(F32)).astype(BF16)
            col_copy(block, side, h).start()

    def col_round(s):
        @pl.when(s + me.col >= 7)
        def _():
            col_pass(s + me.col - 7, 0, me.col < 7)

        @pl.when(s >= me.col)
        def _():
            col_pass(7 - s + me.col, 1, me.col > 0)

    def col_last(unused):
        total = grad_in_of(me.col)
        for h in range(2):

            @pl.when(me.col < 7)
            def _():
                arrived(rr.at[me.col, halves[h]], rr_sem.at[me.col, h], me)

            @pl.when(me.col > 0)
            def _():
                arrived(rl.at[me.col, halves[h]], rl_sem.at[me.col, h], me)

        gx[...] = (total + rr[me.col].astype(F32) + rl[me.col].astype(F32)).astype(BF16)

        for block in range(8):
            for h in range(2):

                @pl.when(block < me.col)
                def _():
                    col_copy(block, 0, h).wait_send()

                @pl.when(block > me.col)
                def _():
                    col_copy(block, 1, h).wait_send()

    to_r, to_l, to_o = ((me.x + by + RING) % RING for by in (1, 3, 2))

    def lanes_of(m):
        return pl.ds(pl.multiple_of(chunk[m] * LANES, LANES), LANES)

    def dw_at(q, h, m):
        return dw.at[
            :, pl.ds(pl.multiple_of(q * rows + h * half, half), half), lanes_of(m)
        ]

    def multiply(m):
        for q in range(RING):
            D[q, m] = jnp.dot(
                XT[q * rows : (q + 1) * rows, :], G[chunk[m]], preferred_element_type=F32
            ).astype(BF16)
        out.start(D.at[to_o, m, top], xrel.at[0, m], xrel_sem.at[0, m], xr)
        out.start(D.at[to_o, m, bottom], xrel.at[1, m], xrel_sem.at[1, m], xl)
        out.start(D.at[to_r, m, bottom], xrec.at[0, m, bottom], xrec_sem.at[0, 1, m], xr)
        out.start(D.at[to_l, m, top], xrec.at[1, m, top], xrec_sem.at[1, 0, m], xl)

    def relay_x(m):
        arrived(xrel.at[0, m], xrel_sem.at[0, m], me)
        D[to_r, m, top] = (D[to_r, m, top].astype(F32) + xrel[0, m].astype(F32)).astype(BF16)
        out.start(D.at[to_r, m, top], xrec.at[0, m, top], xrec_sem.at[0, 0, m], xr)
        arrived(xrel.at[1, m], xrel_sem.at[1, m], me)
        D[to_l, m, bottom] = (D[to_l, m, bottom].astype(F32) + xrel[1, m].astype(F32)).astype(BF16)
        out.start(D.at[to_l, m, bottom], xrec.at[1, m, bottom], xrec_sem.at[1, 1, m], xl)

    def exchange(m):
        for side in range(2):
            for h in range(2):
                arrived(xrec.at[side, m, halves[h]], xrec_sem.at[side, h, m], me)
        S[m] = (D[me.x, m].astype(F32) + xrec[0, m].astype(F32) + xrec[1, m].astype(F32)).astype(BF16)
        out.start(S.at[m, top], zrel.at[0, m], zrel_sem.at[0, m], up)
        out.start(S.at[m, bottom], zrel.at[1, m], zrel_sem.at[1, m], down)

    def relay_z(m):
        arrived(zrel.at[0, m], zrel_sem.at[0, m], me)
        out.start(zrel.at[0, m], zrec.at[m, top], zrec_sem.at[0, m], up)
        arrived(zrel.at[1, m], zrel_sem.at[1, m], me)
        out.start(zrel.at[1, m], zrec.at[m, bottom], zrec_sem.at[1, m], down)

    def gather(q, h, m, device):
        out.start(dw_at(q, h, m), dw_at(q, h, m), out_sem.at[q, h, m], device)

    def gathered(q, h, m):
        arrived(dw_at(q, h, m), out_sem.at[q, h, m], me)

    def total_of(m):
        for h in range(2):
            arrived(zrec.at[m, halves[h]], zrec_sem.at[h, m], me)
        total = (S[m].astype(F32) + zrec[m].astype(F32)).astype(BF16)
        own_rows_x = pl.ds(pl.multiple_of(me.x * rows, rows), rows)
        for c in range(3):
            dw[c, own_rows_x, lanes_of(m)] = total[:, c * LANES : (c + 1) * LANES]
        gather(me.x, 0, m, xr)
        gather(me.x, 1, m, xl)
        gather(me.x, 1, m, xr)
        gather(me.x, 0, m, xl)

    def relay_out(m):
        gathered(to_l, 0, m)
        gather(to_l, 0, m, xr)
        gathered(to_r, 1, m)
        gather(to_r, 1, m, xl)

    def last_out(m):
        gathered(to_l, 1, m)
        gathered(to_r, 0, m)
        gathered(to_o, 0, m)
        gathered(to_o, 1, m)

    stages = {
        "F": projection, "H": channels, "A": relay_g, "B": share_g, "K": whole_g, "W": whole_g,
        "M": multiply, "X": relay_x, "E": exchange, "Z": relay_z, "T": total_of, "O": relay_out,
        "L": last_out, "C": col_round, "G": col_last,
    }
    for group in ORDER:
        for name in group.split():
            stages[name[0]](int(name[1]))
    out.finish()

    @pl.when(me.col < 7)
    def _():
        for u in range(SUBS):
            own_copy(0, u).wait_send()

    @pl.when(me.col > 0)
    def _():
        for u in range(SUBS):
            own_copy(1, u).wait_send()

    for j in range(8):

        @pl.when(jnp.logical_and(j < me.col, me.col < 7))
        def _():
            for u in range(SUBS):
                line_copy(j, u, col_up).wait_send()

        @pl.when(jnp.logical_and(j > me.col, me.col > 0))
        def _():
            for u in range(SUBS):
                line_copy(j, u, col_down).wait_send()

    for n in range(CHUNKS):
        for p in range(RING):
            pair_copy(p, n).wait_send()
        for k in range(6):
            y_copy(k, n).wait_send()

    @pl.when(me.core == 0)
    def _():
        tail_copy.wait_send()

    @pl.when(me.core == 1)
    def _():
        head_copy.wait_send()

    for by in range(RING):
        if by:
            go_part(by, 0)[0].wait_send()

            @pl.when(has_head)
            def _():
                go_part(by, 1)[0].wait_send()

        else:

            @pl.when(jnp.logical_not(stays))
            def _():
                go_part(0, 0)[0].wait_send()


SENDS = CHUNKS * (6 + 8 + 4 + 2 + 2 + 2 + 4 + 2)


def whole(tile, w, ft, it, go):
    rows, deep = tile.shape[0], w.shape[1]
    half, step = rows // 2, 3 * LANES
    vmem, sem = pltpu.VMEM, pltpu.SemaphoreType.DMA
    return pl.pallas_call(
        whole_kernel,
        out_shape=(jax.ShapeDtypeStruct((rows, deep), BF16), jax.ShapeDtypeStruct(w.shape, BF16)),
        in_specs=[
            pl.BlockSpec(memory_space=pltpu.HBM) for _ in range(5)
        ],
        out_specs=(pl.BlockSpec(memory_space=pltpu.VMEM),) * 2,
        scratch_shapes=[
            vmem((CHUNKS, deep, step), BF16),
            vmem(ft.shape, F32),
            vmem(it.shape, F32),
            vmem((8 * rows, deep), BF16),
            vmem((deep, 8 * rows), BF16),
            vmem((RING, CHUNKS, rows, step), F32),
            vmem((RING, CHUNKS, rows, step), BF16),
            vmem((RING, CHUNKS, rows, step), BF16),
            vmem((RING, CHUNKS, rows, step), BF16),
            vmem((2, CHUNKS, half, step), BF16),
            vmem((2, CHUNKS, rows, step), BF16),
            vmem((4 * rows + 2 * HALO, step), BF16),
            vmem((4 * rows + 2 * HALO, LANES), BF16),
            vmem((CHUNKS, 8 * rows, step), BF16),
            vmem((RING, CHUNKS, rows, step), BF16),
            vmem((2, CHUNKS, half, step), BF16),
            vmem((2, CHUNKS, rows, step), BF16),
            vmem((CHUNKS, rows, step), BF16),
            vmem((2, CHUNKS, half, step), BF16),
            vmem((CHUNKS, rows, step), BF16),
            vmem((8, rows, deep), BF16),
            vmem((8, rows, deep), BF16),
            vmem((8, rows, deep), BF16),
            sem((3 + 3 * CHUNKS,)),
            sem((SENDS,)),
            sem((9, SUBS)),
            sem((8, SUBS)),
            sem((RING, CHUNKS)),
            sem((RING, CHUNKS)),
            sem((6, CHUNKS)),
            sem((2, CHUNKS)),
            sem((2, 2, CHUNKS)),
            sem((10,)),
            sem((2,)),
            sem((5,)),
            sem((8, 2)),
            sem((8, 2, CHUNKS)),
            sem((2, CHUNKS)),
            sem((2, 2, CHUNKS)),
            sem((2, CHUNKS)),
            sem((2, CHUNKS)),
            sem((RING, 2, CHUNKS)),
            sem((8, 2)),
            sem((8, 2)),
        ],
        compiler_params=pltpu.CompilerParams(
            collective_id=1, has_side_effects=True, vmem_limit_bytes=52 * 2**20
        ),
        name="whole",
    )(*(pltpu.with_memory_space_constraint(a, pltpu.HBM) for a in (tile, w, ft, it, go)))


def on_device(inputs, weights, feature_taps, inner_taps, grad_out):
    grad_x, grad_w = whole(
        inputs[0], weights.transpose(1, 0, 2), feature_taps, inner_taps, grad_out[0]
    )
    return grad_x[None], grad_w.astype(F32).transpose(1, 0, 2)


def solution(mesh):
    placed = (
        P("dp", "col", "row"),
        P("row", None, "col"),
        P(None, None, "col"),
        P(None, "col"),
        P("dp", "row", "col"),
    )
    return jax.shard_map(
        on_device,
        mesh=mesh,
        in_specs=placed,
        out_specs=(P("dp", "col", "row"), P("row", None, "col")),
        check_vma=False,
    )
```

```python
import jax
import jax.numpy as jnp
from jax import lax
from jax.experimental import pallas as pl
from jax.experimental.pallas import tpu as pltpu
from jax.sharding import PartitionSpec as P

MESH = pl.DeviceIdType.MESH
NT = (((1,), (1,)), ((), ()))
CHUNKS = 4
HALO = 16
LANES = 128
SUBS = 2
RING = 4
ORDER = (
    "F3 F0 F1 F2", "H1 H2 H0 H3", "K0 M0 A0 X0", "A1 A2 A3 E0",
    "B0 B1 W1 M1", "X1 B2 B3 E1", "W2 M2 Z0 X2", "W3 M3 E2 X3",
    "Z1 E3 C0 Z2", "T0 C1 O0 Z3", "C2 L0 T1 C3", "O1 T2 C4 L1",
    "O2 C5 T3 C6", "O3 L2 G0 L3",
)
F32 = jnp.float32
BF16 = jnp.bfloat16


class Place:
    def __init__(self):
        self.dp, self.row, self.col = (lax.axis_index(a) for a in ("dp", "row", "col"))
        self.x, self.zh = self.dp // 2, self.dp % 2
        self.y, self.core = self.row // 2, self.row % 2

    def at_x(self, by):
        return (((self.x + by + RING) % RING) * 2 + self.zh, self.row, self.col)

    def at_y(self, by):
        return (self.dp, ((self.y + by + RING) % RING) * 2 + self.core, self.col)

    def in_row(self, by, core):
        return (self.dp, ((self.y + by) % RING) * 2 + core, self.col)

    def sibling(self):
        return self.in_row(0, 1 - self.core)

    def at_z(self, by):
        z = (self.zh * 8 + self.col + by + 16) % 16
        return (self.x * 2 + z // 8, self.row, z % 8)

    def at_col(self, by):
        return (self.dp, self.row, (self.col + by + 8) % 8)


def greet(partners):
    barrier = pltpu.get_barrier_semaphore()
    for partner in partners:
        pl.semaphore_signal(barrier, inc=1, device_id=partner, device_id_type=MESH)
    pl.semaphore_wait(barrier, len(partners))


class Sends:
    def __init__(self, sems):
        self.sems, self.copies = sems, []

    def start(self, src, dst, recv, device):
        copy = pltpu.make_async_remote_copy(
            src_ref=src, dst_ref=dst, send_sem=self.sems.at[len(self.copies)], recv_sem=recv,
            device_id=device, device_id_type=MESH,
        )
        copy.start()
        self.copies.append(copy)

    def finish(self):
        for copy in self.copies:
            copy.wait_send()


def arrived(ref, sem, place):
    pltpu.make_async_copy(ref, ref, sem).wait()


def whole_kernel(
    tile, w_hbm, ft_hbm, it_hbm, go_hbm, gx, dw,
    w, ft, it, XG, XT, acc, psend, pair, Dy, yrel, yrec, win, ups,
    G, D, xrel, xrec, S, zrel, zrec, rr, rl, part,
    fetch_sem, sends, ag_send, ag_recv, p_send, p_recv, y_send, yrel_sem, yrec_sem, h_send, h_recv, go_recv,
    col_send, g_recv, xrel_sem, xrec_sem, zrel_sem, zrec_sem, out_sem, rr_sem, rl_sem,
):
    me = Place()
    rows = tile.shape[0]
    half = rows // 2
    step = 3 * LANES
    right, left = me.at_y(1), me.at_y(-1)
    sibling = me.sibling()
    xr, xl = me.at_x(1), me.at_x(-1)
    up, down = me.at_z(4), me.at_z(-4)
    col_up, col_down = me.at_col(1), me.at_col(-1)
    others = [me.in_row(by, 1 - me.core) for by in (1, 2, 3)]
    own_rows = pl.ds(pl.multiple_of(me.col * rows, rows), rows)
    fetches = [
        pltpu.make_async_copy(tile, XG.at[own_rows], fetch_sem.at[0]),
        pltpu.make_async_copy(ft_hbm, ft, fetch_sem.at[1]),
        pltpu.make_async_copy(it_hbm, it, fetch_sem.at[2]),
    ]
    for n in range(CHUNKS):
        for c in range(3):
            lanes, to = pl.ds(n * LANES, LANES), pl.ds(c * LANES, LANES)
            fetches.append(
                pltpu.make_async_copy(
                    w_hbm.at[c, :, lanes], w.at[n, :, to], fetch_sem.at[3 + 3 * n + c]
                )
            )
    for copy in fetches:
        copy.start()
    greet([right, left, me.at_y(2), sibling, *others, xr, xl, up, down, col_up, col_down])
    out = Sends(sends)
    top, bottom = pl.ds(0, half), pl.ds(half, half)
    halves = (top, bottom)

    span = 4 * rows
    token_half = me.y // 2

    def go_part(by, head):
        n = (me.y + by) % RING
        lanes = pl.ds(pl.multiple_of(n * LANES, LANES), LANES)
        slot = me.row % 4
        if head:
            src, dst = go_hbm.at[pl.ds(0, HALO), lanes], ups.at[pl.ds(HALO + span, HALO)]
            recv, device = go_recv.at[4], me.in_row(by, 0)
        else:
            src = go_hbm.at[:, lanes]
            dst = ups.at[pl.ds(pl.multiple_of(HALO + slot * rows, HALO), rows)]
            recv, device = go_recv.at[slot], me.in_row(by, token_half)
        remote = pltpu.make_async_remote_copy(
            src_ref=src, dst_ref=dst, send_sem=h_send.at[2 + by + 4 * head], recv_sem=recv,
            device_id=device, device_id_type=MESH,
        )
        return remote, pltpu.make_async_copy(src, dst, recv)

    stays = token_half == me.core
    has_head = me.row == 4
    for by in range(RING):
        remote, local = go_part(by, 0)
        if by:
            remote.start()
        else:

            @pl.when(stays)
            def _():
                local.start()

            @pl.when(jnp.logical_not(stays))
            def _():
                remote.start()

        remote_head, local_head = go_part(by, 1)

        @pl.when(has_head)
        def _():
            (remote_head if by else local_head).start()

    ups[0:HALO, :] = jnp.zeros((HALO, LANES), BF16)

    @pl.when(me.core == 0)
    def _():
        win[0:HALO, :] = jnp.zeros((HALO, step), BF16)

    @pl.when(me.core == 1)
    def _():
        win[span + HALO :, :] = jnp.zeros((HALO, step), BF16)
        ups[span + HALO :, :] = jnp.zeros((HALO, LANES), BF16)

    tail_copy, head_copy = (
        pltpu.make_async_remote_copy(
            src_ref=win.at[pl.ds(src, HALO)], dst_ref=win.at[pl.ds(dst, HALO)],
            send_sem=h_send.at[k], recv_sem=h_recv.at[k], device_id=sibling, device_id_type=MESH,
        )
        for k, (src, dst) in enumerate(((span, 0), (HALO, span + HALO)))
    )

    def block_at(j):
        return pl.ds(pl.multiple_of(j * rows, rows), rows)

    def sub_at(j, u):
        sub = rows // SUBS
        return pl.ds(pl.multiple_of(j * rows + u * sub, sub), sub)

    def line_copy(j, u, device):
        return pltpu.make_async_remote_copy(
            src_ref=XG.at[sub_at(j, u)], dst_ref=XG.at[sub_at(j, u)], send_sem=ag_send.at[j, u],
            recv_sem=ag_recv.at[j, u], device_id=device, device_id_type=MESH,
        )

    def own_copy(n, u):
        sub = rows // SUBS
        return pltpu.make_async_remote_copy(
            src_ref=tile.at[pl.ds(u * sub, sub)], dst_ref=XG.at[sub_at(me.col, u)],
            send_sem=ag_send.at[8, u] if n else ag_send.at[me.col, u],
            recv_sem=ag_recv.at[me.col, u], device_id=col_down if n else col_up,
            device_id_type=MESH,
        )

    @pl.when(me.col < 7)
    def _():
        for u in range(SUBS):
            own_copy(0, u).start()

    @pl.when(me.col > 0)
    def _():
        for u in range(SUBS):
            own_copy(1, u).start()

    for copy in fetches:
        copy.wait()

    def pair_copy(s, n):
        return pltpu.make_async_remote_copy(
            src_ref=psend.at[s, n], dst_ref=pair.at[s, n], send_sem=p_send.at[s, n],
            recv_sem=p_recv.at[s, n], device_id=sibling, device_id_type=MESH,
        )

    y_opp, y_r, y_l = ((me.y + by) % RING for by in (2, 1, 3))

    def project(j):
        x = XG[block_at(j), :]
        s = j % 4
        mine = j // 4 == me.core
        for n in (y_opp, y_r, y_l, me.y):
            product = jnp.dot(x, w[n], preferred_element_type=F32)

            @pl.when(mine)
            def _():
                acc[s, n] = product

            @pl.when(jnp.logical_not(mine))
            def _():
                psend[s, n] = product.astype(BF16)
                pair_copy(s, n).start()

        XT[:, block_at(j)] = x.T

    def y_copy(k, s):
        src, dst, sem, device = (
            (Dy.at[s, y_opp, top], yrel.at[0, s], yrel_sem.at[0, s], right),
            (Dy.at[s, y_opp, bottom], yrel.at[1, s], yrel_sem.at[1, s], left),
            (Dy.at[s, y_r, bottom], yrec.at[0, s, bottom], yrec_sem.at[0, 1, s], right),
            (Dy.at[s, y_l, top], yrec.at[1, s, top], yrec_sem.at[1, 0, s], left),
            (Dy.at[s, y_r, top], yrec.at[0, s, top], yrec_sem.at[0, 0, s], right),
            (Dy.at[s, y_l, bottom], yrec.at[1, s, bottom], yrec_sem.at[1, 1, s], left),
        )[k]
        return pltpu.make_async_remote_copy(
            src_ref=src, dst_ref=dst, send_sem=y_send.at[k, s], recv_sem=sem, device_id=device,
            device_id_type=MESH,
        )

    def pair_sum(s):
        for n, copies in ((y_opp, (0, 1)), (y_r, (2,)), (y_l, (3,)), (me.y, ())):
            arrived(pair.at[s, n], p_recv.at[s, n], me)
            total = acc[s, n] + pair[s, n].astype(F32)
            if copies:
                Dy[s, n] = total.astype(BF16)
                for k in copies:
                    y_copy(k, s).start()
            else:
                acc[s, n] = total

    def relay_y(s):
        for side, n, at, k in ((0, y_r, top, 4), (1, y_l, bottom, 5)):
            arrived(yrel.at[side, s], yrel_sem.at[side, s], me)
            Dy[s, n, at] = (Dy[s, n, at].astype(F32) + yrel[side, s].astype(F32)).astype(BF16)
            y_copy(k, s).start()

    def for_kept(stage, d):
        for side in (-1, 1):
            j = me.col + side * d
            there = jnp.logical_and(jnp.logical_and(j >= 0, j <= 7), d >= (side + 1) // 2)
            there = jnp.logical_and(there, (j + 8) // 4 - 2 == me.core)

            @pl.when(there)
            def _():
                stage(j % 4)

    def pass_on(d, some):
        @pl.when(jnp.logical_and(d <= 7, me.col - d >= 0))
        def _():
            j = me.col - d
            for u in some:
                arrived(XG.at[sub_at(j, u)], ag_recv.at[j, u], me)

                @pl.when(me.col < 7)
                def _():
                    line_copy(j, u, col_up).start()

        @pl.when(jnp.logical_and(d <= 7, me.col + d <= 7))
        def _():
            j = me.col + d
            for u in some:
                arrived(XG.at[sub_at(j, u)], ag_recv.at[j, u], me)

                @pl.when(me.col > 0)
                def _():
                    line_copy(j, u, col_down).start()

    def line_step(d, carry):
        last = d - 1
        pass_on(d, range(SUBS // 2))

        @pl.when(jnp.logical_and(last <= 7, me.col - last >= 0))
        def _():
            project(me.col - last)

        pass_on(d, range(SUBS // 2, SUBS))

        @pl.when(jnp.logical_and(jnp.logical_and(last >= 1, last <= 7), me.col + last <= 7))
        def _():
            project(me.col + last)

        for_kept(relay_y, d - 3)
        for_kept(pair_sum, d - 2)
        return carry

    lax.fori_loop(1, 11, line_step, 0)

    def projection(s):
        for side in range(2):
            for h in range(2):
                arrived(yrec.at[side, s, halves[h]], yrec_sem.at[side, h, s], me)
        total = acc[s, me.y] + yrec[0, s].astype(F32) + yrec[1, s].astype(F32)
        win[HALO + s * rows : HALO + (s + 1) * rows, :] = total.astype(BF16)
        if s == 3:

            @pl.when(me.core == 0)
            def _():
                tail_copy.start()

        if s == 0:

            @pl.when(me.core == 1)
            def _():
                head_copy.start()

    length = rows + 2 * HALO

    def causal(seq, taps):
        total = taps[0] * seq
        for lag in range(1, len(taps)):
            total = total + taps[lag] * pltpu.roll(seq, lag, 0)
        return total

    def anticausal(seq, taps):
        total = taps[0] * seq
        for lag in range(1, len(taps)):
            total = total + taps[lag] * pltpu.roll(seq, length - lag, 0)
        return total

    def take_grad_out():
        for s in range(4):
            arrived(ups.at[pl.ds(HALO + s * rows, rows)], go_recv.at[s], me)

        @pl.when(me.core == 0)
        def _():
            arrived(ups.at[pl.ds(HALO + span, HALO)], go_recv.at[4], me)

    def channels(s):
        if s == 1:
            take_grad_out()
        if s == 0:

            @pl.when(me.core == 1)
            def _():
                arrived(win.at[pl.ds(0, HALO)], h_recv.at[0], me)

        if s == 3:

            @pl.when(me.core == 0)
            def _():
                arrived(win.at[pl.ds(span + HALO, HALO)], h_recv.at[1], me)

        lanes = pl.ds(pl.multiple_of(me.y * LANES, LANES), LANES)
        parts = [slice(c * LANES, (c + 1) * LANES) for c in range(3)]
        taps = [[ft[k, c : c + 1, lanes] for k in range(3)] for c in range(3)]
        inner_taps = [it[k : k + 1, lanes] for k in range(7)]
        tokens = slice(s * rows, s * rows + length)
        query, key, value = (
            causal(win[tokens, parts[c]].astype(F32), taps[c]) for c in range(3)
        )
        upstream = ups[tokens, :].astype(F32)
        product = (key * value).astype(BF16).astype(F32)
        inner = causal(product, inner_taps)
        grad_product = anticausal(upstream * query, inner_taps)
        mixed = (upstream * inner, grad_product * value, grad_product * key)
        at = pl.ds(pl.multiple_of(me.core * span + s * rows, rows), rows)
        for c in range(3):
            grad = anticausal(mixed[c], taps[c])
            G[me.y, at, parts[c]] = grad[HALO : rows + HALO].astype(BF16)
        for h in range(2):
            g_send(me.y, h, s, sibling)
        g_send(me.y, 0, s, right)
        g_send(me.y, 1, s, left)
        g_send(me.y, 1, s, right)
        g_send(me.y, 0, s, left)

    def g_at(n, core, h, s):
        first = core * span + s * rows + h * half
        return G.at[n, pl.ds(pl.multiple_of(first, half), half)]

    def g_send(n, h, s, device):
        at = g_at(n, me.core, h, s)
        out.start(at, at, g_recv.at[n * 2 + me.core, h, s], device)

    def g_wait(n, core, h, s):
        arrived(g_at(n, core, h, s), g_recv.at[n * 2 + core, h, s], me)

    @pl.when(me.col == 7)
    def _():
        rr[...] = jnp.zeros_like(rr)

    @pl.when(me.col == 0)
    def _():
        rl[...] = jnp.zeros_like(rl)

    def relay_g(s):
        g_wait(y_l, me.core, 0, s)
        g_send(y_l, 0, s, right)
        g_send(y_l, 0, s, sibling)
        g_wait(y_r, me.core, 1, s)
        g_send(y_r, 1, s, left)
        g_send(y_r, 1, s, sibling)
        g_wait(y_l, me.core, 1, s)
        g_send(y_l, 1, s, sibling)
        g_wait(y_r, me.core, 0, s)
        g_send(y_r, 0, s, sibling)

    def share_g(s):
        for h in range(2):
            g_wait(y_opp, me.core, h, s)
            g_send(y_opp, h, s, sibling)

    chunk = (me.y, y_r, y_l, y_opp)

    def whole_g(k):
        for s in range(4):
            for h in range(2):
                g_wait(chunk[k], 1 - me.core, h, s)

    def grad_in_of(block):
        at = pl.ds(pl.multiple_of(block * rows, rows), rows)
        total = lax.dot_general(G[0, at], w[0], NT, preferred_element_type=F32)
        for n in range(1, CHUNKS):
            total = total + lax.dot_general(G[n, at], w[n], NT, preferred_element_type=F32)
        return total

    def col_copy(block, side, h):
        landing, sems, device = ((rr, rr_sem, col_down), (rl, rl_sem, col_up))[side]
        return pltpu.make_async_remote_copy(
            src_ref=part.at[block, halves[h]], dst_ref=landing.at[block, halves[h]],
            send_sem=col_send.at[block, h], recv_sem=sems.at[block, h], device_id=device,
            device_id_type=MESH,
        )

    def col_pass(block, side, inner):
        landing, sems = ((rr, rr_sem), (rl, rl_sem))[side]
        total = grad_in_of(block)
        for h in range(2):

            @pl.when(inner)
            def _():
                arrived(landing.at[block, halves[h]], sems.at[block, h], me)

            own = total[h * half : (h + 1) * half]
            part[block, halves[h]] = (own + landing[block, halves[h]].astype(F32)).astype(BF16)
            col_copy(block, side, h).start()

    def col_round(s):
        @pl.when(s + me.col >= 7)
        def _():
            col_pass(s + me.col - 7, 0, me.col < 7)

        @pl.when(s >= me.col)
        def _():
            col_pass(7 - s + me.col, 1, me.col > 0)

    def col_last(unused):
        total = grad_in_of(me.col)
        for h in range(2):

            @pl.when(me.col < 7)
            def _():
                arrived(rr.at[me.col, halves[h]], rr_sem.at[me.col, h], me)

            @pl.when(me.col > 0)
            def _():
                arrived(rl.at[me.col, halves[h]], rl_sem.at[me.col, h], me)

        gx[...] = (total + rr[me.col].astype(F32) + rl[me.col].astype(F32)).astype(BF16)

        for block in range(8):
            for h in range(2):

                @pl.when(block < me.col)
                def _():
                    col_copy(block, 0, h).wait_send()

                @pl.when(block > me.col)
                def _():
                    col_copy(block, 1, h).wait_send()

    to_r, to_l, to_o = ((me.x + by + RING) % RING for by in (1, 3, 2))

    def lanes_of(m):
        return pl.ds(pl.multiple_of(chunk[m] * LANES, LANES), LANES)

    def dw_at(q, h, m):
        return dw.at[
            :, pl.ds(pl.multiple_of(q * rows + h * half, half), half), lanes_of(m)
        ]

    def multiply(m):
        for q in range(RING):
            D[q, m] = jnp.dot(
                XT[q * rows : (q + 1) * rows, :], G[chunk[m]], preferred_element_type=F32
            ).astype(BF16)
        out.start(D.at[to_o, m, top], xrel.at[0, m], xrel_sem.at[0, m], xr)
        out.start(D.at[to_o, m, bottom], xrel.at[1, m], xrel_sem.at[1, m], xl)
        out.start(D.at[to_r, m, bottom], xrec.at[0, m, bottom], xrec_sem.at[0, 1, m], xr)
        out.start(D.at[to_l, m, top], xrec.at[1, m, top], xrec_sem.at[1, 0, m], xl)

    def relay_x(m):
        arrived(xrel.at[0, m], xrel_sem.at[0, m], me)
        D[to_r, m, top] = (D[to_r, m, top].astype(F32) + xrel[0, m].astype(F32)).astype(BF16)
        out.start(D.at[to_r, m, top], xrec.at[0, m, top], xrec_sem.at[0, 0, m], xr)
        arrived(xrel.at[1, m], xrel_sem.at[1, m], me)
        D[to_l, m, bottom] = (D[to_l, m, bottom].astype(F32) + xrel[1, m].astype(F32)).astype(BF16)
        out.start(D.at[to_l, m, bottom], xrec.at[1, m, bottom], xrec_sem.at[1, 1, m], xl)

    def exchange(m):
        for side in range(2):
            for h in range(2):
                arrived(xrec.at[side, m, halves[h]], xrec_sem.at[side, h, m], me)
        S[m] = (D[me.x, m].astype(F32) + xrec[0, m].astype(F32) + xrec[1, m].astype(F32)).astype(BF16)
        out.start(S.at[m, top], zrel.at[0, m], zrel_sem.at[0, m], up)
        out.start(S.at[m, bottom], zrel.at[1, m], zrel_sem.at[1, m], down)

    def relay_z(m):
        arrived(zrel.at[0, m], zrel_sem.at[0, m], me)
        out.start(zrel.at[0, m], zrec.at[m, top], zrec_sem.at[0, m], up)
        arrived(zrel.at[1, m], zrel_sem.at[1, m], me)
        out.start(zrel.at[1, m], zrec.at[m, bottom], zrec_sem.at[1, m], down)

    def gather(q, h, m, device):
        out.start(dw_at(q, h, m), dw_at(q, h, m), out_sem.at[q, h, m], device)

    def gathered(q, h, m):
        arrived(dw_at(q, h, m), out_sem.at[q, h, m], me)

    def total_of(m):
        for h in range(2):
            arrived(zrec.at[m, halves[h]], zrec_sem.at[h, m], me)
        total = (S[m].astype(F32) + zrec[m].astype(F32)).astype(BF16)
        own_rows_x = pl.ds(pl.multiple_of(me.x * rows, rows), rows)
        for c in range(3):
            dw[c, own_rows_x, lanes_of(m)] = total[:, c * LANES : (c + 1) * LANES]
        gather(me.x, 0, m, xr)
        gather(me.x, 1, m, xl)
        gather(me.x, 1, m, xr)
        gather(me.x, 0, m, xl)

    def relay_out(m):
        gathered(to_l, 0, m)
        gather(to_l, 0, m, xr)
        gathered(to_r, 1, m)
        gather(to_r, 1, m, xl)

    def last_out(m):
        gathered(to_l, 1, m)
        gathered(to_r, 0, m)
        gathered(to_o, 0, m)
        gathered(to_o, 1, m)

    stages = {
        "F": projection, "H": channels, "A": relay_g, "B": share_g, "K": whole_g, "W": whole_g,
        "M": multiply, "X": relay_x, "E": exchange, "Z": relay_z, "T": total_of, "O": relay_out,
        "L": last_out, "C": col_round, "G": col_last,
    }
    for group in ORDER:
        for name in group.split():
            stages[name[0]](int(name[1]))
    out.finish()

    @pl.when(me.col < 7)
    def _():
        for u in range(SUBS):
            own_copy(0, u).wait_send()

    @pl.when(me.col > 0)
    def _():
        for u in range(SUBS):
            own_copy(1, u).wait_send()

    for j in range(8):

        @pl.when(jnp.logical_and(j < me.col, me.col < 7))
        def _():
            for u in range(SUBS):
                line_copy(j, u, col_up).wait_send()

        @pl.when(jnp.logical_and(j > me.col, me.col > 0))
        def _():
            for u in range(SUBS):
                line_copy(j, u, col_down).wait_send()

    for n in range(CHUNKS):
        for p in range(RING):
            pair_copy(p, n).wait_send()
        for k in range(6):
            y_copy(k, n).wait_send()

    @pl.when(me.core == 0)
    def _():
        tail_copy.wait_send()

    @pl.when(me.core == 1)
    def _():
        head_copy.wait_send()

    for by in range(RING):
        if by:
            go_part(by, 0)[0].wait_send()

            @pl.when(has_head)
            def _():
                go_part(by, 1)[0].wait_send()

        else:

            @pl.when(jnp.logical_not(stays))
            def _():
                go_part(0, 0)[0].wait_send()


SENDS = CHUNKS * (6 + 8 + 4 + 2 + 2 + 2 + 4 + 2)


def whole(tile, w, ft, it, go):
    rows, deep = tile.shape[0], w.shape[1]
    half, step = rows // 2, 3 * LANES
    vmem, sem = pltpu.VMEM, pltpu.SemaphoreType.DMA
    return pl.pallas_call(
        whole_kernel,
        out_shape=(jax.ShapeDtypeStruct((rows, deep), BF16), jax.ShapeDtypeStruct(w.shape, BF16)),
        in_specs=[
            pl.BlockSpec(memory_space=pltpu.HBM) for _ in range(5)
        ],
        out_specs=(pl.BlockSpec(memory_space=pltpu.VMEM),) * 2,
        scratch_shapes=[
            vmem((CHUNKS, deep, step), BF16),
            vmem(ft.shape, F32),
            vmem(it.shape, F32),
            vmem((8 * rows, deep), BF16),
            vmem((deep, 8 * rows), BF16),
            vmem((RING, CHUNKS, rows, step), F32),
            vmem((RING, CHUNKS, rows, step), BF16),
            vmem((RING, CHUNKS, rows, step), BF16),
            vmem((RING, CHUNKS, rows, step), BF16),
            vmem((2, CHUNKS, half, step), BF16),
            vmem((2, CHUNKS, rows, step), BF16),
            vmem((4 * rows + 2 * HALO, step), BF16),
            vmem((4 * rows + 2 * HALO, LANES), BF16),
            vmem((CHUNKS, 8 * rows, step), BF16),
            vmem((RING, CHUNKS, rows, step), BF16),
            vmem((2, CHUNKS, half, step), BF16),
            vmem((2, CHUNKS, rows, step), BF16),
            vmem((CHUNKS, rows, step), BF16),
            vmem((2, CHUNKS, half, step), BF16),
            vmem((CHUNKS, rows, step), BF16),
            vmem((8, rows, deep), BF16),
            vmem((8, rows, deep), BF16),
            vmem((8, rows, deep), BF16),
            sem((3 + 3 * CHUNKS,)),
            sem((SENDS,)),
            sem((9, SUBS)),
            sem((8, SUBS)),
            sem((RING, CHUNKS)),
            sem((RING, CHUNKS)),
            sem((6, CHUNKS)),
            sem((2, CHUNKS)),
            sem((2, 2, CHUNKS)),
            sem((10,)),
            sem((2,)),
            sem((5,)),
            sem((8, 2)),
            sem((8, 2, CHUNKS)),
            sem((2, CHUNKS)),
            sem((2, 2, CHUNKS)),
            sem((2, CHUNKS)),
            sem((2, CHUNKS)),
            sem((RING, 2, CHUNKS)),
            sem((8, 2)),
            sem((8, 2)),
        ],
        compiler_params=pltpu.CompilerParams(
            collective_id=1, has_side_effects=True, vmem_limit_bytes=52 * 2**20
        ),
        name="whole",
    )(*(pltpu.with_memory_space_constraint(a, pltpu.HBM) for a in (tile, w, ft, it, go)))


def on_device(inputs, weights, feature_taps, inner_taps, grad_out):
    grad_x, grad_w = whole(
        inputs[0], weights.transpose(1, 0, 2), feature_taps, inner_taps, grad_out[0]
    )
    return grad_x[None], grad_w.astype(F32).transpose(1, 0, 2)


def solution(mesh):
    placed = (
        P("dp", "col", "row"),
        P("row", None, "col"),
        P(None, None, "col"),
        P(None, "col"),
        P("dp", "row", "col"),
    )
    return jax.shard_map(
        on_device,
        mesh=mesh,
        in_specs=placed,
        out_specs=(P("dp", "col", "row"), P("row", None, "col")),
        check_vma=False,
    )
```
